32 devices in a mesh: dp: 8 (over z, x), tensor: 4 (over y, core).
Axes of the slice: x: 2, y: 2, z: 4, core: 2. Of those that a mesh axis runs over, the one named last changes fastest.
Arguments:
- tokens: bfloat16 [8192, 768], P(('dp', 'tensor')), may hold values from -6 to 6
- cotangent: bfloat16 [8192, 768], P(('dp', 'tensor')), may hold values from -6 to 6
- seq_lengths: int32 [8], P('dp'), may hold values from 513 to 1024, as said below
- gain_mixer: bfloat16 [768], P('dp'), may hold values from 0.5 to 1.5
- mixer_query: bfloat16 [768, 768], P('dp', 'tensor'), may hold values from -0.21875 to 0.21875
- mixer_key: bfloat16 [768, 768], P('dp', 'tensor'), may hold values from -0.21875 to 0.21875
- mixer_value: bfloat16 [768, 768], P('dp', 'tensor'), may hold values from -0.21875 to 0.21875
- shift_taps: bfloat16 [64, 768], P('dp', 'tensor'), may hold values from -0.75 to 0.75
- ssm_decay: bfloat16 [768, 64], P('tensor', 'dp'), may hold values from 0.0019989014 to 0.5
- ssm_coef: bfloat16 [768, 64], P('tensor', 'dp'), may hold values from -0.75 to 0.75
- mixer_out: bfloat16 [768, 768], P('tensor', 'dp'), may hold values from -0.21875 to 0.21875
- gain_ffn1: bfloat16 [768], P('dp'), may hold values from 0.5 to 1.5
- ffn1_up: bfloat16 [768, 3072], P('dp', 'tensor'), may hold values from -0.21875 to 0.21875
- ffn1_down: bfloat16 [3072, 768], P('tensor', 'dp'), may hold values from -0.109375 to 0.109375
- gain_attn: bfloat16 [768], P('dp'), may hold values from 0.5 to 1.5
- attn_query: bfloat16 [768, 768], P('dp', 'tensor'), may hold values from -0.21875 to 0.21875
- attn_key: bfloat16 [768, 768], P('dp', 'tensor'), may hold values from -0.21875 to 0.21875
- attn_value: bfloat16 [768, 768], P('dp', 'tensor'), may hold values from -0.21875 to 0.21875
- attn_out: bfloat16 [768, 768], P('tensor', 'dp'), may hold values from -3.5 to 3.5
- gain_ffn2: bfloat16 [768], P('dp'), may hold values from 0.5 to 1.5
- ffn2_up: bfloat16 [768, 3072], P('dp', 'tensor'), may hold values from -0.21875 to 0.21875
- ffn2_down: bfloat16 [3072, 768], P('tensor', 'dp'), may hold values from -0.109375 to 0.109375
Outputs:
- output: bfloat16 [8192, 768], P(('dp', 'tensor'))
- input_grad: bfloat16 [8192, 768], P(('dp', 'tensor'))
- grad_gain_mixer: float32 [768], P('dp')
- grad_mixer_query: float32 [768, 768], P('dp', 'tensor')
- grad_mixer_key: float32 [768, 768], P('dp', 'tensor')
- grad_mixer_value: float32 [768, 768], P('dp', 'tensor')
- grad_shift_taps: float32 [64, 768], P('dp', 'tensor')
- grad_ssm_decay: float32 [768, 64], P('tensor', 'dp')
- grad_ssm_coef: float32 [768, 64], P('tensor', 'dp')
- grad_mixer_out: float32 [768, 768], P('tensor', 'dp')
- grad_gain_ffn1: float32 [768], P('dp')
- grad_ffn1_up: float32 [768, 3072], P('dp', 'tensor')
- grad_ffn1_down: float32 [3072, 768], P('tensor', 'dp')
- grad_gain_attn: float32 [768], P('dp')
- grad_attn_query: float32 [768, 768], P('dp', 'tensor')
- grad_attn_key: float32 [768, 768], P('dp', 'tensor')
- grad_attn_value: float32 [768, 768], P('dp', 'tensor')
- grad_attn_out: float32 [768, 768], P('tensor', 'dp')
- grad_gain_ffn2: float32 [768], P('dp')
- grad_ffn2_up: float32 [768, 3072], P('dp', 'tensor')
- grad_ffn2_down: float32 [3072, 768], P('tensor', 'dp')
The draws below stay inside these ranges and needn't reach their ends.
Inputs may be any that keep to these rules, and one draw needn't show every extreme that they name: Row r holds one sequence in its first seq_lengths[r] positions, the rest of the row is padding; some row is full and some row holds 513 live tokens.
All inputs are finite; a program needn't handle non-finite values.
Results may differ from the reference program's by a relative error of at most 0.035.
Values may be sent and summed in bfloat16 or wider, within the bound.
No kernel may reach another device: no remote copies, remote signals or barrier semaphores. Data moves between devices by JAX's collectives and lax.ppermute only.
A program may use at most 320 MiB of HBM per device.

```python
import math
import jax
import jax.numpy as jnp
from jax import lax

D = 768
HEADS = 12
HEAD = 64
FF = 3072
STATE = 64
SHIFT = 64
ROW = 1024
TOKENS = 8192
N_DP = 8


def draw_seq_lengths(key, part):
    base_draw = jax.random.randint(jax.random.fold_in(key, 11), (N_DP,), ROW // 2 + 1, ROW + 1)
    full_row = jax.random.randint(jax.random.fold_in(key, 12), (), 0, N_DP)
    offset_row = jax.random.randint(jax.random.fold_in(key, 13), (), 1, N_DP)
    least_row = (full_row + offset_row) % N_DP
    row_ids = jnp.arange(N_DP)
    base_draw = jnp.where(row_ids == full_row, ROW, base_draw)
    return jnp.where(row_ids == least_row, ROW // 2 + 1, base_draw).astype(jnp.int32)


def block_scale(own_key, dims, cuts, least, high):
    factor_of = 1.0
    for position, shards_of in cuts:
        draws = jax.random.uniform(jax.random.fold_in(jax.random.fold_in(own_key, 6), position), (shards_of,), jnp.float32, least / len(cuts), high / len(cuts))
        factor_of = factor_of * jnp.repeat(jnp.exp(draws), dims[position] // shards_of).reshape((-1,) + (1,) * (len(dims) - 1 - position))
    return factor_of


def noise(own_key, extent, scale, most, pieces=(), dtype=jnp.bfloat16):
    array = jax.random.normal(own_key, extent, jnp.float32) * scale
    if len(pieces) > 0:
        array = block_scale(own_key, extent, pieces, -0.22, 0.18) * array
    return jnp.clip(array, min=-most, max=most).astype(dtype)


def setup_inputs(seed: int = 0) -> dict:
    splits = jax.random.split(jax.random.key(seed), 23)
    tokens = noise(splits[0], (TOKENS, D), 1.0, 6.0, ((0, 32),))
    cotangent = noise(splits[1], (TOKENS, D), 1.0, 6.0, ((0, 32),))
    seq_lengths = draw_seq_lengths(jax.random.fold_in(splits[22], 71), 0)
    gain_mixer = jnp.clip(1.0 + 0.1 * jax.random.normal(splits[3], (D,), jnp.float32), 0.5, 1.5).astype(jnp.bfloat16)
    mixer_query = noise(splits[4], (D, D), D ** -0.5, 0.21875, ((0, 8), (1, 4)))
    mixer_key = noise(splits[5], (D, D), D ** -0.5, 0.21875, ((0, 8), (1, 4)))
    mixer_value = noise(splits[6], (D, D), D ** -0.5, 0.21875, ((0, 8), (1, 4)))
    shift_taps = noise(splits[7], (SHIFT, D), SHIFT ** -0.5, 0.75, ((0, 8), (1, 4)))
    ssm_decay = jnp.clip(jnp.exp(math.log(0.5) - 5.5220104 * jax.random.uniform(splits[8], (D, STATE), jnp.float32) ** block_scale(splits[8], (D, STATE), ((0, 4), (1, 8)), -0.2, 0.2)), 0.0019989014, 0.5).astype(jnp.bfloat16)
    ssm_coef = noise(splits[9], (D, STATE), STATE ** -0.5, 0.75, ((0, 4), (1, 8)))
    mixer_out = noise(splits[10], (D, D), D ** -0.5, 0.21875, ((0, 4), (1, 8)))
    gain_ffn1 = jnp.clip(1.0 + 0.1 * jax.random.normal(splits[11], (D,), jnp.float32), 0.5, 1.5).astype(jnp.bfloat16)
    ffn1_up = noise(splits[12], (D, FF), D ** -0.5, 0.21875, ((0, 8), (1, 4)))
    ffn1_down = noise(splits[13], (FF, D), FF ** -0.5, 0.109375, ((0, 4), (1, 8)))
    gain_attn = jnp.clip(1.0 + 0.1 * jax.random.normal(splits[14], (D,), jnp.float32), 0.5, 1.5).astype(jnp.bfloat16)
    attn_query = noise(splits[15], (D, D), D ** -0.5, 0.21875, ((0, 8), (1, 4)))
    attn_key = noise(splits[16], (D, D), D ** -0.5, 0.21875, ((0, 8), (1, 4)))
    attn_value = noise(splits[17], (D, D), D ** -0.5, 0.21875, ((0, 8), (1, 4)))
    attn_out = noise(splits[18], (D, D), (max(1, 4 * D // ROW)) ** -0.5, 3.5, ((0, 4), (1, 8)))
    gain_ffn2 = jnp.clip(1.0 + 0.1 * jax.random.normal(splits[19], (D,), jnp.float32), 0.5, 1.5).astype(jnp.bfloat16)
    ffn2_up = noise(splits[20], (D, FF), D ** -0.5, 0.21875, ((0, 8), (1, 4)))
    ffn2_down = noise(splits[21], (FF, D), FF ** -0.5, 0.109375, ((0, 4), (1, 8)))
    return {"tokens": tokens, "cotangent": cotangent, "seq_lengths": seq_lengths, "gain_mixer": gain_mixer, "mixer_query": mixer_query, "mixer_key": mixer_key, "mixer_value": mixer_value, "shift_taps": shift_taps, "ssm_decay": ssm_decay, "ssm_coef": ssm_coef, "mixer_out": mixer_out, "gain_ffn1": gain_ffn1, "ffn1_up": ffn1_up, "ffn1_down": ffn1_down, "gain_attn": gain_attn, "attn_query": attn_query, "attn_key": attn_key, "attn_value": attn_value, "attn_out": attn_out, "gain_ffn2": gain_ffn2, "ffn2_up": ffn2_up, "ffn2_down": ffn2_down}


EPSILON = 1e-05
PRECISE = lax.Precision.HIGHEST

@jax.custom_vjp
def low(v):
    return lax.optimization_barrier(v.astype(jnp.bfloat16)).astype(jnp.float32)

@jax.custom_vjp
def low_back(v):
    return v

def low_keep(v):
    return (low(v), None)

def low_pass(kept, grad):
    return (grad,)

def back_keep(v):
    return (v, None)

def back_low(kept, grad):
    return (low(grad),)
low.defvjp(low_keep, low_pass)
low_back.defvjp(back_keep, back_low)

def layer_norm(hidden, gain):
    average = lax.optimization_barrier(jnp.mean(hidden, axis=-1, keepdims=True))
    centred = hidden - average
    return centred * lax.rsqrt(lax.optimization_barrier(jnp.mean(centred * centred, axis=-1, keepdims=True)) + EPSILON) * gain

def product(left, right):
    return jnp.dot(left, right, precision=PRECISE)

def causal_conv(signal, kernel):
    length = signal.shape[0]
    spectrum = jnp.fft.rfft(signal, n=2 * length, axis=0) * jnp.fft.rfft(kernel, n=2 * length, axis=0)
    return jnp.fft.irfft(spectrum, n=2 * length, axis=0)[:length]

def gelu_tanh(values):
    return jax.nn.gelu(values, approximate=True)

def row_pass(params, kernels, row_input, length):
    gain_mixer, mixer_query, mixer_key, mixer_value, shift_taps, ssm_decay, ssm_coef, mixer_out, gain_ffn1, ffn1_up, ffn1_down, gain_attn, attn_query, attn_key, attn_value, attn_out, gain_ffn2, ffn2_up, ffn2_down = params
    shift_kernel, diag_kernel = kernels
    normed = low(layer_norm(row_input, gain_mixer))
    query_one = low_back(product(normed, mixer_query))
    key_one = low_back(product(normed, mixer_key))
    value_one = low_back(product(normed, mixer_value))
    shifted = causal_conv(key_one, shift_kernel)
    state = causal_conv(shifted * value_one, diag_kernel)
    mixed = low(query_one * state)
    hidden = row_input + low_back(product(mixed, mixer_out))
    normed = low(layer_norm(hidden, gain_ffn1))
    active = low(gelu_tanh(low_back(product(normed, ffn1_up))))
    hidden = hidden + low_back(product(active, ffn1_down))
    normed = low(layer_norm(hidden, gain_attn))
    query_two = low(low_back(product(normed, attn_query))).reshape(ROW, HEADS, HEAD)
    key_two = low(low_back(product(normed, attn_key))).reshape(ROW, HEADS, HEAD)
    value_two = low(low_back(product(normed, attn_value))).reshape(ROW, HEADS, HEAD)
    scores = low_back(jnp.einsum('qhd,khd->hqk', query_two, key_two, precision=PRECISE) * HEAD ** (-0.5))
    positions = jnp.arange(ROW)
    allowed = (positions[None, :] <= positions[:, None]) & (positions[None, :] < length)
    scores = jnp.where(allowed[None], scores, -jnp.inf)
    probs = low(jax.nn.softmax(scores, axis=-1))
    attended = low(low_back(jnp.einsum('hqk,khd->qhd', probs, value_two, precision=PRECISE))).reshape(ROW, D)
    hidden = hidden + low_back(product(attended, attn_out))
    normed = low(layer_norm(hidden, gain_ffn2))
    active = low(gelu_tanh(low_back(product(normed, ffn2_up))))
    return hidden + low_back(product(active, ffn2_down))

def reference(tokens, cotangent, seq_lengths, gain_mixer, mixer_query, mixer_key, mixer_value, shift_taps, ssm_decay, ssm_coef, mixer_out, gain_ffn1, ffn1_up, ffn1_down, gain_attn, attn_query, attn_key, attn_value, attn_out, gain_ffn2, ffn2_up, ffn2_down):
    weights = tuple((item.astype(jnp.float32) for item in (gain_mixer, mixer_query, mixer_key, mixer_value, shift_taps, ssm_decay, ssm_coef, mixer_out, gain_ffn1, ffn1_up, ffn1_down, gain_attn, attn_query, attn_key, attn_value, attn_out, gain_ffn2, ffn2_up, ffn2_down)))

    def forward(inputs, *params):
        taps_f, decay_f, coef_f = (params[4], params[5], params[6])
        shift_kernel = jnp.concatenate([taps_f, jnp.zeros((ROW - SHIFT, D), jnp.float32)], axis=0)
        steps_f = jnp.arange(ROW).astype(jnp.float32)
        mixing = jnp.sqrt(2.0 * decay_f) * coef_f
        diag_kernel = jnp.einsum('tcn,cn->tc', jnp.exp(-decay_f[None] * steps_f[:, None, None]), mixing, precision=PRECISE)

        def one_row(operands):
            row_input, length = operands
            return row_pass(params, (shift_kernel, diag_kernel), row_input, length)
        outputs = lax.map(jax.checkpoint(one_row), (inputs.reshape(N_DP, ROW, D), seq_lengths))
        return outputs.reshape(TOKENS, D)
    result, pull_back = jax.vjp(forward, tokens.astype(jnp.float32), *weights)
    live = (jnp.arange(ROW)[None, :] < seq_lengths[:, None]).reshape(TOKENS, 1).astype(jnp.float32)
    grads = pull_back(cotangent.astype(jnp.float32) * live)
    return (result.astype(jnp.bfloat16), grads[0].astype(jnp.bfloat16), grads[1], grads[2], grads[3], grads[4], grads[5], grads[6], grads[7], grads[8], grads[9], grads[10], grads[11], grads[12], grads[13], grads[14], grads[15], grads[16], grads[17], grads[18], grads[19])
```

```python
import math
import numpy as np
import jax
import jax.numpy as jnp
from jax import lax
from jax.experimental import pallas as pl
from jax.experimental.pallas import tpu as pltpu
from jax.sharding import PartitionSpec as P

F32 = jnp.float32
BF16 = jnp.bfloat16
BLK = 128
VMEM_LIMIT = 56 * 1024 * 1024


def dot(a, b):
    return jnp.dot(a, b, preferred_element_type=F32)


def dot_nt(a, b):
    return lax.dot_general(a, b, (((1,), (1,)), ((), ())), preferred_element_type=F32)


def split(x):
    high = x.astype(BF16)
    return high, (x - high.astype(F32)).astype(BF16)


def spectral_tables():
    j = np.arange(BLK)
    f = np.arange(BLK)
    angle = 2.0 * np.pi * np.outer(f, j) / (2 * BLK)
    alternating = (-1.0) ** j
    real = np.cos(angle)
    imag = -np.sin(angle)
    imag[0] = alternating
    forward = np.concatenate([real, imag], axis=0)
    weight = np.full((BLK, 1), 2.0)
    weight[0] = 1.0
    back_real = weight * real / (2 * BLK)
    back_imag = 2.0 * imag / (2 * BLK)
    back_imag[0] = alternating / (2 * BLK)
    inverse = np.concatenate([back_real, back_imag], axis=0).T

    def halves(table):
        high = table.astype(jnp.bfloat16)
        low = (table - high.astype(np.float64)).astype(jnp.bfloat16)
        return high, low

    fh, fl = halves(forward)
    ih, il = halves(inverse)
    fwd = np.concatenate([fh, fh, fl], axis=1)
    inv = np.concatenate([ih, il], axis=0)
    return jnp.asarray(fwd), jnp.asarray(inv)


def to_spectrum(fwd_ref, x):
    high, low = split(x)
    return dot(fwd_ref[:, : 2 * BLK], jnp.concatenate([high, low], axis=0)) + dot(
        fwd_ref[:, 2 * BLK :], high
    )


def from_spectrum(inv_ref, z):
    high, low = split(z)
    both = dot(inv_ref[...], high)
    return both[:BLK] + both[BLK:] + dot(inv_ref[:BLK, :], low)


def sign_rows(shape):
    row = lax.broadcasted_iota(jnp.int32, shape, 0)
    return jnp.where(row % 2 == 0, 1.0, -1.0).astype(F32)


def lane_tiles(width):
    return [(s, min(128, width - s)) for s in range(0, width, 128)]


def fix_first(tile, re, im):
    row = lax.broadcasted_iota(jnp.int32, re.shape, 0)
    special = (row == 0) & (tile == 0)
    return jnp.where(special, im, re), jnp.where(special, 0.0, im)


def kgen_body(decay_ref, coef_ref, taps_ref, fwd_ref, kre_ref, kim_ref, tre_ref, tim_ref, mixp, kern):
    states, width = decay_ref.shape
    blocks = kre_ref.shape[0]
    decay = decay_ref[...]
    mixing = jnp.sqrt(2.0 * decay) * coef_ref[...]
    for m in range(blocks):
        mixp[m] = mixing * jnp.exp(decay * (-float(BLK * m)))
    for start, size in lane_tiles(width):
        lanes = slice(start, start + size)

        def per_tile(jt, _, lanes=lanes, size=size):
            steps = (lax.broadcasted_iota(jnp.int32, (8, size), 0) + jt * 8).astype(F32)

            def per_states(ng, acc):
                rows = pl.ds(pl.multiple_of(ng * 8, 8), 8)
                rates = -decay_ref[rows, lanes]
                scales = [mixp[m, rows, lanes] for m in range(blocks)]
                for i in range(8):
                    e = jnp.exp(rates[i : i + 1] * steps)
                    acc = tuple(a + e * s[i : i + 1] for a, s in zip(acc, scales))
                return acc

            acc = lax.fori_loop(
                0, states // 8, per_states, tuple(jnp.zeros((8, size), F32) for _ in range(blocks))
            )
            for m in range(blocks):
                kern[m, pl.ds(pl.multiple_of(jt * 8, 8), 8), lanes] = acc[m]
            return 0

        lax.fori_loop(0, BLK // 8, per_tile, 0)
    for m in range(blocks):
        spec = to_spectrum(fwd_ref, kern[m])
        kre_ref[m] = spec[:BLK]
        kim_ref[m] = spec[BLK:]
    taps = jnp.concatenate(
        [taps_ref[...], jnp.zeros((BLK - taps_ref.shape[0], width), F32)], axis=0
    )
    spec = to_spectrum(fwd_ref, taps)
    tre_ref[...] = spec[:BLK]
    tim_ref[...] = spec[BLK:]


def kernel_spectra(decay_t, coef_t, taps, fwd, length):
    states, width = decay_t.shape
    blocks = length // BLK
    return pl.pallas_call(
        kgen_body,
        out_shape=(
            jax.ShapeDtypeStruct((blocks, BLK, width), F32),
            jax.ShapeDtypeStruct((blocks, BLK, width), F32),
            jax.ShapeDtypeStruct((BLK, width), F32),
            jax.ShapeDtypeStruct((BLK, width), F32),
        ),
        scratch_shapes=[
            pltpu.VMEM((blocks, states, width), F32),
            pltpu.VMEM((blocks, BLK, width), F32),
        ],
        compiler_params=pltpu.CompilerParams(vmem_limit_bytes=VMEM_LIMIT),
        name="kernel_spectra",
    )(decay_t, coef_t, taps, fwd)


def conv_tiles(width, body):
    for start, size in lane_tiles(width):
        lanes = slice(start, start + size)

        def step(ft, _, lanes=lanes):
            body(ft, pl.ds(pl.multiple_of(ft * 8, 8), 8), lanes)
            return 0

        lax.fori_loop(0, BLK // 8, step, 0)


def mixer_fwd_body(
    x_ref, wq_ref, wk_ref, wv_ref, wo_ref, kre_ref, kim_ref, tre_ref, tim_ref, fwd_ref, inv_ref,
    out_ref, mixed_ref, q_ref, v_ref, sh_ref, st_ref, sre_ref, sim_ref, ure_ref, uim_ref,
    zre, zim,
):
    length, width = q_ref.shape
    blocks = length // BLK
    sign = sign_rows((BLK, width))
    row0 = lax.broadcasted_iota(jnp.int32, (BLK, width), 0) == 0
    x = x_ref[...]
    q_ref[...] = dot(x, wq_ref[...])
    v_ref[...] = dot(x, wv_ref[...])
    keys = dot(x, wk_ref[...])
    tre = tre_ref[...]
    tim = tim_ref[...]
    tre2 = jnp.where(row0, tim, tre)
    tim0 = jnp.where(row0, 0.0, tim)
    last = None
    for p in range(blocks):
        rows = slice(p * BLK, (p + 1) * BLK)
        spec = to_spectrum(fwd_ref, keys[rows])
        re, im = spec[:BLK], spec[BLK:]
        sre_ref[p] = re
        sim_ref[p] = im
        pr = re * tre - im * tim0
        pi = re * tim0 + im * tre2
        if last is None:
            z = jnp.concatenate([pr, pi], axis=0)
        else:
            z = jnp.concatenate([pr + sign * last[0], pi + sign * last[1]], axis=0)
        last = (pr, pi)
        shifted = from_spectrum(inv_ref, z)
        sh_ref[rows] = shifted
        spec = to_spectrum(fwd_ref, shifted * v_ref[rows])
        ure_ref[p] = spec[:BLK]
        uim_ref[p] = spec[BLK:]

    def products(ft, fr, lanes):
        sgn = sign[:8, lanes]
        k = [(kre_ref[m, fr, lanes], kim_ref[m, fr, lanes]) for m in range(blocks)]
        k = [(a,) + fix_first(ft, a, b) for a, b in k]
        u = [(ure_ref[m, fr, lanes], uim_ref[m, fr, lanes]) for m in range(blocks)]
        prev = None
        for p in range(blocks):
            yr = yi = None
            for m in range(p + 1):
                ur, ui = u[m]
                kr, kr2, ki0 = k[p - m]
                a = ur * kr - ui * ki0
                b = ur * ki0 + ui * kr2
                yr = a if yr is None else yr + a
                yi = b if yi is None else yi + b
            if prev is None:
                zre[p, fr, lanes] = yr
                zim[p, fr, lanes] = yi
            else:
                zre[p, fr, lanes] = yr + sgn * prev[0]
                zim[p, fr, lanes] = yi + sgn * prev[1]
            prev = (yr, yi)

    conv_tiles(width, products)
    for p in range(blocks):
        rows = slice(p * BLK, (p + 1) * BLK)
        state = from_spectrum(inv_ref, jnp.concatenate([zre[p], zim[p]], axis=0))
        st_ref[rows] = state
        mixed_ref[rows] = (q_ref[rows] * state).astype(BF16)
    out_ref[...] = dot(mixed_ref[...], wo_ref[...]).astype(BF16)


def mixer_forward_kernel(x, wq, wk, wv, wo, kre, kim, tre, tim, fwd, inv):
    length, model = x.shape
    width = wq.shape[1]
    blocks = length // BLK
    row_f = jax.ShapeDtypeStruct((length, width), F32)
    spec_f = jax.ShapeDtypeStruct((blocks, BLK, width), F32)
    return pl.pallas_call(
        mixer_fwd_body,
        out_shape=(
            jax.ShapeDtypeStruct((length, model), BF16),
            jax.ShapeDtypeStruct((length, width), BF16),
            row_f, row_f, row_f, row_f, spec_f, spec_f, spec_f, spec_f,
        ),
        scratch_shapes=[pltpu.VMEM((blocks, BLK, width), F32)] * 2,
        compiler_params=pltpu.CompilerParams(vmem_limit_bytes=VMEM_LIMIT),
        name="mixer_forward",
    )(x, wq, wk, wv, wo, kre, kim, tre, tim, fwd, inv)


def mixer_bwd_body(
    g_ref, wo_ref, q_ref, v_ref, sh_ref, st_ref, sre_ref, sim_ref, ure_ref, uim_ref,
    kre_ref, kim_ref, tre_ref, tim_ref, fwd_ref, inv_ref,
    gq_ref, gk_ref, gv_ref, taps_ref, dk_ref,
    gre, gim, wre, wim, vre, vim,
):
    length, width = q_ref.shape
    blocks = length // BLK
    sign = sign_rows((BLK, width))
    row0 = lax.broadcasted_iota(jnp.int32, (BLK, width), 0) == 0
    grad_mixed = dot_nt(g_ref[...], wo_ref[...])
    for p in range(blocks):
        rows = slice(p * BLK, (p + 1) * BLK)
        gm = grad_mixed[rows]
        gq_ref[rows] = (gm * st_ref[rows]).astype(BF16)
        spec = to_spectrum(fwd_ref, gm * q_ref[rows])
        gre[p] = spec[:BLK]
        gim[p] = spec[BLK:]

    def products(ft, fr, lanes, other_re, other_im, to_re, to_im):
        sgn = sign[:8, lanes]
        k = [(other_re[m, fr, lanes], other_im[m, fr, lanes]) for m in range(blocks)]
        k = [(a,) + fix_first(ft, a, b) for a, b in k]
        g = [(gre[m, fr, lanes], gim[m, fr, lanes]) for m in range(blocks)]
        after = None
        for p in reversed(range(blocks)):
            wr = wi = None
            for m in range(p, blocks):
                gr, gi = g[m]
                kr, kr2, ki0 = k[m - p]
                a = gr * kr + gi * ki0
                b = gi * kr2 - gr * ki0
                wr = a if wr is None else wr + a
                wi = b if wi is None else wi + b
            if after is None:
                to_re[p, fr, lanes] = wr
                to_im[p, fr, lanes] = wi
            else:
                to_re[p, fr, lanes] = wr + sgn * after[0]
                to_im[p, fr, lanes] = wi + sgn * after[1]
            after = (wr, wi)

    conv_tiles(width, lambda ft, fr, lanes: products(ft, fr, lanes, kre_ref, kim_ref, wre, wim))
    tre = tre_ref[...]
    tim = tim_ref[...]
    tre2 = jnp.where(row0, tim, tre)
    tim0 = jnp.where(row0, 0.0, tim)
    after = None
    next_gs = None
    zero = jnp.zeros((BLK, width), F32)
    corr = [zero, zero, zero, zero]
    for p in reversed(range(blocks)):
        rows = slice(p * BLK, (p + 1) * BLK)
        grad_u = from_spectrum(inv_ref, jnp.concatenate([wre[p], wim[p]], axis=0))
        gv_ref[rows] = (grad_u * sh_ref[rows]).astype(BF16)
        spec = to_spectrum(fwd_ref, grad_u * v_ref[rows])
        re, im = spec[:BLK], spec[BLK:]
        pr = re * tre + im * tim0
        pi = im * tre2 - re * tim0
        if after is None:
            z = jnp.concatenate([pr, pi], axis=0)
        else:
            z = jnp.concatenate([pr + sign * after[0], pi + sign * after[1]], axis=0)
        after = (pr, pi)
        gk_ref[rows] = from_spectrum(inv_ref, z).astype(BF16)
        sr, si = sre_ref[p], sim_ref[p]
        sr2 = jnp.where(row0, si, sr)
        si0 = jnp.where(row0, 0.0, si)
        corr[0] = corr[0] + (re * sr + im * si0)
        corr[1] = corr[1] + (im * sr2 - re * si0)
        if next_gs is not None:
            nr, ni = next_gs
            corr[2] = corr[2] + (nr * sr + ni * si0)
            corr[3] = corr[3] + (ni * sr2 - nr * si0)
        next_gs = (re, im)
    z = jnp.concatenate([corr[0] + sign * corr[2], corr[1] + sign * corr[3]], axis=0)
    taps_ref[...] = from_spectrum(inv_ref, z)[: taps_ref.shape[0]]
    conv_tiles(width, lambda ft, fr, lanes: products(ft, fr, lanes, ure_ref, uim_ref, vre, vim))
    for p in range(blocks):
        rows = slice(p * BLK, (p + 1) * BLK)
        dk_ref[rows] = from_spectrum(inv_ref, jnp.concatenate([vre[p], vim[p]], axis=0))


def mixer_backward_kernel(g, wo, saved, kre, kim, tre, tim, fwd, inv, taps):
    q, v, sh, st, sre, sim, ure, uim = saved
    length, width = q.shape
    blocks = length // BLK
    row_b = jax.ShapeDtypeStruct((length, width), BF16)
    return pl.pallas_call(
        mixer_bwd_body,
        out_shape=(
            row_b, row_b, row_b,
            jax.ShapeDtypeStruct((taps, width), F32),
            jax.ShapeDtypeStruct((length, width), F32),
        ),
        scratch_shapes=[pltpu.VMEM((blocks, BLK, width), F32)] * 6,
        compiler_params=pltpu.CompilerParams(vmem_limit_bytes=VMEM_LIMIT),
        name="mixer_backward",
    )(g, wo, q, v, sh, st, sre, sim, ure, uim, kre, kim, tre, tim, fwd, inv)


def ssm_grad_body(dk_ref, decay_ref, coef_ref, gd_ref, gc_ref):
    states, width = decay_ref.shape
    length = dk_ref.shape[0]
    blocks = length // BLK
    group = 4
    for start, size in lane_tiles(width):
        lanes = slice(start, start + size)
        base = lax.broadcasted_iota(jnp.int32, (8, size), 0).astype(F32)

        def per_group(ng, _, lanes=lanes, size=size, base=base):
            rows = pl.ds(pl.multiple_of(ng * 8, 8), 8)
            rates = decay_ref[rows, lanes]
            row_ids = lax.broadcasted_iota(jnp.int32, (8, size), 0)
            sums_a = jnp.zeros((8, size), F32)
            sums_b = jnp.zeros((8, size), F32)
            for half in range(8 // group):
                d = [rates[half * group + i : half * group + i + 1] for i in range(group)]
                p = [jnp.broadcast_to(jnp.exp(-float(BLK) * x), (8, size)) for x in d]
                step8 = [jnp.broadcast_to(jnp.exp(-8.0 * x), (8, size)) for x in d]
                e0 = tuple(jnp.exp(-x * base) for x in d)
                zero = jnp.zeros((8, size), F32)

                def per_tile(jt, carry, p=p, step8=step8):
                    e, a, b = carry
                    steps = base + (jt * 8).astype(F32)
                    dk = [
                        dk_ref[pl.ds(pl.multiple_of(m * BLK + jt * 8, 8), 8), lanes]
                        for m in range(blocks)
                    ]
                    ne, na, nb = [], [], []
                    for i in range(group):
                        h = dk[blocks - 1]
                        s = None
                        for m in reversed(range(blocks - 1)):
                            s = h if s is None else s * p[i] + h
                            h = h * p[i] + dk[m]
                        eh = e[i] * h
                        na.append(a[i] + eh)
                        nb.append(b[i] + steps * eh + (float(BLK) * e[i]) * (s * p[i]))
                        ne.append(e[i] * step8[i])
                    return tuple(ne), tuple(na), tuple(nb)

                _, a, b = lax.fori_loop(
                    0, BLK // 8, per_tile, (e0, (zero,) * group, (zero,) * group)
                )
                for i in range(group):
                    here = row_ids == half * group + i
                    sums_a = jnp.where(here, jnp.sum(a[i], axis=0, keepdims=True), sums_a)
                    sums_b = jnp.where(here, jnp.sum(b[i], axis=0, keepdims=True), sums_b)
            root = jnp.sqrt(2.0 * rates)
            gc_ref[rows, lanes] = root * sums_a
            gd_ref[rows, lanes] = coef_ref[rows, lanes] * (sums_a / root - root * sums_b)
            return 0

        lax.fori_loop(0, states // 8, per_group, 0)


def ssm_grad_kernel(dk, decay_t, coef_t):
    states, width = decay_t.shape
    out = jax.ShapeDtypeStruct((states, width), F32)
    return pl.pallas_call(
        ssm_grad_body,
        out_shape=(out, out),
        compiler_params=pltpu.CompilerParams(vmem_limit_bytes=VMEM_LIMIT),
        name="ssm_grad",
    )(dk, decay_t, coef_t)


HEAD = 64
QROWS = 256


def dot_tn(a, b):
    return lax.dot_general(a, b, (((0,), (0,)), ((), ())), preferred_element_type=F32)


def allowed_keys(keys, first_query, queries, length):
    key = lax.broadcasted_iota(jnp.int32, (keys, queries), 0)
    query = lax.broadcasted_iota(jnp.int32, (keys, queries), 1) + first_query
    return (key <= query) & (key < length)


def attn_fwd_body(len_ref, x_ref, w_ref, out_ref, q_ref, k_ref, v_ref, att_ref, lse_ref):
    rows, width = q_ref.shape
    x = x_ref[...]
    q_ref[...] = dot(x, w_ref[:, :width]).astype(BF16)
    k_ref[...] = dot(x, w_ref[:, width : 2 * width]).astype(BF16)
    v_ref[...] = dot(x, w_ref[:, 2 * width : 3 * width]).astype(BF16)
    length = len_ref[0]
    lse_ref[...] = jnp.zeros(lse_ref.shape, F32)
    scale = HEAD**-0.5
    for h in range(width // HEAD):
        lanes = slice(h * HEAD, (h + 1) * HEAD)
        q = q_ref[:, lanes] * jnp.asarray(scale, BF16)
        k = k_ref[:, lanes]
        vt = v_ref[:, lanes].T
        for first in range(0, rows, QROWS):
            n = first + QROWS
            s = dot_nt(k[:n], q[first:n])
            s = jnp.where(allowed_keys(n, first, QROWS, length), s, -jnp.inf)
            top = jnp.max(s, axis=0, keepdims=True)
            e = jnp.exp(s - top)
            total = jnp.sum(e, axis=0, keepdims=True)
            probs = (e * (1.0 / total)).astype(BF16)
            att_ref[lanes, first:n] = dot(vt[:, :n], probs).astype(BF16)
            lse_ref[h : h + 1, first:n] = top + jnp.log(total)
    out_ref[...] = lax.dot_general(
        att_ref[...], w_ref[:, 3 * width :], (((0,), (1,)), ((), ())), preferred_element_type=F32
    ).astype(BF16)


def attn_forward_kernel(length, x, w):
    rows, model = x.shape
    width = w.shape[1] // 4
    row_b = jax.ShapeDtypeStruct((rows, width), BF16)
    vmem = pl.BlockSpec(memory_space=pltpu.VMEM)
    return pl.pallas_call(
        attn_fwd_body,
        in_specs=[pl.BlockSpec(memory_space=pltpu.SMEM), vmem, vmem],
        out_shape=(
            jax.ShapeDtypeStruct((rows, model), BF16),
            row_b, row_b, row_b,
            jax.ShapeDtypeStruct((width, rows), BF16),
            jax.ShapeDtypeStruct((8, rows), F32),
        ),
        compiler_params=pltpu.CompilerParams(vmem_limit_bytes=VMEM_LIMIT),
        name="attn_forward",
    )(length, x, w)


def attn_bwd_body(
    len_ref, g_ref, w_ref, q_ref, k_ref, v_ref, lse_ref, out_ref, gq_ref, gk_ref, gv_ref, ga, gqt, acck, accv
):
    rows, width = q_ref.shape
    ga[...] = dot(g_ref[...], w_ref[:, 3 * width :]).astype(BF16)
    length = len_ref[0]
    scale = HEAD**-0.5
    acck[...] = jnp.zeros(acck.shape, F32)
    accv[...] = jnp.zeros(accv.shape, F32)
    for h in range(width // HEAD):
        lanes = slice(h * HEAD, (h + 1) * HEAD)
        q = q_ref[:, lanes] * jnp.asarray(scale, BF16)
        k = k_ref[:, lanes]
        kt = k.T
        v = v_ref[:, lanes]
        g = ga[:, lanes]
        for first in range(0, rows, QROWS):
            n = first + QROWS
            s = dot_nt(k[:n], q[first:n])
            probs = jnp.where(
                allowed_keys(n, first, QROWS, length), jnp.exp(s - lse_ref[h : h + 1, first:n]), 0.0
            )
            gp = dot_nt(v[:n], g[first:n])
            inner = jnp.sum(probs * gp, axis=0, keepdims=True)
            gs = (probs * (gp - inner)).astype(BF16)
            gqt[lanes, first:n] = dot(kt[:, :n], gs) * scale
            acck[h, :n] += dot(gs, q[first:n])
            accv[h, :n] += dot(probs.astype(BF16), g[first:n])
        gk_ref[:, lanes] = acck[h].astype(BF16)
        gv_ref[:, lanes] = accv[h].astype(BF16)
    gq_ref[...] = gqt[...].T.astype(BF16)
    out_ref[...] = (
        dot_nt(gq_ref[...], w_ref[:, :width])
        + dot_nt(gk_ref[...], w_ref[:, width : 2 * width])
        + dot_nt(gv_ref[...], w_ref[:, 2 * width : 3 * width])
    ).astype(BF16)


def attn_backward_kernel(length, g, w, q, k, v, lse):
    rows, width = q.shape
    row_b = jax.ShapeDtypeStruct((rows, width), BF16)
    vmem = pl.BlockSpec(memory_space=pltpu.VMEM)
    heads = width // HEAD
    return pl.pallas_call(
        attn_bwd_body,
        in_specs=[pl.BlockSpec(memory_space=pltpu.SMEM)] + [vmem] * 6,
        out_shape=(jax.ShapeDtypeStruct(g.shape, BF16), row_b, row_b, row_b),
        scratch_shapes=[
            pltpu.VMEM((rows, width), BF16),
            pltpu.VMEM((width, rows), F32),
            pltpu.VMEM((heads, rows, HEAD), F32),
            pltpu.VMEM((heads, rows, HEAD), F32),
        ],
        compiler_params=pltpu.CompilerParams(vmem_limit_bytes=VMEM_LIMIT),
        name="attn_backward",
    )(length, g, w, q, k, v, lse)


EPSILON = 1e-05
TENSOR = "tensor"
DATA = "dp"


def swap(x, bit):
    return lax.ppermute(x, TENSOR, [(i, i ^ bit) for i in range(4)])


def norm_rows(hidden, gain):
    average = jnp.mean(hidden, axis=-1, keepdims=True)
    centred = hidden - average
    inverse = lax.rsqrt(jnp.mean(centred * centred, axis=-1, keepdims=True) + EPSILON)
    unit = centred * inverse
    return (unit * gain).astype(BF16), unit, inverse


def norm_back(grad_norm, unit, inverse, gain):
    scaled = grad_norm * gain
    first_mean = jnp.mean(scaled, axis=-1, keepdims=True)
    second_mean = jnp.mean(scaled * unit, axis=-1, keepdims=True)
    return inverse * (scaled - first_mean - unit * second_mean)


def rows_dot(left, right):
    return lax.dot_general(left, right, (((0,), (0,)), ((), ())), preferred_element_type=F32)


def gelu_tanh(values):
    return jax.nn.gelu(values, approximate=True)


class Group:
    def __init__(self):
        index = lax.axis_index(TENSOR)
        self.core = index & 1
        self.chip = index >> 1

    def all_rows(self, mine):
        other = swap(mine, 1)
        first = jnp.where(self.core == 0, mine, other)
        second = jnp.where(self.core == 0, other, mine)
        return jnp.stack([first, second], axis=1).reshape(-1, mine.shape[-1])

    def both_halves(self, mine):
        other = swap(mine, 2)
        first = jnp.where(self.chip == 0, mine, other)
        second = jnp.where(self.chip == 0, other, mine)
        return jnp.stack([first, second], axis=0)

    def total(self, partial):
        quarters = partial.reshape(2, 2, -1, partial.shape[-1])
        keep = lax.dynamic_index_in_dim(quarters, self.core, 1, keepdims=False)
        send = lax.dynamic_index_in_dim(quarters, 1 - self.core, 1, keepdims=False)
        pair = (keep.astype(F32) + swap(send, 1).astype(F32)).astype(BF16)
        return pair.astype(F32) + swap(pair, 2).astype(F32)


def ffn_forward(x, up, down_t):
    hidden = jnp.dot(x, up, preferred_element_type=F32)
    active = gelu_tanh(hidden).astype(BF16)
    out = lax.dot_general(
        active, down_t, (((1,), (1,)), ((), ())), preferred_element_type=F32
    ).astype(BF16)
    return out, hidden


def ffn_backward(x, hidden, grad, up, down_t):
    active, pull = jax.vjp(gelu_tanh, hidden)
    active = active.astype(BF16)
    grad_hidden = pull(jnp.dot(grad, down_t, preferred_element_type=F32))[0].astype(BF16)
    out = lax.dot_general(
        grad_hidden, up, (((1,), (1,)), ((), ())), preferred_element_type=F32
    ).astype(BF16)
    grads = jnp.concatenate([rows_dot(x, grad_hidden), rows_dot(grad, active)], axis=1)
    return out, grads.astype(BF16)


def gather_rows(x):
    return lax.all_gather(x, DATA, axis=0, tiled=True)


def scatter_rows(x):
    return lax.psum_scatter(x, DATA, scatter_dimension=0, tiled=True).astype(F32)


def on_device(
    tokens, cotangent, seq_lengths,
    gain_mixer, mixer_query, mixer_key, mixer_value, shift_taps, ssm_decay, ssm_coef, mixer_out,
    gain_ffn1, ffn1_up, ffn1_down,
    gain_attn, attn_query, attn_key, attn_value, attn_out,
    gain_ffn2, ffn2_up, ffn2_down,
):
    group = Group()
    fwd, inv = spectral_tables()
    quarter, model = tokens.shape
    length = 4 * quarter
    width = mixer_query.shape[1]
    states = ssm_decay.shape[1] * lax.axis_size(DATA)
    taps = shift_taps.shape[0] * lax.axis_size(DATA)

    own_gains = jnp.stack([gain_mixer, gain_ffn1, gain_attn, gain_ffn2], axis=0)
    small = gather_rows(
        jnp.concatenate([shift_taps, ssm_decay.T, ssm_coef.T], axis=1)
    ).astype(F32)
    gains = lax.all_gather(own_gains, DATA, axis=1, tiled=True).astype(F32)
    mixer_w = gather_rows(
        jnp.concatenate([mixer_query, mixer_key, mixer_value, mixer_out.T], axis=1)
    )
    ffn1_w = gather_rows(jnp.concatenate([ffn1_up, ffn1_down.T], axis=1))
    attn_w = gather_rows(jnp.concatenate([attn_query, attn_key, attn_value, attn_out.T], axis=1))
    ffn2_w = gather_rows(jnp.concatenate([ffn2_up, ffn2_down.T], axis=1))
    hidden_units = ffn1_up.shape[1]

    start = group.both_halves(tokens).astype(F32)
    taps_w, decay_t, coef_t = (small[:, i * width : (i + 1) * width] for i in range(3))
    spectra = kernel_spectra(decay_t, coef_t, taps_w, fwd, length)

    normed1, unit1, inverse1 = norm_rows(start, gains[0])
    x1 = group.all_rows(normed1)
    saved = mixer_forward_kernel(
        x1, mixer_w[:, :width], mixer_w[:, width : 2 * width], mixer_w[:, 2 * width : 3 * width],
        mixer_w[:, 3 * width :].T, *spectra, fwd, inv,
    )
    mixed = saved[1]
    after_mixer = start + group.total(saved[0])

    normed2, unit2, inverse2 = norm_rows(after_mixer, gains[1])
    x2 = group.all_rows(normed2)
    out, hidden1 = ffn_forward(x2, ffn1_w[:, :hidden_units], ffn1_w[:, hidden_units:])
    after_ffn1 = after_mixer + group.total(out)

    normed3, unit3, inverse3 = norm_rows(after_ffn1, gains[2])
    x3 = group.all_rows(normed3)
    out, q2, k2, v2, attended_t, log_total = attn_forward_kernel(seq_lengths, x3, attn_w)
    after_attn = after_ffn1 + group.total(out)

    normed4, unit4, inverse4 = norm_rows(after_attn, gains[3])
    x4 = group.all_rows(normed4)
    out, hidden2 = ffn_forward(x4, ffn2_w[:, :hidden_units], ffn2_w[:, hidden_units:])
    final = after_attn + group.total(out)
    output = lax.dynamic_index_in_dim(final, group.chip, 0, keepdims=False).astype(BF16)

    positions = lax.axis_index(TENSOR) * quarter + jnp.arange(quarter)
    live = (positions < seq_lengths[0])[:, None]
    masked = jnp.where(live, cotangent, jnp.zeros_like(cotangent))
    grad_low = group.both_halves(masked)
    grad = grad_low.astype(F32)

    g4 = group.all_rows(grad_low)
    out, ffn2_g = ffn_backward(x4, hidden2, g4, ffn2_w[:, :hidden_units], ffn2_w[:, hidden_units:])
    grad = grad + norm_back(group.total(out), unit4, inverse4, gains[3])
    ffn2_g = scatter_rows(ffn2_g)

    g3 = group.all_rows(grad.astype(BF16))
    out, gq, gk, gv = attn_backward_kernel(seq_lengths, g3, attn_w, q2, k2, v2, log_total)
    attn_g = jnp.concatenate(
        [rows_dot(x3, gq), rows_dot(x3, gk), rows_dot(x3, gv), rows_dot(g3, attended_t.T)], axis=1
    )
    grad = grad + norm_back(group.total(out), unit3, inverse3, gains[2])
    attn_g = scatter_rows(attn_g.astype(BF16))

    g2 = group.all_rows(grad.astype(BF16))
    out, ffn1_g = ffn_backward(x2, hidden1, g2, ffn1_w[:, :hidden_units], ffn1_w[:, hidden_units:])
    grad = grad + norm_back(group.total(out), unit2, inverse2, gains[1])
    ffn1_g = scatter_rows(ffn1_g)

    g1 = group.all_rows(grad.astype(BF16))
    gq, gk, gv, grad_taps, grad_kernel = mixer_backward_kernel(
        g1, mixer_w[:, 3 * width :].T, saved[2:], *spectra, fwd, inv, taps
    )
    grad_joined = jnp.concatenate([gq, gk, gv], axis=1)
    out = lax.dot_general(
        grad_joined, mixer_w[:, : 3 * width], (((1,), (1,)), ((), ())), preferred_element_type=F32
    ).astype(BF16)
    grad = grad + norm_back(group.total(out), unit1, inverse1, gains[0])
    input_grad = lax.dynamic_index_in_dim(grad, group.chip, 0, keepdims=False).astype(BF16)
    mixer_g = scatter_rows(
        jnp.concatenate([rows_dot(x1, grad_joined), rows_dot(g1, mixed)], axis=1).astype(BF16)
    )
    grad_decay, grad_coef = ssm_grad_kernel(grad_kernel, decay_t, coef_t)
    small_g = scatter_rows(
        jnp.concatenate([grad_taps, grad_decay, grad_coef], axis=1).astype(BF16)
    )

    def gain_sum(grads, weights, gain):
        products = sum(g * w.astype(F32) for g, w in zip(grads, weights))
        return jnp.sum(products, axis=1) / gain.astype(F32)

    def cut(grads, size):
        return [grads[:, i : i + size] for i in range(0, grads.shape[1], size)]

    mq, mk, mv, mo = cut(mixer_g, width)
    aq, ak, av, ao = cut(attn_g, width)
    u1, d1 = cut(ffn1_g, hidden_units)
    u2, d2 = cut(ffn2_g, hidden_units)
    gt, gd, gc = cut(small_g, width)
    gain_grads = lax.psum(
        jnp.stack(
            [
                gain_sum((mq, mk, mv), (mixer_query, mixer_key, mixer_value), gain_mixer),
                gain_sum((u1,), (ffn1_up,), gain_ffn1),
                gain_sum((aq, ak, av), (attn_query, attn_key, attn_value), gain_attn),
                gain_sum((u2,), (ffn2_up,), gain_ffn2),
            ]
        ),
        TENSOR,
    )
    return (
        output, input_grad,
        gain_grads[0], mq, mk, mv, gt, gd.T, gc.T, mo.T,
        gain_grads[1], u1, d1.T,
        gain_grads[2], aq, ak, av, ao.T,
        gain_grads[3], u2, d2.T,
    )


def solution(mesh):
    rows = P(("dp", "tensor"), None)
    up = P("dp", "tensor")
    down = P("tensor", "dp")
    vector = P("dp")
    mixer = (vector, up, up, up, up, down, down, down)
    ffn = (vector, up, down)
    attn = (vector, up, up, up, down)
    weights = mixer + ffn + attn + ffn
    return jax.shard_map(
        on_device,
        mesh=mesh,
        in_specs=(rows, rows, vector) + weights,
        out_specs=(rows, rows) + weights,
        check_vma=False,
    )
```

```python
import math
import numpy as np
import jax
import jax.numpy as jnp
from jax import lax
from jax.experimental import pallas as pl
from jax.experimental.pallas import tpu as pltpu
from jax.sharding import PartitionSpec as P

F32 = jnp.float32
BF16 = jnp.bfloat16
BLK = 128
VMEM_LIMIT = 56 * 1024 * 1024


def dot(a, b):
    return jnp.dot(a, b, preferred_element_type=F32)


def dot_nt(a, b):
    return lax.dot_general(a, b, (((1,), (1,)), ((), ())), preferred_element_type=F32)


def split(x):
    high = x.astype(BF16)
    return high, (x - high.astype(F32)).astype(BF16)


def spectral_tables():
    j = np.arange(BLK)
    f = np.arange(BLK)
    angle = 2.0 * np.pi * np.outer(f, j) / (2 * BLK)
    alternating = (-1.0) ** j
    real = np.cos(angle)
    imag = -np.sin(angle)
    imag[0] = alternating
    forward = np.concatenate([real, imag], axis=0)
    weight = np.full((BLK, 1), 2.0)
    weight[0] = 1.0
    back_real = weight * real / (2 * BLK)
    back_imag = 2.0 * imag / (2 * BLK)
    back_imag[0] = alternating / (2 * BLK)
    inverse = np.concatenate([back_real, back_imag], axis=0).T

    def halves(table):
        high = table.astype(jnp.bfloat16)
        low = (table - high.astype(np.float64)).astype(jnp.bfloat16)
        return high, low

    fh, fl = halves(forward)
    ih, il = halves(inverse)
    fwd = np.concatenate([fh, fh, fl], axis=1)
    inv = np.concatenate([ih, il], axis=0)
    return jnp.asarray(fwd), jnp.asarray(inv)


def to_spectrum(fwd_ref, x):
    high, low = split(x)
    return dot(fwd_ref[:, : 2 * BLK], jnp.concatenate([high, low], axis=0)) + dot(
        fwd_ref[:, 2 * BLK :], high
    )


def from_spectrum(inv_ref, z):
    high, low = split(z)
    both = dot(inv_ref[...], high)
    return both[:BLK] + both[BLK:] + dot(inv_ref[:BLK, :], low)


def sign_rows(shape):
    row = lax.broadcasted_iota(jnp.int32, shape, 0)
    return jnp.where(row % 2 == 0, 1.0, -1.0).astype(F32)


def lane_tiles(width):
    return [(s, min(128, width - s)) for s in range(0, width, 128)]


def fix_first(tile, re, im):
    row = lax.broadcasted_iota(jnp.int32, re.shape, 0)
    special = (row == 0) & (tile == 0)
    return jnp.where(special, im, re), jnp.where(special, 0.0, im)


def kgen_body(decay_ref, coef_ref, taps_ref, fwd_ref, kre_ref, kim_ref, tre_ref, tim_ref, mixp, kern):
    states, width = decay_ref.shape
    blocks = kre_ref.shape[0]
    decay = decay_ref[...]
    mixing = jnp.sqrt(2.0 * decay) * coef_ref[...]
    for m in range(blocks):
        mixp[m] = mixing * jnp.exp(decay * (-float(BLK * m)))
    for start, size in lane_tiles(width):
        lanes = slice(start, start + size)

        def per_tile(jt, _, lanes=lanes, size=size):
            steps = (lax.broadcasted_iota(jnp.int32, (8, size), 0) + jt * 8).astype(F32)

            def per_states(ng, acc):
                rows = pl.ds(pl.multiple_of(ng * 8, 8), 8)
                rates = -decay_ref[rows, lanes]
                scales = [mixp[m, rows, lanes] for m in range(blocks)]
                for i in range(8):
                    e = jnp.exp(rates[i : i + 1] * steps)
                    acc = tuple(a + e * s[i : i + 1] for a, s in zip(acc, scales))
                return acc

            acc = lax.fori_loop(
                0, states // 8, per_states, tuple(jnp.zeros((8, size), F32) for _ in range(blocks))
            )
            for m in range(blocks):
                kern[m, pl.ds(pl.multiple_of(jt * 8, 8), 8), lanes] = acc[m]
            return 0

        lax.fori_loop(0, BLK // 8, per_tile, 0)
    for m in range(blocks):
        spec = to_spectrum(fwd_ref, kern[m])
        kre_ref[m] = spec[:BLK]
        kim_ref[m] = spec[BLK:]
    taps = jnp.concatenate(
        [taps_ref[...], jnp.zeros((BLK - taps_ref.shape[0], width), F32)], axis=0
    )
    spec = to_spectrum(fwd_ref, taps)
    tre_ref[...] = spec[:BLK]
    tim_ref[...] = spec[BLK:]


def kernel_spectra(decay_t, coef_t, taps, fwd, length):
    states, width = decay_t.shape
    blocks = length // BLK
    return pl.pallas_call(
        kgen_body,
        out_shape=(
            jax.ShapeDtypeStruct((blocks, BLK, width), F32),
            jax.ShapeDtypeStruct((blocks, BLK, width), F32),
            jax.ShapeDtypeStruct((BLK, width), F32),
            jax.ShapeDtypeStruct((BLK, width), F32),
        ),
        scratch_shapes=[
            pltpu.VMEM((blocks, states, width), F32),
            pltpu.VMEM((blocks, BLK, width), F32),
        ],
        compiler_params=pltpu.CompilerParams(vmem_limit_bytes=VMEM_LIMIT),
        name="kernel_spectra",
    )(decay_t, coef_t, taps, fwd)


def conv_tiles(width, body):
    for start, size in lane_tiles(width):
        lanes = slice(start, start + size)

        def step(ft, _, lanes=lanes):
            body(ft, pl.ds(pl.multiple_of(ft * 8, 8), 8), lanes)
            return 0

        lax.fori_loop(0, BLK // 8, step, 0)


def mixer_fwd_body(
    x_ref, wq_ref, wk_ref, wv_ref, wo_ref, kre_ref, kim_ref, tre_ref, tim_ref, fwd_ref, inv_ref,
    out_ref, mixed_ref, q_ref, v_ref, sh_ref, st_ref, sre_ref, sim_ref, ure_ref, uim_ref,
    zre, zim,
):
    length, width = q_ref.shape
    blocks = length // BLK
    sign = sign_rows((BLK, width))
    row0 = lax.broadcasted_iota(jnp.int32, (BLK, width), 0) == 0
    x = x_ref[...]
    q_ref[...] = dot(x, wq_ref[...])
    v_ref[...] = dot(x, wv_ref[...])
    keys = dot(x, wk_ref[...])
    tre = tre_ref[...]
    tim = tim_ref[...]
    tre2 = jnp.where(row0, tim, tre)
    tim0 = jnp.where(row0, 0.0, tim)
    last = None
    for p in range(blocks):
        rows = slice(p * BLK, (p + 1) * BLK)
        spec = to_spectrum(fwd_ref, keys[rows])
        re, im = spec[:BLK], spec[BLK:]
        sre_ref[p] = re
        sim_ref[p] = im
        pr = re * tre - im * tim0
        pi = re * tim0 + im * tre2
        if last is None:
            z = jnp.concatenate([pr, pi], axis=0)
        else:
            z = jnp.concatenate([pr + sign * last[0], pi + sign * last[1]], axis=0)
        last = (pr, pi)
        shifted = from_spectrum(inv_ref, z)
        sh_ref[rows] = shifted
        spec = to_spectrum(fwd_ref, shifted * v_ref[rows])
        ure_ref[p] = spec[:BLK]
        uim_ref[p] = spec[BLK:]

    def products(ft, fr, lanes):
        sgn = sign[:8, lanes]
        k = [(kre_ref[m, fr, lanes], kim_ref[m, fr, lanes]) for m in range(blocks)]
        k = [(a,) + fix_first(ft, a, b) for a, b in k]
        u = [(ure_ref[m, fr, lanes], uim_ref[m, fr, lanes]) for m in range(blocks)]
        prev = None
        for p in range(blocks):
            yr = yi = None
            for m in range(p + 1):
                ur, ui = u[m]
                kr, kr2, ki0 = k[p - m]
                a = ur * kr - ui * ki0
                b = ur * ki0 + ui * kr2
                yr = a if yr is None else yr + a
                yi = b if yi is None else yi + b
            if prev is None:
                zre[p, fr, lanes] = yr
                zim[p, fr, lanes] = yi
            else:
                zre[p, fr, lanes] = yr + sgn * prev[0]
                zim[p, fr, lanes] = yi + sgn * prev[1]
            prev = (yr, yi)

    conv_tiles(width, products)
    for p in range(blocks):
        rows = slice(p * BLK, (p + 1) * BLK)
        state = from_spectrum(inv_ref, jnp.concatenate([zre[p], zim[p]], axis=0))
        st_ref[rows] = state
        mixed_ref[rows] = (q_ref[rows] * state).astype(BF16)
    out_ref[...] = dot(mixed_ref[...], wo_ref[...]).astype(BF16)


def mixer_forward_kernel(x, wq, wk, wv, wo, kre, kim, tre, tim, fwd, inv):
    length, model = x.shape
    width = wq.shape[1]
    blocks = length // BLK
    row_f = jax.ShapeDtypeStruct((length, width), F32)
    spec_f = jax.ShapeDtypeStruct((blocks, BLK, width), F32)
    return pl.pallas_call(
        mixer_fwd_body,
        out_shape=(
            jax.ShapeDtypeStruct((length, model), BF16),
            jax.ShapeDtypeStruct((length, width), BF16),
            row_f, row_f, row_f, row_f, spec_f, spec_f, spec_f, spec_f,
        ),
        scratch_shapes=[pltpu.VMEM((blocks, BLK, width), F32)] * 2,
        compiler_params=pltpu.CompilerParams(vmem_limit_bytes=VMEM_LIMIT),
        name="mixer_forward",
    )(x, wq, wk, wv, wo, kre, kim, tre, tim, fwd, inv)


def mixer_bwd_body(
    g_ref, wo_ref, q_ref, v_ref, sh_ref, st_ref, sre_ref, sim_ref, ure_ref, uim_ref,
    kre_ref, kim_ref, tre_ref, tim_ref, fwd_ref, inv_ref,
    gq_ref, gk_ref, gv_ref, taps_ref, dk_ref,
    gre, gim, wre, wim, vre, vim,
):
    length, width = q_ref.shape
    blocks = length // BLK
    sign = sign_rows((BLK, width))
    row0 = lax.broadcasted_iota(jnp.int32, (BLK, width), 0) == 0
    grad_mixed = dot_nt(g_ref[...], wo_ref[...])
    for p in range(blocks):
        rows = slice(p * BLK, (p + 1) * BLK)
        gm = grad_mixed[rows]
        gq_ref[rows] = (gm * st_ref[rows]).astype(BF16)
        spec = to_spectrum(fwd_ref, gm * q_ref[rows])
        gre[p] = spec[:BLK]
        gim[p] = spec[BLK:]

    def products(ft, fr, lanes, other_re, other_im, to_re, to_im):
        sgn = sign[:8, lanes]
        k = [(other_re[m, fr, lanes], other_im[m, fr, lanes]) for m in range(blocks)]
        k = [(a,) + fix_first(ft, a, b) for a, b in k]
        g = [(gre[m, fr, lanes], gim[m, fr, lanes]) for m in range(blocks)]
        after = None
        for p in reversed(range(blocks)):
            wr = wi = None
            for m in range(p, blocks):
                gr, gi = g[m]
                kr, kr2, ki0 = k[m - p]
                a = gr * kr + gi * ki0
                b = gi * kr2 - gr * ki0
                wr = a if wr is None else wr + a
                wi = b if wi is None else wi + b
            if after is None:
                to_re[p, fr, lanes] = wr
                to_im[p, fr, lanes] = wi
            else:
                to_re[p, fr, lanes] = wr + sgn * after[0]
                to_im[p, fr, lanes] = wi + sgn * after[1]
            after = (wr, wi)

    conv_tiles(width, lambda ft, fr, lanes: products(ft, fr, lanes, kre_ref, kim_ref, wre, wim))
    tre = tre_ref[...]
    tim = tim_ref[...]
    tre2 = jnp.where(row0, tim, tre)
    tim0 = jnp.where(row0, 0.0, tim)
    after = None
    next_gs = None
    zero = jnp.zeros((BLK, width), F32)
    corr = [zero, zero, zero, zero]
    for p in reversed(range(blocks)):
        rows = slice(p * BLK, (p + 1) * BLK)
        grad_u = from_spectrum(inv_ref, jnp.concatenate([wre[p], wim[p]], axis=0))
        gv_ref[rows] = (grad_u * sh_ref[rows]).astype(BF16)
        spec = to_spectrum(fwd_ref, grad_u * v_ref[rows])
        re, im = spec[:BLK], spec[BLK:]
        pr = re * tre + im * tim0
        pi = im * tre2 - re * tim0
        if after is None:
            z = jnp.concatenate([pr, pi], axis=0)
        else:
            z = jnp.concatenate([pr + sign * after[0], pi + sign * after[1]], axis=0)
        after = (pr, pi)
        gk_ref[rows] = from_spectrum(inv_ref, z).astype(BF16)
        sr, si = sre_ref[p], sim_ref[p]
        sr2 = jnp.where(row0, si, sr)
        si0 = jnp.where(row0, 0.0, si)
        corr[0] = corr[0] + (re * sr + im * si0)
        corr[1] = corr[1] + (im * sr2 - re * si0)
        if next_gs is not None:
            nr, ni = next_gs
            corr[2] = corr[2] + (nr * sr + ni * si0)
            corr[3] = corr[3] + (ni * sr2 - nr * si0)
        next_gs = (re, im)
    z = jnp.concatenate([corr[0] + sign * corr[2], corr[1] + sign * corr[3]], axis=0)
    taps_ref[...] = from_spectrum(inv_ref, z)[: taps_ref.shape[0]]
    conv_tiles(width, lambda ft, fr, lanes: products(ft, fr, lanes, ure_ref, uim_ref, vre, vim))
    for p in range(blocks):
        rows = slice(p * BLK, (p + 1) * BLK)
        dk_ref[rows] = from_spectrum(inv_ref, jnp.concatenate([vre[p], vim[p]], axis=0))


def mixer_backward_kernel(g, wo, saved, kre, kim, tre, tim, fwd, inv, taps):
    q, v, sh, st, sre, sim, ure, uim = saved
    length, width = q.shape
    blocks = length // BLK
    row_b = jax.ShapeDtypeStruct((length, width), BF16)
    return pl.pallas_call(
        mixer_bwd_body,
        out_shape=(
            row_b, row_b, row_b,
            jax.ShapeDtypeStruct((taps, width), F32),
            jax.ShapeDtypeStruct((length, width), F32),
        ),
        scratch_shapes=[pltpu.VMEM((blocks, BLK, width), F32)] * 6,
        compiler_params=pltpu.CompilerParams(vmem_limit_bytes=VMEM_LIMIT),
        name="mixer_backward",
    )(g, wo, q, v, sh, st, sre, sim, ure, uim, kre, kim, tre, tim, fwd, inv)


def ssm_grad_body(dk_ref, decay_ref, coef_ref, gd_ref, gc_ref):
    states, width = decay_ref.shape
    length = dk_ref.shape[0]
    blocks = length // BLK
    group = 4
    for start, size in lane_tiles(width):
        lanes = slice(start, start + size)
        base = lax.broadcasted_iota(jnp.int32, (8, size), 0).astype(F32)

        def per_group(ng, _, lanes=lanes, size=size, base=base):
            rows = pl.ds(pl.multiple_of(ng * 8, 8), 8)
            rates = decay_ref[rows, lanes]
            row_ids = lax.broadcasted_iota(jnp.int32, (8, size), 0)
            sums_a = jnp.zeros((8, size), F32)
            sums_b = jnp.zeros((8, size), F32)
            for half in range(8 // group):
                d = [rates[half * group + i : half * group + i + 1] for i in range(group)]
                p = [jnp.broadcast_to(jnp.exp(-float(BLK) * x), (8, size)) for x in d]
                step8 = [jnp.broadcast_to(jnp.exp(-8.0 * x), (8, size)) for x in d]
                e0 = tuple(jnp.exp(-x * base) for x in d)
                zero = jnp.zeros((8, size), F32)

                def per_tile(jt, carry, p=p, step8=step8):
                    e, a, b = carry
                    steps = base + (jt * 8).astype(F32)
                    dk = [
                        dk_ref[pl.ds(pl.multiple_of(m * BLK + jt * 8, 8), 8), lanes]
                        for m in range(blocks)
                    ]
                    ne, na, nb = [], [], []
                    for i in range(group):
                        h = dk[blocks - 1]
                        s = None
                        for m in reversed(range(blocks - 1)):
                            s = h if s is None else s * p[i] + h
                            h = h * p[i] + dk[m]
                        eh = e[i] * h
                        na.append(a[i] + eh)
                        nb.append(b[i] + steps * eh + (float(BLK) * e[i]) * (s * p[i]))
                        ne.append(e[i] * step8[i])
                    return tuple(ne), tuple(na), tuple(nb)

                _, a, b = lax.fori_loop(
                    0, BLK // 8, per_tile, (e0, (zero,) * group, (zero,) * group)
                )
                for i in range(group):
                    here = row_ids == half * group + i
                    sums_a = jnp.where(here, jnp.sum(a[i], axis=0, keepdims=True), sums_a)
                    sums_b = jnp.where(here, jnp.sum(b[i], axis=0, keepdims=True), sums_b)
            root = jnp.sqrt(2.0 * rates)
            gc_ref[rows, lanes] = root * sums_a
            gd_ref[rows, lanes] = coef_ref[rows, lanes] * (sums_a / root - root * sums_b)
            return 0

        lax.fori_loop(0, states // 8, per_group, 0)


def ssm_grad_kernel(dk, decay_t, coef_t):
    states, width = decay_t.shape
    out = jax.ShapeDtypeStruct((states, width), F32)
    return pl.pallas_call(
        ssm_grad_body,
        out_shape=(out, out),
        compiler_params=pltpu.CompilerParams(vmem_limit_bytes=VMEM_LIMIT),
        name="ssm_grad",
    )(dk, decay_t, coef_t)


HEAD = 64
QROWS = 256


def dot_tn(a, b):
    return lax.dot_general(a, b, (((0,), (0,)), ((), ())), preferred_element_type=F32)


def allowed_keys(keys, first_query, queries, length):
    key = lax.broadcasted_iota(jnp.int32, (keys, queries), 0)
    query = lax.broadcasted_iota(jnp.int32, (keys, queries), 1) + first_query
    return (key <= query) & (key < length)


def attn_fwd_body(len_ref, x_ref, w_ref, out_ref, q_ref, k_ref, v_ref, att_ref, lse_ref):
    rows, width = q_ref.shape
    x = x_ref[...]
    q_ref[...] = dot(x, w_ref[:, :width]).astype(BF16)
    k_ref[...] = dot(x, w_ref[:, width : 2 * width]).astype(BF16)
    v_ref[...] = dot(x, w_ref[:, 2 * width : 3 * width]).astype(BF16)
    length = len_ref[0]
    lse_ref[...] = jnp.zeros(lse_ref.shape, F32)
    scale = HEAD**-0.5
    for h in range(width // HEAD):
        lanes = slice(h * HEAD, (h + 1) * HEAD)
        q = q_ref[:, lanes] * jnp.asarray(scale, BF16)
        k = k_ref[:, lanes]
        vt = v_ref[:, lanes].T
        for first in range(0, rows, QROWS):
            n = first + QROWS
            s = dot_nt(k[:n], q[first:n])
            s = jnp.where(allowed_keys(n, first, QROWS, length), s, -jnp.inf)
            top = jnp.max(s, axis=0, keepdims=True)
            e = jnp.exp(s - top)
            total = jnp.sum(e, axis=0, keepdims=True)
            probs = (e * (1.0 / total)).astype(BF16)
            att_ref[lanes, first:n] = dot(vt[:, :n], probs).astype(BF16)
            lse_ref[h : h + 1, first:n] = top + jnp.log(total)
    out_ref[...] = lax.dot_general(
        att_ref[...], w_ref[:, 3 * width :], (((0,), (1,)), ((), ())), preferred_element_type=F32
    ).astype(BF16)


def attn_forward_kernel(length, x, w):
    rows, model = x.shape
    width = w.shape[1] // 4
    row_b = jax.ShapeDtypeStruct((rows, width), BF16)
    vmem = pl.BlockSpec(memory_space=pltpu.VMEM)
    return pl.pallas_call(
        attn_fwd_body,
        in_specs=[pl.BlockSpec(memory_space=pltpu.SMEM), vmem, vmem],
        out_shape=(
            jax.ShapeDtypeStruct((rows, model), BF16),
            row_b, row_b, row_b,
            jax.ShapeDtypeStruct((width, rows), BF16),
            jax.ShapeDtypeStruct((8, rows), F32),
        ),
        compiler_params=pltpu.CompilerParams(vmem_limit_bytes=VMEM_LIMIT),
        name="attn_forward",
    )(length, x, w)


def attn_bwd_body(
    len_ref, g_ref, w_ref, q_ref, k_ref, v_ref, lse_ref, out_ref, gq_ref, gk_ref, gv_ref, ga, gqt, acck, accv
):
    rows, width = q_ref.shape
    ga[...] = dot(g_ref[...], w_ref[:, 3 * width :]).astype(BF16)
    length = len_ref[0]
    scale = HEAD**-0.5
    acck[...] = jnp.zeros(acck.shape, F32)
    accv[...] = jnp.zeros(accv.shape, F32)
    for h in range(width // HEAD):
        lanes = slice(h * HEAD, (h + 1) * HEAD)
        q = q_ref[:, lanes] * jnp.asarray(scale, BF16)
        k = k_ref[:, lanes]
        kt = k.T
        v = v_ref[:, lanes]
        g = ga[:, lanes]
        for first in range(0, rows, QROWS):
            n = first + QROWS
            s = dot_nt(k[:n], q[first:n])
            probs = jnp.where(
                allowed_keys(n, first, QROWS, length), jnp.exp(s - lse_ref[h : h + 1, first:n]), 0.0
            )
            gp = dot_nt(v[:n], g[first:n])
            inner = jnp.sum(probs * gp, axis=0, keepdims=True)
            gs = (probs * (gp - inner)).astype(BF16)
            gqt[lanes, first:n] = dot(kt[:, :n], gs) * scale
            acck[h, :n] += dot(gs, q[first:n])
            accv[h, :n] += dot(probs.astype(BF16), g[first:n])
        gk_ref[:, lanes] = acck[h].astype(BF16)
        gv_ref[:, lanes] = accv[h].astype(BF16)
    gq_ref[...] = gqt[...].T.astype(BF16)
    out_ref[...] = (
        dot_nt(gq_ref[...], w_ref[:, :width])
        + dot_nt(gk_ref[...], w_ref[:, width : 2 * width])
        + dot_nt(gv_ref[...], w_ref[:, 2 * width : 3 * width])
    ).astype(BF16)


def attn_backward_kernel(length, g, w, q, k, v, lse):
    rows, width = q.shape
    row_b = jax.ShapeDtypeStruct((rows, width), BF16)
    vmem = pl.BlockSpec(memory_space=pltpu.VMEM)
    heads = width // HEAD
    return pl.pallas_call(
        attn_bwd_body,
        in_specs=[pl.BlockSpec(memory_space=pltpu.SMEM)] + [vmem] * 6,
        out_shape=(jax.ShapeDtypeStruct(g.shape, BF16), row_b, row_b, row_b),
        scratch_shapes=[
            pltpu.VMEM((rows, width), BF16),
            pltpu.VMEM((width, rows), F32),
            pltpu.VMEM((heads, rows, HEAD), F32),
            pltpu.VMEM((heads, rows, HEAD), F32),
        ],
        compiler_params=pltpu.CompilerParams(vmem_limit_bytes=VMEM_LIMIT),
        name="attn_backward",
    )(length, g, w, q, k, v, lse)


EPSILON = 1e-05
TENSOR = "tensor"
DATA = "dp"


def swap(x, bit):
    return lax.ppermute(x, TENSOR, [(i, i ^ bit) for i in range(4)])


def norm_rows(hidden, gain):
    average = jnp.mean(hidden, axis=-1, keepdims=True)
    centred = hidden - average
    inverse = lax.rsqrt(jnp.mean(centred * centred, axis=-1, keepdims=True) + EPSILON)
    unit = centred * inverse
    return (unit * gain).astype(BF16), unit, inverse


def norm_back(grad_norm, unit, inverse, gain):
    scaled = grad_norm * gain
    first_mean = jnp.mean(scaled, axis=-1, keepdims=True)
    second_mean = jnp.mean(scaled * unit, axis=-1, keepdims=True)
    return inverse * (scaled - first_mean - unit * second_mean)


def rows_dot(left, right):
    return lax.dot_general(left, right, (((0,), (0,)), ((), ())), preferred_element_type=F32)


def gelu_tanh(values):
    return jax.nn.gelu(values, approximate=True)


class Group:
    def __init__(self):
        index = lax.axis_index(TENSOR)
        self.core = index & 1
        self.chip = index >> 1

    def all_rows(self, mine):
        other = swap(mine, 1)
        first = jnp.where(self.core == 0, mine, other)
        second = jnp.where(self.core == 0, other, mine)
        return jnp.stack([first, second], axis=1).reshape(-1, mine.shape[-1])

    def both_halves(self, mine):
        other = swap(mine, 2)
        first = jnp.where(self.chip == 0, mine, other)
        second = jnp.where(self.chip == 0, other, mine)
        return jnp.stack([first, second], axis=0)

    def total(self, partial):
        quarters = partial.reshape(2, 2, -1, partial.shape[-1])
        keep = lax.dynamic_index_in_dim(quarters, self.core, 1, keepdims=False)
        send = lax.dynamic_index_in_dim(quarters, 1 - self.core, 1, keepdims=False)
        pair = (keep.astype(F32) + swap(send, 1).astype(F32)).astype(BF16)
        return pair.astype(F32) + swap(pair, 2).astype(F32)


def ffn_forward(x, up, down_t):
    hidden = jnp.dot(x, up, preferred_element_type=F32)
    active = gelu_tanh(hidden).astype(BF16)
    out = lax.dot_general(
        active, down_t, (((1,), (1,)), ((), ())), preferred_element_type=F32
    ).astype(BF16)
    return out, hidden


def ffn_backward(x, hidden, grad, up, down_t):
    active, pull = jax.vjp(gelu_tanh, hidden)
    active = active.astype(BF16)
    grad_hidden = pull(jnp.dot(grad, down_t, preferred_element_type=F32))[0].astype(BF16)
    out = lax.dot_general(
        grad_hidden, up, (((1,), (1,)), ((), ())), preferred_element_type=F32
    ).astype(BF16)
    return out, rows_dot(x, grad_hidden), rows_dot(grad, active)


class Rows:
    def __init__(self):
        self.count = lax.axis_size(DATA)
        self.index = lax.axis_index(DATA)
        self.bits = [1 << i for i in reversed(range(self.count.bit_length() - 1))]

    def swap(self, x, bit):
        return lax.ppermute(x, DATA, [(i, i ^ bit) for i in range(self.count)])

    def gather(self, x):
        for bit in self.bits:
            x = jnp.concatenate([x, self.swap(x, bit)], axis=0)
        return x

    def scatter(self, x):
        for bit in reversed(self.bits):
            half = x.shape[0] // 2
            x = x[:half].astype(F32) + self.swap(x[half:].astype(BF16), bit).astype(F32)
        return x

    def order(self, size):
        block = size // self.count
        mask = [0]
        for bit in self.bits:
            mask = mask + [m | bit for m in mask]
        relative = jnp.repeat(jnp.asarray(mask, jnp.int32) ^ self.index, block) * block
        relative = relative + jnp.tile(jnp.arange(block, dtype=jnp.int32), self.count)
        return (jnp.arange(size, dtype=jnp.int32)[:, None] == relative[None, :]).astype(BF16)


def on_device(
    tokens, cotangent, seq_lengths,
    gain_mixer, mixer_query, mixer_key, mixer_value, shift_taps, ssm_decay, ssm_coef, mixer_out,
    gain_ffn1, ffn1_up, ffn1_down,
    gain_attn, attn_query, attn_key, attn_value, attn_out,
    gain_ffn2, ffn2_up, ffn2_down,
):
    group = Group()
    fwd, inv = spectral_tables()
    quarter, model = tokens.shape
    length = 4 * quarter
    width = mixer_query.shape[1]
    states = ssm_decay.shape[1] * lax.axis_size(DATA)
    taps = shift_taps.shape[0] * lax.axis_size(DATA)

    rows = Rows()
    order = rows.order(model)
    taps_order = rows.order(taps)
    block = mixer_query.shape[0]
    unit_rows = shift_taps.shape[0]
    own_gains = jnp.stack([gain_mixer, gain_ffn1, gain_attn, gain_ffn2], axis=0)
    small = jnp.zeros((16, model), BF16)
    small = small.at[:unit_rows, : 3 * width].set(
        jnp.concatenate([shift_taps, ssm_decay.T, ssm_coef.T], axis=1)
    )
    small = small.at[12:16, :block].set(own_gains)
    small = rows.gather(small).reshape(rows.count, 16, model)
    mixer_w = rows.gather(
        jnp.concatenate([mixer_query, mixer_key, mixer_value, mixer_out.T], axis=1)
    )
    up1 = rows.gather(ffn1_up)
    down1 = rows.gather(ffn1_down.T)
    attn_w = rows.gather(jnp.concatenate([attn_query, attn_key, attn_value, attn_out.T], axis=1))
    up2 = rows.gather(ffn2_up)
    down2 = rows.gather(ffn2_down.T)

    def to_relative(x):
        return jnp.dot(x, order, preferred_element_type=F32).astype(BF16)

    def to_true(x):
        return lax.dot_general(
            x.astype(BF16), order, (((1,), (1,)), ((), ())), preferred_element_type=F32
        ).astype(BF16)

    gains = small[:, 12:16, :block].transpose(1, 0, 2).reshape(4, model).astype(F32)
    vectors = small[:, :unit_rows, : 3 * width].reshape(states, 3 * width)
    taps_w = jnp.dot(taps_order, vectors[:, :width], preferred_element_type=F32)
    decay_t = vectors[:, width : 2 * width].astype(F32)
    coef_t = vectors[:, 2 * width :].astype(F32)
    start = group.both_halves(to_relative(tokens)).astype(F32)
    spectra = kernel_spectra(decay_t, coef_t, taps_w, fwd, length)

    normed1, unit1, inverse1 = norm_rows(start, gains[0])
    x1 = group.all_rows(normed1)
    saved = mixer_forward_kernel(
        x1, mixer_w[:, :width], mixer_w[:, width : 2 * width], mixer_w[:, 2 * width : 3 * width],
        mixer_w[:, 3 * width :].T, *spectra, fwd, inv,
    )
    mixed = saved[1]
    after_mixer = start + group.total(saved[0])

    normed2, unit2, inverse2 = norm_rows(after_mixer, gains[1])
    x2 = group.all_rows(normed2)
    out, hidden1 = ffn_forward(x2, up1, down1)
    after_ffn1 = after_mixer + group.total(out)

    normed3, unit3, inverse3 = norm_rows(after_ffn1, gains[2])
    x3 = group.all_rows(normed3)
    out, q2, k2, v2, attended_t, log_total = attn_forward_kernel(seq_lengths, x3, attn_w)
    after_attn = after_ffn1 + group.total(out)

    normed4, unit4, inverse4 = norm_rows(after_attn, gains[3])
    x4 = group.all_rows(normed4)
    out, hidden2 = ffn_forward(x4, up2, down2)
    final = after_attn + group.total(out)
    output = to_true(lax.dynamic_index_in_dim(final, group.chip, 0, keepdims=False))

    positions = lax.axis_index(TENSOR) * quarter + jnp.arange(quarter)
    live = (positions < seq_lengths[0])[:, None]
    masked = jnp.where(live, cotangent, jnp.zeros_like(cotangent))
    grad_low = group.both_halves(to_relative(masked))
    grad = grad_low.astype(F32)

    g4 = group.all_rows(grad_low)
    out, u2, d2 = ffn_backward(x4, hidden2, g4, up2, down2)
    grad = grad + norm_back(group.total(out), unit4, inverse4, gains[3])
    u2 = rows.scatter(u2)
    d2 = rows.scatter(d2)

    g3 = group.all_rows(grad.astype(BF16))
    out, gq, gk, gv = attn_backward_kernel(seq_lengths, g3, attn_w, q2, k2, v2, log_total)
    attn_g = jnp.concatenate(
        [rows_dot(x3, gq), rows_dot(x3, gk), rows_dot(x3, gv), rows_dot(g3, attended_t.T)], axis=1
    )
    grad = grad + norm_back(group.total(out), unit3, inverse3, gains[2])
    attn_g = rows.scatter(attn_g)

    g2 = group.all_rows(grad.astype(BF16))
    out, u1, d1 = ffn_backward(x2, hidden1, g2, up1, down1)
    grad = grad + norm_back(group.total(out), unit2, inverse2, gains[1])
    u1 = rows.scatter(u1)
    d1 = rows.scatter(d1)

    g1 = group.all_rows(grad.astype(BF16))
    gq, gk, gv, grad_taps, grad_kernel = mixer_backward_kernel(
        g1, mixer_w[:, 3 * width :].T, saved[2:], *spectra, fwd, inv, taps
    )
    grad_joined = jnp.concatenate([gq, gk, gv], axis=1)
    out = lax.dot_general(
        grad_joined, mixer_w[:, : 3 * width], (((1,), (1,)), ((), ())), preferred_element_type=F32
    ).astype(BF16)
    grad = grad + norm_back(group.total(out), unit1, inverse1, gains[0])
    input_grad = to_true(lax.dynamic_index_in_dim(grad, group.chip, 0, keepdims=False))
    mixer_g = rows.scatter(
        jnp.concatenate([rows_dot(x1, grad_joined), rows_dot(g1, mixed)], axis=1)
    )
    grad_decay, grad_coef = ssm_grad_kernel(grad_kernel, decay_t, coef_t)
    grad_taps = rows_dot(taps_order, grad_taps.astype(BF16))
    small_g = rows.scatter(jnp.concatenate([grad_taps, grad_decay, grad_coef], axis=1))

    def gain_sum(grads, weights, gain):
        products = sum(g * w.astype(F32) for g, w in zip(grads, weights))
        return jnp.sum(products, axis=1) / gain.astype(F32)

    def cut(grads, size):
        return [grads[:, i : i + size] for i in range(0, grads.shape[1], size)]

    mq, mk, mv, mo = cut(mixer_g, width)
    aq, ak, av, ao = cut(attn_g, width)
    gt, gd, gc = cut(small_g, width)
    gain_grads = lax.psum(
        jnp.stack(
            [
                gain_sum((mq, mk, mv), (mixer_query, mixer_key, mixer_value), gain_mixer),
                gain_sum((u1,), (ffn1_up,), gain_ffn1),
                gain_sum((aq, ak, av), (attn_query, attn_key, attn_value), gain_attn),
                gain_sum((u2,), (ffn2_up,), gain_ffn2),
            ]
        ),
        TENSOR,
    )
    return (
        output, input_grad,
        gain_grads[0], mq, mk, mv, gt, gd.T, gc.T, mo.T,
        gain_grads[1], u1, d1.T,
        gain_grads[2], aq, ak, av, ao.T,
        gain_grads[3], u2, d2.T,
    )


def solution(mesh):
    rows = P(("dp", "tensor"), None)
    up = P("dp", "tensor")
    down = P("tensor", "dp")
    vector = P("dp")
    mixer = (vector, up, up, up, up, down, down, down)
    ffn = (vector, up, down)
    attn = (vector, up, up, up, down)
    weights = mixer + ffn + attn + ffn
    return jax.shard_map(
        on_device,
        mesh=mesh,
        in_specs=(rows, rows, vector) + weights,
        out_specs=(rows, rows) + weights,
        check_vma=False,
    )
```

```python
import numpy as np
import jax
import jax.numpy as jnp
from jax import lax
from jax.experimental import pallas as pl
from jax.experimental.pallas import tpu as pltpu
from jax.experimental.layout import Layout, with_layout_constraint
from jax.sharding import PartitionSpec as P

F32 = jnp.float32
BF16 = jnp.bfloat16
BLK = 128
VMEM_LIMIT = 56 * 1024 * 1024


def cost(us):
    return pl.CostEstimate(
        flops=int(us * 1.1e8), transcendentals=0, bytes_accessed=int(us * 3.5e5)
    )


def dot(a, b):
    return jnp.dot(a, b, preferred_element_type=F32)


def dot_nt(a, b):
    return lax.dot_general(a, b, (((1,), (1,)), ((), ())), preferred_element_type=F32)


def split(x):
    high = x.astype(BF16)
    return high, (x - high.astype(F32)).astype(BF16)


def spectral_tables():
    j = np.arange(BLK)
    f = np.arange(BLK)
    angle = 2.0 * np.pi * np.outer(f, j) / (2 * BLK)
    alternating = (-1.0) ** j
    real = np.cos(angle)
    imag = -np.sin(angle)
    imag[0] = alternating
    forward = np.concatenate([real, imag], axis=0)
    weight = np.full((BLK, 1), 2.0)
    weight[0] = 1.0
    back_real = weight * real / (2 * BLK)
    back_imag = 2.0 * imag / (2 * BLK)
    back_imag[0] = alternating / (2 * BLK)
    inverse = np.concatenate([back_real, back_imag], axis=0).T

    def halves(table):
        high = table.astype(jnp.bfloat16)
        low = (table - high.astype(np.float64)).astype(jnp.bfloat16)
        return high, low

    fh, fl = halves(forward)
    ih, il = halves(inverse)
    fwd = np.concatenate([fh, fh, fl], axis=1)
    inv = np.concatenate([ih, il], axis=0)
    return jnp.asarray(fwd), jnp.asarray(inv)


def to_spectrum(fwd_ref, x):
    high, low = split(x)
    return dot(fwd_ref[:, : 2 * BLK], jnp.concatenate([high, low], axis=0)) + dot(
        fwd_ref[:, 2 * BLK :], high
    )


def from_spectrum(inv_ref, z):
    high, low = split(z)
    both = dot(inv_ref[...], high)
    return both[:BLK] + both[BLK:] + dot(inv_ref[:BLK, :], low)


def sign_rows(shape):
    row = lax.broadcasted_iota(jnp.int32, shape, 0)
    return jnp.where(row % 2 == 0, 1.0, -1.0).astype(F32)


def lane_tiles(width):
    return [(s, min(128, width - s)) for s in range(0, width, 128)]


def fix_first(tile, re, im):
    row = lax.broadcasted_iota(jnp.int32, re.shape, 0)
    special = (row == 0) & (tile == 0)
    return jnp.where(special, im, re), jnp.where(special, 0.0, im)


def kgen_body(decay_ref, coef_ref, taps_ref, fwd_ref, kre_ref, kim_ref, tre_ref, tim_ref, mixp, kern):
    states, width = decay_ref.shape
    blocks = kre_ref.shape[0]
    decay = decay_ref[...]
    mixing = jnp.sqrt(2.0 * decay) * coef_ref[...]
    for m in range(blocks):
        mixp[m] = mixing * jnp.exp(decay * (-float(BLK * m)))
    for start, size in lane_tiles(width):
        lanes = slice(start, start + size)

        def per_tile(jt, _, lanes=lanes, size=size):
            steps = (lax.broadcasted_iota(jnp.int32, (8, size), 0) + jt * 8).astype(F32)

            def per_states(ng, acc):
                rows = pl.ds(pl.multiple_of(ng * 8, 8), 8)
                rates = -decay_ref[rows, lanes]
                scales = [mixp[m, rows, lanes] for m in range(blocks)]
                for i in range(8):
                    e = jnp.exp(rates[i : i + 1] * steps)
                    acc = tuple(a + e * s[i : i + 1] for a, s in zip(acc, scales))
                return acc

            acc = lax.fori_loop(
                0, states // 8, per_states, tuple(jnp.zeros((8, size), F32) for _ in range(blocks))
            )
            for m in range(blocks):
                kern[m, pl.ds(pl.multiple_of(jt * 8, 8), 8), lanes] = acc[m]
            return 0

        lax.fori_loop(0, BLK // 8, per_tile, 0)
    for m in range(blocks):
        spec = to_spectrum(fwd_ref, kern[m])
        kre_ref[m] = spec[:BLK]
        kim_ref[m] = spec[BLK:]
    taps = jnp.concatenate(
        [taps_ref[...], jnp.zeros((BLK - taps_ref.shape[0], width), F32)], axis=0
    )
    spec = to_spectrum(fwd_ref, taps)
    tre_ref[...] = spec[:BLK]
    tim_ref[...] = spec[BLK:]


def kernel_spectra(decay_t, coef_t, taps, fwd, length):
    states, width = decay_t.shape
    blocks = length // BLK
    return pl.pallas_call(
        kgen_body,
        out_shape=(
            jax.ShapeDtypeStruct((blocks, BLK, width), F32),
            jax.ShapeDtypeStruct((blocks, BLK, width), F32),
            jax.ShapeDtypeStruct((BLK, width), F32),
            jax.ShapeDtypeStruct((BLK, width), F32),
        ),
        scratch_shapes=[
            pltpu.VMEM((blocks, states, width), F32),
            pltpu.VMEM((blocks, BLK, width), F32),
        ],
        compiler_params=pltpu.CompilerParams(vmem_limit_bytes=VMEM_LIMIT),
        cost_estimate=cost(11),
        name="kernel_spectra",
    )(decay_t, coef_t, taps, fwd)


def conv_tiles(width, body):
    for start, size in lane_tiles(width):
        lanes = slice(start, start + size)

        def step(ft, _, lanes=lanes):
            body(ft, pl.ds(pl.multiple_of(ft * 8, 8), 8), lanes)
            return 0

        lax.fori_loop(0, BLK // 8, step, 0)


def piece_rows(core, quarter):
    places = []
    for half in range(2):
        for side in (core, 1 - core):
            places.append(pl.ds(pl.multiple_of((2 * half + side) * quarter, quarter), quarter))
    return places


def mixer_fwd_body(
    core_ref, a_ref, b_ref, c_ref, d_ref, w_ref, kre_ref, kim_ref, tre_ref, tim_ref, fwd_ref, inv_ref,
    keep_ref, send_ref,
    x_ref, mixed_ref, q_ref, v_ref, sh_ref, st_ref, sre_ref, sim_ref, ure_ref, uim_ref,
    zre, zim, keys,
):
    length, width = q_ref.shape
    blocks = length // BLK
    sign = sign_rows((BLK, width))
    row0 = lax.broadcasted_iota(jnp.int32, (BLK, width), 0) == 0
    places = piece_rows(core_ref[0], a_ref.shape[0])
    wq = w_ref[:, :width]
    wk = w_ref[:, width : 2 * width]
    wv = w_ref[:, 2 * width : 3 * width]
    for piece_ref, place in zip((a_ref, b_ref, c_ref, d_ref), places):
        piece = piece_ref[...]
        x_ref[place] = piece
        q_ref[place] = dot(piece, wq)
        v_ref[place] = dot(piece, wv)
        keys[place] = dot(piece, wk)
    tre = tre_ref[...]
    tim = tim_ref[...]
    tre2 = jnp.where(row0, tim, tre)
    tim0 = jnp.where(row0, 0.0, tim)
    last = None
    for p in range(blocks):
        rows = slice(p * BLK, (p + 1) * BLK)
        spec = to_spectrum(fwd_ref, keys[rows])
        re, im = spec[:BLK], spec[BLK:]
        sre_ref[p] = re
        sim_ref[p] = im
        pr = re * tre - im * tim0
        pi = re * tim0 + im * tre2
        if last is None:
            z = jnp.concatenate([pr, pi], axis=0)
        else:
            z = jnp.concatenate([pr + sign * last[0], pi + sign * last[1]], axis=0)
        last = (pr, pi)
        shifted = from_spectrum(inv_ref, z)
        sh_ref[rows] = shifted
        spec = to_spectrum(fwd_ref, shifted * v_ref[rows])
        ure_ref[p] = spec[:BLK]
        uim_ref[p] = spec[BLK:]

    def products(ft, fr, lanes):
        sgn = sign[:8, lanes]
        k = [(kre_ref[m, fr, lanes], kim_ref[m, fr, lanes]) for m in range(blocks)]
        k = [(a,) + fix_first(ft, a, b) for a, b in k]
        u = [(ure_ref[m, fr, lanes], uim_ref[m, fr, lanes]) for m in range(blocks)]
        prev = None
        for p in range(blocks):
            yr = yi = None
            for m in range(p + 1):
                ur, ui = u[m]
                kr, kr2, ki0 = k[p - m]
                a = ur * kr - ui * ki0
                b = ur * ki0 + ui * kr2
                yr = a if yr is None else yr + a
                yi = b if yi is None else yi + b
            if prev is None:
                zre[p, fr, lanes] = yr
                zim[p, fr, lanes] = yi
            else:
                zre[p, fr, lanes] = yr + sgn * prev[0]
                zim[p, fr, lanes] = yi + sgn * prev[1]
            prev = (yr, yi)

    conv_tiles(width, products)
    wo = w_ref[:, 3 * width :]
    for half in range(2):
        for p in range(half * blocks // 2, (half + 1) * blocks // 2):
            rows = slice(p * BLK, (p + 1) * BLK)
            state = from_spectrum(inv_ref, jnp.concatenate([zre[p], zim[p]], axis=0))
            st_ref[rows] = state
            mixed_ref[rows] = (q_ref[rows] * state).astype(BF16)
        for out_ref, place in zip((keep_ref, send_ref), places[2 * half : 2 * half + 2]):
            out_ref[half] = dot_nt(mixed_ref[place], wo).astype(BF16)


SCALAR = pl.BlockSpec(memory_space=pltpu.SMEM)
WHOLE = pl.BlockSpec(memory_space=pltpu.VMEM)


def mixer_forward_kernel(core, pieces, w, spectra, fwd, inv):
    quarter, model = pieces[0].shape
    length = 4 * quarter
    width = w.shape[1] // 4
    blocks = length // BLK
    row_f = jax.ShapeDtypeStruct((length, width), F32)
    spec_f = jax.ShapeDtypeStruct((blocks, BLK, width), F32)
    piece = jax.ShapeDtypeStruct((2, quarter, model), BF16)
    return pl.pallas_call(
        mixer_fwd_body,
        in_specs=[SCALAR] + [WHOLE] * 11,
        out_shape=(
            piece, piece,
            jax.ShapeDtypeStruct((length, model), BF16),
            jax.ShapeDtypeStruct((length, width), BF16),
            row_f, row_f, row_f, row_f, spec_f, spec_f, spec_f, spec_f,
        ),
        scratch_shapes=[pltpu.VMEM((blocks, BLK, width), F32)] * 2
        + [pltpu.VMEM((length, width), F32)],
        compiler_params=pltpu.CompilerParams(vmem_limit_bytes=VMEM_LIMIT),
        cost_estimate=cost(14),
        name="mixer_forward",
    )(core, *pieces, w, *spectra, fwd, inv)


def correlate_tiles(width, blocks, left, other, result):
    left_re, left_im = left
    other_re, other_im = other
    to_re, to_im = result
    sign = sign_rows((8, width))

    def products(ft, fr, lanes):
        sgn = sign[:, lanes]
        k = [(other_re[m, fr, lanes], other_im[m, fr, lanes]) for m in range(blocks)]
        k = [(a,) + fix_first(ft, a, b) for a, b in k]
        g = [(left_re[m, fr, lanes], left_im[m, fr, lanes]) for m in range(blocks)]
        after = None
        for p in reversed(range(blocks)):
            wr = wi = None
            for m in range(p, blocks):
                gr, gi = g[m]
                kr, kr2, ki0 = k[m - p]
                a = gr * kr + gi * ki0
                b = gi * kr2 - gr * ki0
                wr = a if wr is None else wr + a
                wi = b if wi is None else wi + b
            if after is None:
                to_re[p, fr, lanes] = wr
                to_im[p, fr, lanes] = wi
            else:
                to_re[p, fr, lanes] = wr + sgn * after[0]
                to_im[p, fr, lanes] = wi + sgn * after[1]
            after = (wr, wi)

    conv_tiles(width, products)


def mixer_bwd_body(
    core_ref, a_ref, b_ref, c_ref, d_ref, w_ref, q_ref, v_ref, sh_ref, st_ref, sre_ref, sim_ref,
    kre_ref, kim_ref, tre_ref, tim_ref, fwd_ref, inv_ref,
    keep_ref, send_ref, g_ref, gp_ref, taps_ref, gre, gim,
    wre, wim, grad_mixed,
):
    length, width = q_ref.shape
    blocks = length // BLK
    sign = sign_rows((BLK, width))
    row0 = lax.broadcasted_iota(jnp.int32, (BLK, width), 0) == 0
    places = piece_rows(core_ref[0], a_ref.shape[0])
    wo = w_ref[:, 3 * width :]
    for piece_ref, place in zip((a_ref, b_ref, c_ref, d_ref), places):
        piece = piece_ref[...]
        g_ref[place] = piece
        grad_mixed[place] = dot(piece, wo)
    for p in range(blocks):
        rows = slice(p * BLK, (p + 1) * BLK)
        gm = grad_mixed[rows]
        gp_ref[rows, :width] = (gm * st_ref[rows]).astype(BF16)
        spec = to_spectrum(fwd_ref, gm * q_ref[rows])
        gre[p] = spec[:BLK]
        gim[p] = spec[BLK:]
    correlate_tiles(width, blocks, (gre, gim), (kre_ref, kim_ref), (wre, wim))
    tre = tre_ref[...]
    tim = tim_ref[...]
    tre2 = jnp.where(row0, tim, tre)
    tim0 = jnp.where(row0, 0.0, tim)
    after = None
    next_gs = None
    zero = jnp.zeros((BLK, width), F32)
    corr = [zero, zero, zero, zero]
    for p in reversed(range(blocks)):
        rows = slice(p * BLK, (p + 1) * BLK)
        grad_u = from_spectrum(inv_ref, jnp.concatenate([wre[p], wim[p]], axis=0))
        gp_ref[rows, 2 * width :] = (grad_u * sh_ref[rows]).astype(BF16)
        spec = to_spectrum(fwd_ref, grad_u * v_ref[rows])
        re, im = spec[:BLK], spec[BLK:]
        pr = re * tre + im * tim0
        pi = im * tre2 - re * tim0
        if after is None:
            z = jnp.concatenate([pr, pi], axis=0)
        else:
            z = jnp.concatenate([pr + sign * after[0], pi + sign * after[1]], axis=0)
        after = (pr, pi)
        gp_ref[rows, width : 2 * width] = from_spectrum(inv_ref, z).astype(BF16)
        sr, si = sre_ref[p], sim_ref[p]
        sr2 = jnp.where(row0, si, sr)
        si0 = jnp.where(row0, 0.0, si)
        corr[0] = corr[0] + (re * sr + im * si0)
        corr[1] = corr[1] + (im * sr2 - re * si0)
        if next_gs is not None:
            nr, ni = next_gs
            corr[2] = corr[2] + (nr * sr + ni * si0)
            corr[3] = corr[3] + (ni * sr2 - nr * si0)
        next_gs = (re, im)
    z = jnp.concatenate([corr[0] + sign * corr[2], corr[1] + sign * corr[3]], axis=0)
    taps_ref[...] = from_spectrum(inv_ref, z)[: taps_ref.shape[0]]
    wp = w_ref[:, : 3 * width]
    for i, place in enumerate(places):
        (keep_ref, send_ref)[i % 2][i // 2] = dot_nt(gp_ref[place], wp).astype(BF16)


def mixer_backward_kernel(core, pieces, w, saved, spectra, fwd, inv, taps):
    quarter, model = pieces[0].shape
    length = 4 * quarter
    width = w.shape[1] // 4
    blocks = length // BLK
    piece = jax.ShapeDtypeStruct((2, quarter, model), BF16)
    spec_f = jax.ShapeDtypeStruct((blocks, BLK, width), F32)
    return pl.pallas_call(
        mixer_bwd_body,
        in_specs=[SCALAR] + [WHOLE] * 17,
        out_shape=(
            piece, piece,
            jax.ShapeDtypeStruct((length, model), BF16),
            jax.ShapeDtypeStruct((length, 3 * width), BF16),
            jax.ShapeDtypeStruct((taps, width), F32),
            spec_f, spec_f,
        ),
        scratch_shapes=[pltpu.VMEM((blocks, BLK, width), F32)] * 2
        + [pltpu.VMEM((length, width), F32)],
        compiler_params=pltpu.CompilerParams(vmem_limit_bytes=VMEM_LIMIT),
        cost_estimate=cost(15),
        name="mixer_backward",
    )(core, *pieces, w, *saved, *spectra, fwd, inv)


def ssm_grad_body(
    gre, gim, ure, uim, decay_ref, coef_ref, inv_ref, gd_ref, gc_ref, vre, vim, dk_ref
):
    states, width = decay_ref.shape
    blocks = gre.shape[0]
    correlate_tiles(width, blocks, (gre, gim), (ure, uim), (vre, vim))
    for p in range(blocks):
        dk_ref[p * BLK : (p + 1) * BLK] = from_spectrum(
            inv_ref, jnp.concatenate([vre[p], vim[p]], axis=0)
        )
    group = 4
    for start, size in lane_tiles(width):
        lanes = slice(start, start + size)
        base = lax.broadcasted_iota(jnp.int32, (8, size), 0).astype(F32)

        def per_group(ng, _, lanes=lanes, size=size, base=base):
            rows = pl.ds(pl.multiple_of(ng * 8, 8), 8)
            rates = decay_ref[rows, lanes]
            row_ids = lax.broadcasted_iota(jnp.int32, (8, size), 0)
            sums_a = jnp.zeros((8, size), F32)
            sums_b = jnp.zeros((8, size), F32)
            for half in range(8 // group):
                d = [rates[half * group + i : half * group + i + 1] for i in range(group)]
                p = [jnp.broadcast_to(jnp.exp(-float(BLK) * x), (8, size)) for x in d]
                step8 = [jnp.broadcast_to(jnp.exp(-8.0 * x), (8, size)) for x in d]
                e0 = tuple(jnp.exp(-x * base) for x in d)
                zero = jnp.zeros((8, size), F32)

                def per_tile(jt, carry, p=p, step8=step8):
                    e, a, b = carry
                    steps = base + (jt * 8).astype(F32)
                    dk = [
                        dk_ref[pl.ds(pl.multiple_of(m * BLK + jt * 8, 8), 8), lanes]
                        for m in range(blocks)
                    ]
                    ne, na, nb = [], [], []
                    for i in range(group):
                        h = dk[blocks - 1]
                        s = None
                        for m in reversed(range(blocks - 1)):
                            s = h if s is None else s * p[i] + h
                            h = h * p[i] + dk[m]
                        eh = e[i] * h
                        na.append(a[i] + eh)
                        nb.append(b[i] + steps * eh + (float(BLK) * e[i]) * (s * p[i]))
                        ne.append(e[i] * step8[i])
                    return tuple(ne), tuple(na), tuple(nb)

                _, a, b = lax.fori_loop(
                    0, BLK // 8, per_tile, (e0, (zero,) * group, (zero,) * group)
                )
                for i in range(group):
                    here = row_ids == half * group + i
                    sums_a = jnp.where(here, jnp.sum(a[i], axis=0, keepdims=True), sums_a)
                    sums_b = jnp.where(here, jnp.sum(b[i], axis=0, keepdims=True), sums_b)
            root = jnp.sqrt(2.0 * rates)
            gc_ref[rows, lanes] = root * sums_a
            gd_ref[rows, lanes] = coef_ref[rows, lanes] * (sums_a / root - root * sums_b)
            return 0

        lax.fori_loop(0, states // 8, per_group, 0)


def ssm_grad_kernel(g_spectrum, u_spectrum, decay_t, coef_t, inv):
    states, width = decay_t.shape
    blocks = g_spectrum[0].shape[0]
    out = jax.ShapeDtypeStruct((states, width), F32)
    return pl.pallas_call(
        ssm_grad_body,
        out_shape=(out, out),
        scratch_shapes=[pltpu.VMEM((blocks, BLK, width), F32)] * 2
        + [pltpu.VMEM((blocks * BLK, width), F32)],
        compiler_params=pltpu.CompilerParams(vmem_limit_bytes=VMEM_LIMIT),
        cost_estimate=cost(19),
        name="ssm_grad",
    )(*g_spectrum, *u_spectrum, decay_t, coef_t, inv)


HEAD = 64
QROWS = 256


def dot_tn(a, b):
    return lax.dot_general(a, b, (((0,), (0,)), ((), ())), preferred_element_type=F32)


def allowed_keys(keys, first_query, queries, length):
    key = lax.broadcasted_iota(jnp.int32, (keys, queries), 0)
    query = lax.broadcasted_iota(jnp.int32, (keys, queries), 1) + first_query
    return (key <= query) & (key < length)


def attn_fwd_body(
    core_ref, len_ref, a_ref, b_ref, c_ref, d_ref, w_ref,
    keep_ref, send_ref, x_ref, q_ref, k_ref, v_ref, att_ref, lse_ref,
):
    rows, width = q_ref.shape
    places = piece_rows(core_ref[0], a_ref.shape[0])
    wq = w_ref[:, :width]
    wk = w_ref[:, width : 2 * width]
    wv = w_ref[:, 2 * width : 3 * width]
    for piece_ref, place in zip((a_ref, b_ref, c_ref, d_ref), places):
        piece = piece_ref[...]
        x_ref[place] = piece
        q_ref[place] = dot(piece, wq).astype(BF16)
        k_ref[place] = dot(piece, wk).astype(BF16)
        v_ref[place] = dot(piece, wv).astype(BF16)
    length = len_ref[0]
    lse_ref[...] = jnp.zeros(lse_ref.shape, F32)
    scale = HEAD**-0.5
    for h in range(width // HEAD):
        lanes = slice(h * HEAD, (h + 1) * HEAD)
        q = q_ref[:, lanes] * jnp.asarray(scale, BF16)
        k = k_ref[:, lanes]
        vt = v_ref[:, lanes].T
        for first in range(0, rows, QROWS):
            n = first + QROWS
            s = dot_nt(k[:n], q[first:n])
            s = jnp.where(allowed_keys(n, first, QROWS, length), s, -jnp.inf)
            top = jnp.max(s, axis=0, keepdims=True)
            e = jnp.exp(s - top)
            total = jnp.sum(e, axis=0, keepdims=True)
            probs = (e * (1.0 / total)).astype(BF16)
            att_ref[lanes, first:n] = dot(vt[:, :n], probs).astype(BF16)
            lse_ref[h : h + 1, first:n] = top + jnp.log(total)
    wo = w_ref[:, 3 * width :]
    out = lax.dot_general(
        att_ref[...], wo, (((0,), (1,)), ((), ())), preferred_element_type=F32
    ).astype(BF16)
    quarter = a_ref.shape[0]
    first = core_ref[0] == 0
    for half in range(2):
        low = out[2 * half * quarter : (2 * half + 1) * quarter]
        high = out[(2 * half + 1) * quarter : (2 * half + 2) * quarter]
        keep_ref[half] = jnp.where(first, low, high)
        send_ref[half] = jnp.where(first, high, low)


def attn_forward_kernel(core, length, pieces, w):
    quarter, model = pieces[0].shape
    rows = 4 * quarter
    width = w.shape[1] // 4
    row_b = jax.ShapeDtypeStruct((rows, width), BF16)
    piece = jax.ShapeDtypeStruct((2, quarter, model), BF16)
    return pl.pallas_call(
        attn_fwd_body,
        in_specs=[SCALAR, SCALAR] + [WHOLE] * 5,
        out_shape=(
            piece, piece,
            jax.ShapeDtypeStruct((rows, model), BF16),
            row_b, row_b, row_b,
            jax.ShapeDtypeStruct((width, rows), BF16),
            jax.ShapeDtypeStruct((8, rows), F32),
        ),
        compiler_params=pltpu.CompilerParams(vmem_limit_bytes=VMEM_LIMIT),
        cost_estimate=cost(12),
        name="attn_forward",
    )(core, length, *pieces, w)


def attn_bwd_body(
    core_ref, len_ref, a_ref, b_ref, c_ref, d_ref, w_ref, q_ref, k_ref, v_ref, lse_ref,
    keep_ref, send_ref, g_ref, gp_ref, ga, gqt, acck, accv
):
    rows, width = q_ref.shape
    places = piece_rows(core_ref[0], a_ref.shape[0])
    wo = w_ref[:, 3 * width :]
    for piece_ref, place in zip((a_ref, b_ref, c_ref, d_ref), places):
        piece = piece_ref[...]
        g_ref[place] = piece
        ga[place] = dot(piece, wo).astype(BF16)
    length = len_ref[0]
    scale = HEAD**-0.5
    acck[...] = jnp.zeros(acck.shape, F32)
    accv[...] = jnp.zeros(accv.shape, F32)
    for h in range(width // HEAD):
        lanes = slice(h * HEAD, (h + 1) * HEAD)
        q = q_ref[:, lanes] * jnp.asarray(scale, BF16)
        k = k_ref[:, lanes]
        kt = k.T
        v = v_ref[:, lanes]
        g = ga[:, lanes]
        for first in range(0, rows, QROWS):
            n = first + QROWS
            s = dot_nt(k[:n], q[first:n])
            probs = jnp.where(
                allowed_keys(n, first, QROWS, length), jnp.exp(s - lse_ref[h : h + 1, first:n]), 0.0
            )
            gp = dot_nt(v[:n], g[first:n])
            inner = jnp.sum(probs * gp, axis=0, keepdims=True)
            gs = (probs * (gp - inner)).astype(BF16)
            gqt[lanes, first:n] = dot(kt[:, :n], gs) * scale
            acck[h, :n] += dot(gs, q[first:n])
            accv[h, :n] += dot(probs.astype(BF16), g[first:n])
        gp_ref[:, width + h * HEAD : width + (h + 1) * HEAD] = acck[h].astype(BF16)
        gp_ref[:, 2 * width + h * HEAD : 2 * width + (h + 1) * HEAD] = accv[h].astype(BF16)
    gp_ref[:, :width] = gqt[...].T.astype(BF16)
    wp = w_ref[:, : 3 * width]
    for i, place in enumerate(places):
        (keep_ref, send_ref)[i % 2][i // 2] = dot_nt(gp_ref[place], wp).astype(BF16)


def attn_backward_kernel(core, length, pieces, w, q, k, v, lse):
    quarter, model = pieces[0].shape
    rows, width = q.shape
    piece = jax.ShapeDtypeStruct((2, quarter, model), BF16)
    heads = width // HEAD
    return pl.pallas_call(
        attn_bwd_body,
        in_specs=[SCALAR, SCALAR] + [WHOLE] * 9,
        out_shape=(
            piece, piece,
            jax.ShapeDtypeStruct((rows, model), BF16),
            jax.ShapeDtypeStruct((rows, 3 * width), BF16),
        ),
        scratch_shapes=[
            pltpu.VMEM((rows, width), BF16),
            pltpu.VMEM((width, rows), F32),
            pltpu.VMEM((heads, rows, HEAD), F32),
            pltpu.VMEM((heads, rows, HEAD), F32),
        ],
        compiler_params=pltpu.CompilerParams(vmem_limit_bytes=VMEM_LIMIT),
        cost_estimate=cost(14),
        name="attn_backward",
    )(core, length, *pieces, w, q, k, v, lse)


EPSILON = 1e-05


def kernel_call(body, outs, name, us, scalars=0, scratch=()):
    def call(*args):
        return pl.pallas_call(
            body,
            in_specs=[SCALAR] * scalars + [WHOLE] * (len(args) - scalars),
            out_shape=outs,
            scratch_shapes=list(scratch),
            cost_estimate=cost(us),
            compiler_params=pltpu.CompilerParams(vmem_limit_bytes=VMEM_LIMIT),
            name=name,
        )(*args)

    return call


def shaped(shape, dtype):
    return jax.ShapeDtypeStruct(shape, dtype)


def statistics(h):
    average = jnp.mean(h, axis=1, keepdims=True)
    centred = h - average
    inverse = lax.rsqrt(jnp.mean(centred * centred, axis=1, keepdims=True) + EPSILON)
    return centred * inverse, inverse


def norm_gradient(grad_normed, h, gain):
    unit, inverse = statistics(h)
    scaled = grad_normed * gain
    first_mean = jnp.mean(scaled, axis=1, keepdims=True)
    second_mean = jnp.mean(scaled * unit, axis=1, keepdims=True)
    return inverse * (scaled - first_mean - unit * second_mean)


def first_norm_body(chip_ref, mine_ref, other_ref, gain_ref, h0_ref, n0_ref, h1_ref, n1_ref):
    mine = mine_ref[...].astype(F32)
    other = other_ref[...].astype(F32)
    first = chip_ref[0] == 0
    for h, h_ref, n_ref in (
        (jnp.where(first, mine, other), h0_ref, n0_ref),
        (jnp.where(first, other, mine), h1_ref, n1_ref),
    ):
        h_ref[...] = h
        unit, _ = statistics(h)
        n_ref[...] = (unit * gain_ref[...]).astype(BF16)


def first_norm(chip, mine, other, gain):
    state, normed = shaped(mine.shape, F32), shaped(mine.shape, BF16)
    outs = (state, normed, state, normed)
    return kernel_call(first_norm_body, outs, "first_norm", 2.5, 1)(chip, mine, other, gain)


def both(pair_ref, received_ref):
    return pair_ref[...].astype(F32) + received_ref[...].astype(F32)


def norm_body(h_ref, pair_ref, received_ref, gain_ref, state_ref, normed_ref):
    h = h_ref[...] + both(pair_ref, received_ref)
    state_ref[...] = h
    unit, _ = statistics(h)
    normed_ref[...] = (unit * gain_ref[...]).astype(BF16)


def norm_step(h, pair, received, gain):
    outs = (shaped(h.shape, F32), shaped(h.shape, BF16))
    return kernel_call(norm_body, outs, "norm_step", 1.5)(h, pair, received, gain)


def back_body(g_ref, pair_ref, received_ref, h_ref, gain_ref, grad_ref, low_ref):
    grad = g_ref[...].astype(F32) + norm_gradient(
        both(pair_ref, received_ref), h_ref[...], gain_ref[...]
    )
    grad_ref[...] = grad
    low_ref[...] = grad.astype(BF16)


def back_step(g, pair, received, h, gain):
    outs = (shaped(g.shape, F32), shaped(g.shape, BF16))
    return kernel_call(back_body, outs, "back_step", 2)(g, pair, received, h, gain)


def last_back_body(chip_ref, g0, p0, h0, g1, p1, h1, received_ref, gain_ref, out_ref):
    first = chip_ref[0] == 0
    grad_normed = jnp.where(first, p0[...], p1[...]).astype(F32) + received_ref[...].astype(F32)
    h = jnp.where(first, h0[...], h1[...])
    grad = jnp.where(first, g0[...], g1[...])
    out_ref[...] = (grad + norm_gradient(grad_normed, h, gain_ref[...])).astype(BF16)


def last_back(chip, grads, pairs, states, received, gain):
    outs = shaped(received.shape, BF16)
    return kernel_call(last_back_body, outs, "last_back", 2, 1)(
        chip, grads[0], pairs[0], states[0], grads[1], pairs[1], states[1], received, gain
    )


ROOT = 0.7978845608028654
CUBIC = 0.044715


def gelu(u):
    return 0.5 * u * (1.0 + jnp.tanh(ROOT * (u + CUBIC * u * u * u)))


def gelu_parts(u):
    square = u * u
    t = jnp.tanh(ROOT * (u + CUBIC * u * square))
    half = 0.5 * (1.0 + t)
    slope = half + 0.5 * u * (1.0 - t * t) * (ROOT * (1.0 + 3.0 * CUBIC * square))
    return u * half, slope


def ffn_fwd_body(
    h_ref, pair_ref, received_ref, gain_ref, own_ref, mate_ref, state_ref, n_ref, hidden_ref, out_ref
):
    units = own_ref.shape[1] // 2
    h = h_ref[...] + both(pair_ref, received_ref)
    state_ref[...] = h
    unit, _ = statistics(h)
    n = (unit * gain_ref[...]).astype(BF16)
    n_ref[...] = n
    out = None
    for side, w_ref in enumerate((own_ref, mate_ref)):
        hidden = dot(n, w_ref[:, :units])
        hidden_ref[:, side * units : (side + 1) * units] = hidden
        part = dot_nt(gelu(hidden).astype(BF16), w_ref[:, units:])
        out = part if out is None else out + part
    out_ref[...] = out.astype(BF16)


def ffn_forward(h, pair, received, gain, own, mate):
    piece = shaped(h.shape, BF16)
    outs = (shaped(h.shape, F32), piece, shaped((h.shape[0], own.shape[1]), F32), piece)
    return kernel_call(ffn_fwd_body, outs, "ffn_forward", 5)(h, pair, received, gain, own, mate)


def ffn_both_body(
    h_ref, pair_ref, received_ref, gain_ref, g_ref, own_ref, mate_ref,
    state_ref, n_ref, grad_ref, active_ref, out_ref,
):
    units = own_ref.shape[1] // 2
    h = h_ref[...] + both(pair_ref, received_ref)
    state_ref[...] = h
    unit, _ = statistics(h)
    n = (unit * gain_ref[...]).astype(BF16)
    n_ref[...] = n
    g = g_ref[...]
    out = None
    for side, w_ref in enumerate((own_ref, mate_ref)):
        lanes = slice(side * units, (side + 1) * units)
        active, slope = gelu_parts(dot(n, w_ref[:, :units]))
        active_ref[:, lanes] = active.astype(BF16)
        grad = (dot(g, w_ref[:, units:]) * slope).astype(BF16)
        grad_ref[:, lanes] = grad
        part = dot_nt(grad, w_ref[:, :units])
        out = part if out is None else out + part
    out_ref[...] = out.astype(BF16)


def ffn_both(h, pair, received, gain, g, own, mate):
    piece = shaped(h.shape, BF16)
    rows = shaped((h.shape[0], own.shape[1]), BF16)
    outs = (shaped(h.shape, F32), piece, rows, rows, piece)
    return kernel_call(ffn_both_body, outs, "ffn_both", 6)(h, pair, received, gain, g, own, mate)


def ffn_bwd_body(
    g_ref, pair_ref, received_ref, h_ref, gain_ref, hidden_ref, own_ref, mate_ref,
    total_ref, low_ref, grad_ref, active_ref, out_ref,
):
    units = own_ref.shape[1] // 2
    total = g_ref[...] + norm_gradient(both(pair_ref, received_ref), h_ref[...], gain_ref[...])
    total_ref[...] = total
    g = total.astype(BF16)
    low_ref[...] = g
    out = None
    for side, w_ref in enumerate((own_ref, mate_ref)):
        lanes = slice(side * units, (side + 1) * units)
        active, slope = gelu_parts(hidden_ref[:, lanes])
        active_ref[:, lanes] = active.astype(BF16)
        grad = (dot(g, w_ref[:, units:]) * slope).astype(BF16)
        grad_ref[:, lanes] = grad
        part = dot_nt(grad, w_ref[:, :units])
        out = part if out is None else out + part
    out_ref[...] = out.astype(BF16)


def ffn_backward(g, pair, received, h, gain, hidden, own, mate):
    piece = shaped(h.shape, BF16)
    rows = shaped(hidden.shape, BF16)
    outs = (shaped(h.shape, F32), piece, rows, rows, piece)
    return kernel_call(ffn_bwd_body, outs, "ffn_backward", 6)(
        g, pair, received, h, gain, hidden, own, mate
    )


def ffn_out_body(a0_ref, a1_ref, own_ref, mate_ref, out0_ref, out1_ref):
    units = own_ref.shape[1] // 2
    for a_ref, out_ref in ((a0_ref, out0_ref), (a1_ref, out1_ref)):
        out = dot_nt(a_ref[:, :units], own_ref[:, units:]) + dot_nt(
            a_ref[:, units:], mate_ref[:, units:]
        )
        out_ref[...] = out.astype(BF16)


def ffn_out(active0, active1, own, mate):
    piece = shaped((active0.shape[0], own.shape[0]), BF16)
    return kernel_call(ffn_out_body, (piece, piece), "ffn_out", 3)(active0, active1, own, mate)


def ffn_grads_body(n0, n1, g0, g1, gh0, gh1, a0, a1, own_ref, mate_ref):
    units = own_ref.shape[1] // 2
    for side, out_ref in ((1, mate_ref), (0, own_ref)):
        lanes = slice(side * units, (side + 1) * units)
        out_ref[:, :units] = (
            dot_tn(n0[...], gh0[:, lanes]) + dot_tn(n1[...], gh1[:, lanes])
        ).astype(BF16)
        out_ref[:, units:] = (
            dot_tn(g0[...], a0[:, lanes]) + dot_tn(g1[...], a1[:, lanes])
        ).astype(BF16)


def ffn_grads(n, g, grad_hidden, active):
    outs = shaped((n[0].shape[1], active[0].shape[1]), BF16)
    return kernel_call(ffn_grads_body, (outs, outs), "ffn_grads", 6)(
        *n, *g, *grad_hidden, *active
    )


def attn_grads_body(x_ref, gp_ref, g_ref, att_ref, own_ref, mate_ref, out_ref):
    first = own_ref.shape[1]
    joined = first + gp_ref.shape[1]
    out_ref[:, :first] = (own_ref[...].astype(F32) + mate_ref[...].astype(F32)).astype(BF16)
    out_ref[:, first:joined] = dot_tn(x_ref[...], gp_ref[...]).astype(BF16)
    out_ref[:, joined:] = lax.dot_general(
        g_ref[...], att_ref[...], (((0,), (1,)), ((), ())), preferred_element_type=F32
    ).astype(BF16)


def attn_grads(x, joined, g, attended_t, own, mate):
    columns = own.shape[1] + joined.shape[1] + attended_t.shape[0]
    outs = shaped((x.shape[1], columns), BF16)
    return kernel_call(attn_grads_body, outs, "attn_grads", 8)(
        x, joined, g, attended_t, own, mate
    )


def halved(side, count, bit, rows_of, keep_ref, send_ref):
    block = keep_ref.shape[0] * 2 // count
    place = 0
    for j in range(count):
        if j & bit:
            continue
        low, high = rows_of(j * block, block), rows_of((j | bit) * block, block)
        here = slice(place, place + block)
        keep_ref[here] = jnp.where(side == 0, low, high).astype(BF16)
        send_ref[here] = jnp.where(side == 0, high, low).astype(BF16)
        place += block


def halves_of(rows, columns):
    return (shaped((rows // 2, columns), BF16),) * 2


def ffn_cut(side, own, mate, count, bit):
    def body(side_ref, own_ref, mate_ref, keep_ref, send_ref):
        def rows_of(first, size):
            here = slice(first, first + size)
            return own_ref[here].astype(F32) + mate_ref[here].astype(F32)

        halved(side_ref[0], count, bit, rows_of, keep_ref, send_ref)

    return kernel_call(body, halves_of(*own.shape), "ffn_cut", 3, 1)(side, own, mate)


def mixer_grads(side, x, joined, g, mixed, count, bit):
    model, columns = x.shape[1], joined.shape[1] + mixed.shape[1]

    def body(side_ref, x_ref, gp_ref, g_ref, mixed_ref, keep_ref, send_ref, total):
        total[:, : gp_ref.shape[1]] = dot_tn(x_ref[...], gp_ref[...])
        total[:, gp_ref.shape[1] :] = dot_tn(g_ref[...], mixed_ref[...])
        halved(
            side_ref[0], count, bit, lambda first, size: total[first : first + size], keep_ref, send_ref
        )

    return kernel_call(
        body, halves_of(model, columns), "mixer_grads", 6, 1, [pltpu.VMEM((model, columns), F32)]
    )(side, x, joined, g, mixed)


TENSOR = "tensor"
DATA = "dp"


def swap(x, bit):
    return lax.ppermute(x, TENSOR, [(i, i ^ bit) for i in range(4)])


def from_mate(x):
    return swap(x, 1)


def from_chip(x):
    return swap(x, 2)


def tie(*values):
    return lax.optimization_barrier(values)


def after(value, *others):
    return lax.optimization_barrier((value,) + others)[0]


def row_major(x):
    return with_layout_constraint(x, Layout(major_to_minor=tuple(range(x.ndim))))


def add_cores(keep, send):
    return (keep.astype(F32) + from_mate(send).astype(F32)).astype(BF16)


class Rows:
    def __init__(self):
        self.count = lax.axis_size(DATA)
        self.index = lax.axis_index(DATA)
        self.depth = self.count.bit_length() - 1
        self.bits = [1 << i for i in reversed(range(self.depth))]

    def swap(self, x, bit):
        return lax.ppermute(x, DATA, [(i, i ^ bit) for i in range(self.count)])

    def gather_send(self, x, step):
        return self.swap(x, self.bits[step])

    def gather_merge(self, x, other, step):
        upper = (self.index & self.bits[step]) != 0
        return jnp.stack([jnp.where(upper, other, x), jnp.where(upper, x, other)], axis=step)

    def gather_step(self, x, step):
        return self.gather_merge(x, self.gather_send(x, step), step)

    def gather(self, x, first=0, last=None):
        for step in range(first, self.depth if last is None else last):
            x = self.gather_step(x, step)
        return x

    def flat(self, x):
        return x.reshape(self.count * x.shape[-2], x.shape[-1])

    def parts(self, x):
        return x.reshape((2,) * self.depth + (x.shape[0] // self.count, x.shape[1]))

    def cut(self, x, step):
        side = ((self.index & self.bits[step]) != 0).astype(jnp.int32)
        keep = lax.dynamic_slice_in_dim(x, side, 1, step)
        send = lax.dynamic_slice_in_dim(x, 1 - side, 1, step)
        return keep, send.astype(BF16)

    def side(self, step):
        return ((self.index & self.bits[step]) != 0).astype(jnp.int32).reshape(1)

    def without(self, x, step):
        shape = [2] * self.depth
        shape[step] = 1
        return x.reshape(tuple(shape) + (x.shape[0] * 2 // self.count, x.shape[1]))

    def scatter(self, x, steps):
        for step in steps:
            keep, send = self.cut(x, step)
            x = keep.astype(F32) + self.swap(send, self.bits[step]).astype(F32)
        return x.reshape(x.shape[-2:])


def on_device(
    tokens, cotangent, seq_lengths,
    gain_mixer, mixer_query, mixer_key, mixer_value, shift_taps, ssm_decay, ssm_coef, mixer_out,
    gain_ffn1, ffn1_up, ffn1_down,
    gain_attn, attn_query, attn_key, attn_value, attn_out,
    gain_ffn2, ffn2_up, ffn2_down,
):
    place = lax.axis_index(TENSOR)
    chip = place >> 1
    core = (place & 1).astype(jnp.int32).reshape(1)
    chips = chip.astype(jnp.int32).reshape(1)
    rows = Rows()
    fwd, inv = spectral_tables()
    quarter, model = tokens.shape
    length = 4 * quarter
    block, width = mixer_query.shape
    units = ffn1_up.shape[1]
    unit_rows = shift_taps.shape[0]
    states = unit_rows * rows.count

    own_gains = jnp.stack([gain_mixer, gain_ffn1, gain_attn, gain_ffn2], axis=0)
    small = jnp.zeros((16, model), BF16)
    small = small.at[:unit_rows, : 3 * width].set(
        jnp.concatenate([shift_taps, ssm_decay.T, ssm_coef.T], axis=1)
    )
    small = small.at[12:16, :block].set(own_gains)
    mixer_own = jnp.concatenate([mixer_query, mixer_key, mixer_value, mixer_out.T], axis=1)
    ffn1_own = jnp.concatenate([ffn1_up, ffn1_down.T], axis=1)
    attn_own = jnp.concatenate([attn_query, attn_key, attn_value, attn_out.T], axis=1)
    ffn2_own = jnp.concatenate([ffn2_up, ffn2_down.T], axis=1)
    top = rows.depth - 1
    positions = place * quarter + jnp.arange(quarter)
    live = (positions < seq_lengths[0])[:, None]
    masked = jnp.where(live, cotangent, jnp.zeros_like(cotangent))
    small = rows.gather(small, 0, 1)
    mixer_w = rows.gather(mixer_own, 0, 1)
    there = from_chip(tokens)
    first_w = lax.all_gather(
        jnp.concatenate([ffn1_own, attn_own], axis=1), DATA, axis=0, tiled=True
    )
    small = rows.gather(small, 1, top)
    mixer_w = rows.gather(mixer_w, 1, top)
    small = rows.gather(small, top).reshape(rows.count, 16, model)
    small, mixer_w = tie(small, mixer_w)
    mixer_other = rows.gather_send(mixer_w, top)

    gains = small[:, 12:16, :block].transpose(1, 0, 2).reshape(4, 1, model).astype(F32)
    vectors = small[:, :unit_rows, : 3 * width].reshape(states, 3 * width).astype(F32)
    taps_w, decay_t, coef_t = (vectors[:, i * width : (i + 1) * width] for i in range(3))
    h0, n0, h1, n1 = first_norm(chips, tokens, there, gains[0])
    start = [h0, h1]
    grad_other = from_chip(after(masked, n0))
    spectra = kernel_spectra(after(decay_t, n0), coef_t, taps_w, fwd, length)
    pieces = [n0, from_mate(n0), n1, from_mate(n1)]
    mixer_other, grad_other = after((mixer_other, grad_other), spectra[0])
    mixer_w = rows.flat(rows.gather_merge(mixer_w, mixer_other, top))
    keep, send, x1, mixed, *saved = mixer_forward_kernel(
        core, pieces, mixer_w, spectra, fwd, inv
    )

    def core_sums(keep, send):
        other = from_mate(send)
        return [(keep[i].astype(F32) + other[i].astype(F32)).astype(BF16) for i in range(2)]

    def exchanged(keep, send):
        sums = core_sums(keep, send)
        return sums, [from_chip(p) for p in sums]

    pairs, received = exchanged(keep, send)
    first_w = after(first_w, pairs[1])
    ffn1_w, attn_w = first_w[:, : 2 * units], first_w[:, 2 * units :]
    ffn1_mate = from_mate(ffn1_w)
    ffn2_w = lax.all_gather(after(ffn2_own, pairs[1]), DATA, axis=0, tiled=True)
    ffn1_mate = after(ffn1_mate, received[0])
    after_mixer, n2, hidden1, nexts, arrived = [], [], [], [], []
    for half in range(2):
        wait = received[0] if half == 0 else after(received[1], nexts[0])
        h, n, hidden, out = ffn_forward(
            start[half], pairs[half], wait, gains[1], ffn1_w, ffn1_mate
        )
        after_mixer.append(h)
        n2.append(n)
        hidden1.append(hidden)
        nexts.append(out)
        arrived.append(from_chip(out))
    after_ffn1, pieces = [], []
    for half in range(2):
        wait = after(arrived[half], nexts[1]) if half == 0 else after(arrived[1], pieces[0])
        h, n = norm_step(after_mixer[half], nexts[half], wait, gains[2])
        after_ffn1.append(h)
        pieces += [n, from_mate(n)]
    attn_w, pieces[2] = tie(attn_w, pieces[2])
    keep, send, x3, q2, k2, v2, attended_t, log_total = attn_forward_kernel(
        core, seq_lengths, pieces, attn_w
    )
    pairs, received = exchanged(keep, send)

    ffn2_w = after(ffn2_w, pairs[1])
    ffn2_mate = from_mate(ffn2_w)
    grad = [jnp.where(chip == 0, masked, grad_other), jnp.where(chip == 0, grad_other, masked)]
    g4 = list(grad)
    ffn2_mate = after(ffn2_mate, received[0])
    after_attn, n4, gh, act, nexts, arrived = [], [], [], [], [], []
    for half in range(2):
        wait = received[0] if half == 0 else after(received[1], nexts[0])
        h, n, grad_hidden, active, out = ffn_both(
            after_ffn1[half], pairs[half], wait, gains[3], g4[half], ffn2_w, ffn2_mate
        )
        after_attn.append(h)
        n4.append(n)
        gh.append(grad_hidden)
        act.append(active)
        nexts.append(out)
        arrived.append(from_chip(out))
    lows = []
    wait = after(arrived[0], nexts[1])
    grad[0], low = back_step(grad[0], nexts[0], wait, after_attn[0], gains[3])
    lows.append(low)
    gh, act = after((gh, act), low)
    own, mate = ffn_grads(n4, g4, gh, act)
    wait = after(arrived[1], mate)
    grad[1], low = back_step(grad[1], nexts[1], wait, after_attn[1], gains[3])
    lows.append(low)
    pieces = [lows[0], from_mate(after(lows[0], low)), lows[1], from_mate(lows[1])]
    ffn2_mate_g = from_mate(after(mate, pieces[1], pieces[3]))
    keep, send, g3, grad_joined = attn_backward_kernel(
        core, seq_lengths, pieces, attn_w, q2, k2, v2, log_total
    )
    pairs, received = exchanged(keep, send)
    own, ffn2_mate_g = after((own, ffn2_mate_g), pairs[1])
    second_p = attn_grads(x3, grad_joined, g3, attended_t, own, ffn2_mate_g)
    second_g = lax.psum_scatter(second_p, DATA, scatter_dimension=0, tiled=True)
    step = rows.depth - 1
    received[0] = after(received[0], second_p)
    final = ffn_out(*after(tuple(act), second_p), ffn2_w, ffn2_mate)
    final_sent = jnp.where(chip == 0, final[1], final[0])
    received[0], final_sent = tie(received[0], final_sent)

    g2, gh, act_b, nexts, arrived = [], [], [], [], []
    for half in range(2):
        wait = received[0] if half == 0 else after(received[1], nexts[0])
        grad[half], low, grad_hidden, active, out = ffn_backward(
            grad[half].astype(F32), pairs[half], wait, after_ffn1[half], gains[2], hidden1[half],
            ffn1_w, ffn1_mate,
        )
        g2.append(low)
        gh.append(grad_hidden)
        act_b.append(active)
        nexts.append(out)
        arrived.append(from_chip(out))
    lows = []
    wait = after(arrived[0], nexts[1])
    grad[0], low = back_step(grad[0], nexts[0], wait, after_mixer[0], gains[1])
    lows.append(low)
    gh, act_b = after((gh, act_b), low)
    own, mate = ffn_grads(n2, g2, gh, act_b)
    wait = after(arrived[1], mate)
    grad[1], low = back_step(grad[1], nexts[1], wait, after_mixer[1], gains[1])
    lows.append(low)
    final_sent = after(final_sent, low)
    mate_g = from_mate(after(mate, low))
    pieces = [lows[0], from_mate(lows[0]), lows[1], from_mate(lows[1])]
    mate_g, pieces[1], pieces[3] = tie(mate_g, pieces[1], pieces[3])
    ffn1_keep, ffn1_send = ffn_cut(rows.side(step), own, mate_g, rows.count, rows.bits[step])
    pieces[0], ffn1_send, final_sent = tie(pieces[0], ffn1_send, final_sent)
    ffn1_received = rows.swap(ffn1_send, rows.bits[step])
    final_received = from_chip(final_sent)
    keep, send, g1, grad_joined, grad_taps, *g_spectrum = mixer_backward_kernel(
        core, pieces, mixer_w, saved[:6], spectra, fwd, inv, states
    )
    final_received = after(final_received, keep)
    mixer_keep, mixer_send = mixer_grads(
        rows.side(step - 1), x1, grad_joined, g1, mixed, rows.count, rows.bits[step - 1]
    )
    mixer_received = rows.swap(mixer_send, rows.bits[step - 1])
    g_spectrum = after(tuple(g_spectrum), mixer_send, second_g)
    grad_decay, grad_coef = ssm_grad_kernel(g_spectrum, saved[6:], decay_t, coef_t, inv)
    ffn1_received, send = after((ffn1_received, send), grad_decay)
    last = core_sums(keep, send)
    last_sent = jnp.where(chip == 0, last[1], last[0])
    last_received = from_chip(last_sent)
    ffn1_g = rows.without(ffn1_keep.astype(F32) + ffn1_received.astype(F32), step)
    ffn1_keep, ffn1_send = rows.cut(ffn1_g, step - 1)
    ffn1_received = rows.swap(ffn1_send, rows.bits[step - 1])
    mixer_received = after(mixer_received, ffn1_send)
    mixer_g = rows.without(mixer_keep.astype(F32) + mixer_received.astype(F32), step - 1)
    small_g = rows.parts(jnp.concatenate([grad_taps, grad_decay, grad_coef], axis=1))
    mixer_g, small_g, last_received = tie(mixer_g, small_g, last_received)
    rest = list(reversed(range(step - 1)))
    mixer_g = rows.scatter(mixer_g, [step] + rest)
    small_g = rows.scatter(small_g, [step, step - 1] + rest)
    ffn1_g = rows.scatter(ffn1_keep.astype(F32) + ffn1_received.astype(F32), rest)
    output = jnp.where(chip == 0, after_attn[0], after_attn[1]) + (
        jnp.where(chip == 0, final[0], final[1]).astype(F32) + final_received.astype(F32)
    )
    second_g = second_g.astype(F32)
    ffn2_g, attn_g = second_g[:, : 2 * units], second_g[:, 2 * units :]
    input_grad = last_back(chips, grad, last, start, last_received, gains[0])

    def gain_sum(grads, weights, gain):
        products = sum(g * w.astype(F32) for g, w in zip(grads, weights))
        return jnp.sum(products, axis=1) / gain.astype(F32)

    def cut(grads, size):
        return [grads[:, i : i + size] for i in range(0, grads.shape[1], size)]

    mq, mk, mv, mo = cut(mixer_g, width)
    aq, ak, av, ao = cut(attn_g, width)
    u1, d1 = cut(ffn1_g, units)
    u2, d2 = cut(ffn2_g, units)
    gt, gd, gc = cut(small_g, width)
    gain_grads = jnp.stack(
        [
            gain_sum((mq, mk, mv), (mixer_query, mixer_key, mixer_value), gain_mixer),
            gain_sum((u1,), (ffn1_up,), gain_ffn1),
            gain_sum((aq, ak, av), (attn_query, attn_key, attn_value), gain_attn),
            gain_sum((u2,), (ffn2_up,), gain_ffn2),
        ]
    )
    gain_grads = gain_grads + swap(gain_grads, 1)
    gain_grads = gain_grads + swap(gain_grads, 2)
    return (
        output.astype(BF16), input_grad,
        gain_grads[0], mq, mk, mv, gt, gd.T, gc.T, mo.T,
        gain_grads[1], u1, d1.T,
        gain_grads[2], aq, ak, av, ao.T,
        gain_grads[3], u2, d2.T,
    )


def solution(mesh):
    rows = P(("dp", "tensor"), None)
    up = P("dp", "tensor")
    down = P("tensor", "dp")
    vector = P("dp")
    mixer = (vector, up, up, up, up, down, down, down)
    ffn = (vector, up, down)
    attn = (vector, up, up, up, down)
    weights = mixer + ffn + attn + ffn
    return jax.shard_map(
        on_device,
        mesh=mesh,
        in_specs=(rows, rows, vector) + weights,
        out_specs=(rows, rows) + weights,
        check_vma=False,
    )
```

```python
import numpy as np
import jax
import jax.numpy as jnp
from jax import lax
from jax.experimental import pallas as pl
from jax.experimental.pallas import tpu as pltpu
from jax.experimental.layout import Layout, with_layout_constraint
from jax.sharding import PartitionSpec as P

F32 = jnp.float32
BF16 = jnp.bfloat16
BLK = 128
GROUP = 8
UNROLL = 2
VMEM_LIMIT = 56 * 1024 * 1024


def cost(us):
    return pl.CostEstimate(
        flops=int(us * 1.1e8), transcendentals=0, bytes_accessed=int(us * 3.5e5)
    )


def dot(a, b):
    return jnp.dot(a, b, preferred_element_type=F32)


def dot_nt(a, b):
    return lax.dot_general(a, b, (((1,), (1,)), ((), ())), preferred_element_type=F32)


def split(x):
    high = x.astype(BF16)
    return high, (x - high.astype(F32)).astype(BF16)


def spectral_tables():
    j = np.arange(BLK)
    f = np.arange(BLK)
    angle = 2.0 * np.pi * np.outer(f, j) / (2 * BLK)
    alternating = (-1.0) ** j
    real = np.cos(angle)
    imag = -np.sin(angle)
    imag[0] = alternating
    forward = np.concatenate([real, imag], axis=0)
    weight = np.full((BLK, 1), 2.0)
    weight[0] = 1.0
    back_real = weight * real / (2 * BLK)
    back_imag = 2.0 * imag / (2 * BLK)
    back_imag[0] = alternating / (2 * BLK)
    inverse = np.concatenate([back_real, back_imag], axis=0).T

    def halves(table):
        high = table.astype(jnp.bfloat16)
        low = (table - high.astype(np.float64)).astype(jnp.bfloat16)
        return high, low

    fh, fl = halves(forward)
    ih, il = halves(inverse)
    fwd = np.concatenate([fh, fh, fl], axis=1)
    inv = np.concatenate([ih, il], axis=0)
    return jnp.asarray(fwd), jnp.asarray(inv)


def to_spectrum_exact(fwd_ref, x):
    high, low = split(x)
    return dot(fwd_ref[:, : 2 * BLK], jnp.concatenate([high, low], axis=0)) + dot(
        fwd_ref[:, 2 * BLK :], high
    )


def to_spectrum(fwd_ref, x):
    return dot(fwd_ref[:, :BLK], x.astype(BF16))


def from_spectrum(inv_ref, re, im):
    return dot(inv_ref[:BLK], jnp.concatenate([re.astype(BF16), im.astype(BF16)], axis=0))


def sign_rows(shape):
    row = lax.broadcasted_iota(jnp.int32, shape, 0)
    return jnp.where(row % 2 == 0, 1.0, -1.0).astype(F32)


def lane_tiles(width):
    return [(s, min(128, width - s)) for s in range(0, width, 128)]


def fix_first(tile, re, im):
    row = lax.broadcasted_iota(jnp.int32, re.shape, 0)
    special = (row == 0) & (tile == 0)
    return jnp.where(special, im, re), jnp.where(special, 0.0, im)


def channel_tiles(width):
    return [(s, min(128, width - s), 128 // min(128, width - s)) for s in range(0, width, 128)]


def side_by_side(x, start, size, copies):
    rows = x.shape[0] // copies
    parts = [x[i * rows : (i + 1) * rows, start : start + size] for i in range(copies)]
    return parts[0] if copies == 1 else jnp.concatenate(parts, axis=1)


def kgen_body(decay_ref, coef_ref, taps_ref, fwd_ref, kre_ref, kim_ref, tre_ref, tim_ref, rate, mixp, kern):
    states, width = decay_ref.shape
    blocks = kre_ref.shape[0]
    decay = decay_ref[...]
    mixing = jnp.sqrt(2.0 * decay) * coef_ref[...]
    for start, size, copies in channel_tiles(width):
        rows = states // copies
        tile_decay = side_by_side(decay, start, size, copies)
        tile_mixing = side_by_side(mixing, start, size, copies)
        rate[:rows] = -tile_decay
        for m in range(blocks):
            mixp[m, :rows] = tile_mixing * jnp.exp(tile_decay * (-float(BLK * m)))

        def per_tile(jt, _, start=start, size=size, copies=copies, rows=rows):
            steps = (lax.broadcasted_iota(jnp.int32, (8, 128), 0) + jt * 8).astype(F32)

            def per_states(ng, acc):
                here = pl.ds(pl.multiple_of(ng * 8, 8), 8)
                rates = rate[here]
                scales = [mixp[m, here] for m in range(blocks)]
                for i in range(8):
                    e = jnp.exp(rates[i : i + 1] * steps)
                    acc = tuple(a + e * s[i : i + 1] for a, s in zip(acc, scales))
                return acc

            acc = lax.fori_loop(
                0, rows // 8, per_states, tuple(jnp.zeros((8, 128), F32) for _ in range(blocks))
            )
            place = pl.ds(pl.multiple_of(jt * 8, 8), 8)
            for m in range(blocks):
                total = acc[m][:, :size]
                for i in range(1, copies):
                    total = total + acc[m][:, i * size : (i + 1) * size]
                kern[m, place, start : start + size] = total
            return 0

        lax.fori_loop(0, BLK // 8, per_tile, 0)
    for m in range(blocks):
        spec = to_spectrum_exact(fwd_ref, kern[m])
        kre_ref[m] = spec[:BLK]
        kim_ref[m] = spec[BLK:]
    taps = jnp.concatenate(
        [taps_ref[...], jnp.zeros((BLK - taps_ref.shape[0], width), F32)], axis=0
    )
    spec = to_spectrum_exact(fwd_ref, taps)
    tre_ref[...] = spec[:BLK]
    tim_ref[...] = spec[BLK:]


def kernel_spectra(decay_t, coef_t, taps, fwd, length):
    states, width = decay_t.shape
    blocks = length // BLK
    return pl.pallas_call(
        kgen_body,
        out_shape=(
            jax.ShapeDtypeStruct((blocks, BLK, width), F32),
            jax.ShapeDtypeStruct((blocks, BLK, width), F32),
            jax.ShapeDtypeStruct((BLK, width), F32),
            jax.ShapeDtypeStruct((BLK, width), F32),
        ),
        scratch_shapes=[
            pltpu.VMEM((states, 128), F32),
            pltpu.VMEM((blocks, states, 128), F32),
            pltpu.VMEM((blocks, BLK, width), F32),
        ],
        compiler_params=pltpu.CompilerParams(vmem_limit_bytes=VMEM_LIMIT),
        cost_estimate=cost(11),
        name="kernel_spectra",
    )(decay_t, coef_t, taps, fwd)


def conv_tiles(width, body):
    for start, size in lane_tiles(width):
        lanes = slice(start, start + size)

        def step(ft, _, lanes=lanes):
            body(ft, pl.ds(pl.multiple_of(ft * 8, 8), 8), lanes)
            return 0

        lax.fori_loop(0, BLK // 8, step, 0)


def piece_rows(core, quarter):
    places = []
    for half in range(2):
        for side in (core, 1 - core):
            places.append(pl.ds(pl.multiple_of((2 * half + side) * quarter, quarter), quarter))
    return places


def mixer_fwd_body(
    core_ref, a_ref, b_ref, c_ref, d_ref, w_ref, kre_ref, kim_ref, tre_ref, tim_ref, fwd_ref, inv_ref,
    keep_ref, send_ref,
    x_ref, mixed_ref, q_ref, v_ref, sh_ref, st_ref, sre_ref, sim_ref, ure_ref, uim_ref,
    zre, zim, keys, queries, values, ure, uim,
):
    length, width = q_ref.shape
    blocks = length // BLK
    sign = sign_rows((BLK, width))
    row0 = lax.broadcasted_iota(jnp.int32, (BLK, width), 0) == 0
    places = piece_rows(core_ref[0], a_ref.shape[0])
    wq = w_ref[:, :width]
    wk = w_ref[:, width : 2 * width]
    wv = w_ref[:, 2 * width : 3 * width]
    for piece_ref, place in zip((a_ref, b_ref, c_ref, d_ref), places):
        piece = piece_ref[...]
        x_ref[place] = piece
        queries[place] = dot(piece, wq)
        values[place] = dot(piece, wv)
        keys[place] = dot(piece, wk)
    q_ref[...] = queries[...].astype(BF16)
    v_ref[...] = values[...].astype(BF16)
    tre = tre_ref[...]
    tim = tim_ref[...]
    tre2 = jnp.where(row0, tim, tre)
    tim0 = jnp.where(row0, 0.0, tim)
    last = None
    for p in range(blocks):
        rows = slice(p * BLK, (p + 1) * BLK)
        spec = to_spectrum(fwd_ref, keys[rows])
        re, im = spec[:BLK], spec[BLK:]
        sre_ref[p] = re.astype(BF16)
        sim_ref[p] = im.astype(BF16)
        pr = re * tre - im * tim0
        pi = re * tim0 + im * tre2
        if last is None:
            z = (pr, pi)
        else:
            z = (pr + sign * last[0], pi + sign * last[1])
        last = (pr, pi)
        shifted = from_spectrum(inv_ref, *z)
        sh_ref[rows] = shifted.astype(BF16)
        spec = to_spectrum(fwd_ref, shifted * values[rows])
        ure[p] = spec[:BLK]
        uim[p] = spec[BLK:]
        ure_ref[p] = spec[:BLK].astype(BF16)
        uim_ref[p] = spec[BLK:].astype(BF16)

    def products(ft, fr, lanes):
        sgn = sign[:8, lanes]
        k = [(kre_ref[m, fr, lanes], kim_ref[m, fr, lanes]) for m in range(blocks)]
        k = [(a,) + fix_first(ft, a, b) for a, b in k]
        u = [(ure[m, fr, lanes], uim[m, fr, lanes]) for m in range(blocks)]
        prev = None
        for p in range(blocks):
            yr = yi = None
            for m in range(p + 1):
                ur, ui = u[m]
                kr, kr2, ki0 = k[p - m]
                a = ur * kr - ui * ki0
                b = ur * ki0 + ui * kr2
                yr = a if yr is None else yr + a
                yi = b if yi is None else yi + b
            if prev is None:
                zre[p, fr, lanes] = yr
                zim[p, fr, lanes] = yi
            else:
                zre[p, fr, lanes] = yr + sgn * prev[0]
                zim[p, fr, lanes] = yi + sgn * prev[1]
            prev = (yr, yi)

    conv_tiles(width, products)
    wo = w_ref[:, 3 * width :]
    for half in range(2):
        for p in range(half * blocks // 2, (half + 1) * blocks // 2):
            rows = slice(p * BLK, (p + 1) * BLK)
            state = from_spectrum(inv_ref, zre[p], zim[p])
            st_ref[rows] = state.astype(BF16)
            mixed_ref[rows] = (queries[rows] * state).astype(BF16)
        for out_ref, place in zip((keep_ref, send_ref), places[2 * half : 2 * half + 2]):
            out_ref[half] = dot_nt(mixed_ref[place], wo).astype(BF16)


SCALAR = pl.BlockSpec(memory_space=pltpu.SMEM)
WHOLE = pl.BlockSpec(memory_space=pltpu.VMEM)


def mixer_forward_kernel(core, pieces, w, spectra, fwd, inv):
    quarter, model = pieces[0].shape
    length = 4 * quarter
    width = w.shape[1] // 4
    blocks = length // BLK
    row_f = jax.ShapeDtypeStruct((length, width), BF16)
    spec_f = jax.ShapeDtypeStruct((blocks, BLK, width), BF16)
    piece = jax.ShapeDtypeStruct((2, quarter, model), BF16)
    return pl.pallas_call(
        mixer_fwd_body,
        in_specs=[SCALAR] + [WHOLE] * 11,
        out_shape=(
            piece, piece,
            jax.ShapeDtypeStruct((length, model), BF16),
            jax.ShapeDtypeStruct((length, width), BF16),
            row_f, row_f, row_f, row_f, spec_f, spec_f, spec_f, spec_f,
        ),
        scratch_shapes=[pltpu.VMEM((blocks, BLK, width), F32)] * 2
        + [pltpu.VMEM((length, width), F32)] * 3
        + [pltpu.VMEM((blocks, BLK, width), F32)] * 2,
        compiler_params=pltpu.CompilerParams(vmem_limit_bytes=VMEM_LIMIT),
        cost_estimate=cost(14),
        name="mixer_forward",
    )(core, *pieces, w, *spectra, fwd, inv)


def correlate_tiles(width, blocks, left, other, result):
    left_re, left_im = left
    other_re, other_im = other
    to_re, to_im = result
    sign = sign_rows((8, width))

    def products(ft, fr, lanes):
        sgn = sign[:, lanes]
        k = [(other_re[m, fr, lanes], other_im[m, fr, lanes]) for m in range(blocks)]
        k = [(a,) + fix_first(ft, a, b) for a, b in k]
        g = [(left_re[m, fr, lanes], left_im[m, fr, lanes]) for m in range(blocks)]
        after = None
        for p in reversed(range(blocks)):
            wr = wi = None
            for m in range(p, blocks):
                gr, gi = g[m]
                kr, kr2, ki0 = k[m - p]
                a = gr * kr + gi * ki0
                b = gi * kr2 - gr * ki0
                wr = a if wr is None else wr + a
                wi = b if wi is None else wi + b
            if after is None:
                to_re[p, fr, lanes] = wr
                to_im[p, fr, lanes] = wi
            else:
                to_re[p, fr, lanes] = wr + sgn * after[0]
                to_im[p, fr, lanes] = wi + sgn * after[1]
            after = (wr, wi)

    conv_tiles(width, products)


def mixer_bwd_body(
    core_ref, a_ref, b_ref, c_ref, d_ref, w_ref, q_ref, v_ref, sh_ref, st_ref, sre_ref, sim_ref,
    kre_ref, kim_ref, tre_ref, tim_ref, fwd_ref, inv_ref,
    keep_ref, send_ref, g_ref, gp_ref, taps_ref, gre_ref, gim_ref,
    wre, wim, gre, gim, grad_mixed,
):
    length, width = q_ref.shape
    blocks = length // BLK
    sign = sign_rows((BLK, width))
    row0 = lax.broadcasted_iota(jnp.int32, (BLK, width), 0) == 0
    places = piece_rows(core_ref[0], a_ref.shape[0])
    wo = w_ref[:, 3 * width :]
    for piece_ref, place in zip((a_ref, b_ref, c_ref, d_ref), places):
        piece = piece_ref[...]
        g_ref[place] = piece
        grad_mixed[place] = dot(piece, wo)
    for p in range(blocks):
        rows = slice(p * BLK, (p + 1) * BLK)
        gm = grad_mixed[rows]
        gp_ref[rows, :width] = (gm * st_ref[rows].astype(F32)).astype(BF16)
        spec = to_spectrum(fwd_ref, gm * q_ref[rows].astype(F32))
        gre[p] = spec[:BLK]
        gim[p] = spec[BLK:]
        gre_ref[p] = spec[:BLK].astype(BF16)
        gim_ref[p] = spec[BLK:].astype(BF16)
    correlate_tiles(width, blocks, (gre, gim), (kre_ref, kim_ref), (wre, wim))
    tre = tre_ref[...]
    tim = tim_ref[...]
    tre2 = jnp.where(row0, tim, tre)
    tim0 = jnp.where(row0, 0.0, tim)
    after = None
    next_gs = None
    zero = jnp.zeros((BLK, width), F32)
    corr = [zero, zero, zero, zero]
    for p in reversed(range(blocks)):
        rows = slice(p * BLK, (p + 1) * BLK)
        grad_u = from_spectrum(inv_ref, wre[p], wim[p])
        gp_ref[rows, 2 * width :] = (grad_u * sh_ref[rows].astype(F32)).astype(BF16)
        spec = to_spectrum(fwd_ref, grad_u * v_ref[rows].astype(F32))
        re, im = spec[:BLK], spec[BLK:]
        pr = re * tre + im * tim0
        pi = im * tre2 - re * tim0
        if after is None:
            z = (pr, pi)
        else:
            z = (pr + sign * after[0], pi + sign * after[1])
        after = (pr, pi)
        gp_ref[rows, width : 2 * width] = from_spectrum(inv_ref, *z).astype(BF16)
        sr, si = sre_ref[p].astype(F32), sim_ref[p].astype(F32)
        sr2 = jnp.where(row0, si, sr)
        si0 = jnp.where(row0, 0.0, si)
        corr[0] = corr[0] + (re * sr + im * si0)
        corr[1] = corr[1] + (im * sr2 - re * si0)
        if next_gs is not None:
            nr, ni = next_gs
            corr[2] = corr[2] + (nr * sr + ni * si0)
            corr[3] = corr[3] + (ni * sr2 - nr * si0)
        next_gs = (re, im)
    taps = from_spectrum(inv_ref, corr[0] + sign * corr[2], corr[1] + sign * corr[3])
    taps_ref[...] = taps[: taps_ref.shape[0]]
    wp = w_ref[:, : 3 * width]
    for i, place in enumerate(places):
        (keep_ref, send_ref)[i % 2][i // 2] = dot_nt(gp_ref[place], wp).astype(BF16)


def mixer_backward_kernel(core, pieces, w, saved, spectra, fwd, inv, taps):
    quarter, model = pieces[0].shape
    length = 4 * quarter
    width = w.shape[1] // 4
    blocks = length // BLK
    piece = jax.ShapeDtypeStruct((2, quarter, model), BF16)
    spec_f = jax.ShapeDtypeStruct((blocks, BLK, width), BF16)
    return pl.pallas_call(
        mixer_bwd_body,
        in_specs=[SCALAR] + [WHOLE] * 17,
        out_shape=(
            piece, piece,
            jax.ShapeDtypeStruct((length, model), BF16),
            jax.ShapeDtypeStruct((length, 3 * width), BF16),
            jax.ShapeDtypeStruct((taps, width), F32),
            spec_f, spec_f,
        ),
        scratch_shapes=[pltpu.VMEM((blocks, BLK, width), F32)] * 4
        + [pltpu.VMEM((length, width), F32)],
        compiler_params=pltpu.CompilerParams(vmem_limit_bytes=VMEM_LIMIT),
        cost_estimate=cost(15),
        name="mixer_backward",
    )(core, *pieces, w, *saved, *spectra, fwd, inv)


def ssm_grad_kernel(g_spectrum, u_spectrum, decay_t, coef_t, inv, tile):
    states, width = decay_t.shape
    blocks = g_spectrum[0].shape[0]
    start, size, copies = channel_tiles(width)[tile]
    lanes = slice(start, start + size)
    rows = states // copies
    group = GROUP

    def body(g_re, g_im, u_re, u_im, decay_ref, coef_ref, inv_ref, gd_ref, gc_ref,
             gre, gim, ure, uim, vre, vim, dk_ref, rate, sum_a, sum_b):
        for scratch, ref in ((gre, g_re), (gim, g_im), (ure, u_re), (uim, u_im)):
            scratch[...] = ref[:, :, lanes].astype(F32)
        correlate_tiles(size, blocks, (gre, gim), (ure, uim), (vre, vim))
        rate[:rows] = side_by_side(decay_ref[...], start, size, copies)
        for p in range(blocks):
            part = from_spectrum(inv_ref, vre[p], vim[p])
            dk_ref[p] = part if copies == 1 else jnp.concatenate([part] * copies, axis=1)
        base = lax.broadcasted_iota(jnp.int32, (8, 128), 0).astype(F32)

        def per_group(ng, _):
            here = pl.ds(pl.multiple_of(ng * 8, 8), 8)
            rates = rate[here]
            row_ids = lax.broadcasted_iota(jnp.int32, (8, 128), 0)
            sums_a = jnp.zeros((8, 128), F32)
            sums_b = jnp.zeros((8, 128), F32)
            for first in range(0, 8, group):
                d = [rates[first + i : first + i + 1] for i in range(group)]
                p = [jnp.broadcast_to(jnp.exp(-float(BLK) * x), (8, 128)) for x in d]
                step8 = [jnp.broadcast_to(jnp.exp(-8.0 * x), (8, 128)) for x in d]
                e0 = tuple(jnp.exp(-x * base) for x in d)
                zero = jnp.zeros((8, 128), F32)

                def per_tile(jt, carry, p=p, step8=step8):
                    e, a, b = carry
                    steps = base + (jt * 8).astype(F32)
                    place = pl.ds(pl.multiple_of(jt * 8, 8), 8)
                    dk = [dk_ref[m, place] for m in range(blocks)]
                    ne, na, nb = [], [], []
                    for i in range(group):
                        h = dk[blocks - 1]
                        s = None
                        for m in reversed(range(blocks - 1)):
                            s = h if s is None else s * p[i] + h
                            h = h * p[i] + dk[m]
                        na.append(a[i] + e[i] * h)
                        nb.append(b[i] + e[i] * (steps * h + float(BLK) * (s * p[i])))
                        ne.append(e[i] * step8[i])
                    return tuple(ne), tuple(na), tuple(nb)

                _, a, b = lax.fori_loop(
                    0, BLK // 8, per_tile, (e0, (zero,) * group, (zero,) * group), unroll=UNROLL
                )
                for i in range(group):
                    mine = row_ids == first + i
                    sums_a = jnp.where(mine, jnp.sum(a[i], axis=0, keepdims=True), sums_a)
                    sums_b = jnp.where(mine, jnp.sum(b[i], axis=0, keepdims=True), sums_b)
            sum_a[here] = sums_a
            sum_b[here] = sums_b
            return 0

        lax.fori_loop(0, rows // 8, per_group, 0)
        for i in range(copies):
            here = slice(i * rows, (i + 1) * rows)
            part = slice(i * size, (i + 1) * size)
            a, b = sum_a[:rows, part], sum_b[:rows, part]
            root = jnp.sqrt(2.0 * decay_ref[here, lanes])
            gc_ref[here] = root * a
            gd_ref[here] = coef_ref[here, lanes] * (a / root - root * b)

    out = jax.ShapeDtypeStruct((states, size), F32)
    return pl.pallas_call(
        body,
        out_shape=(out, out),
        scratch_shapes=[pltpu.VMEM((blocks, BLK, size), F32)] * 6
        + [pltpu.VMEM((blocks, BLK, 128), F32)]
        + [pltpu.VMEM((states, 128), F32)] * 3,
        cost_estimate=cost(10),
        compiler_params=pltpu.CompilerParams(vmem_limit_bytes=VMEM_LIMIT),
        name="ssm_grad",
    )(*g_spectrum, *u_spectrum, decay_t, coef_t, inv)


HEAD = 64
QROWS = 256


def dot_tn(a, b):
    return lax.dot_general(a, b, (((0,), (0,)), ((), ())), preferred_element_type=F32)


def allowed_keys(keys, first_query, queries, length):
    key = lax.broadcasted_iota(jnp.int32, (keys, queries), 0)
    query = lax.broadcasted_iota(jnp.int32, (keys, queries), 1) + first_query
    return (key <= query) & (key < length)


def attn_fwd_body(
    core_ref, len_ref, a_ref, b_ref, c_ref, d_ref, w_ref,
    keep_ref, send_ref, x_ref, q_ref, k_ref, v_ref, att_ref, lse_ref,
):
    rows, width = q_ref.shape
    places = piece_rows(core_ref[0], a_ref.shape[0])
    wq = w_ref[:, :width]
    wk = w_ref[:, width : 2 * width]
    wv = w_ref[:, 2 * width : 3 * width]
    for piece_ref, place in zip((a_ref, b_ref, c_ref, d_ref), places):
        piece = piece_ref[...]
        x_ref[place] = piece
        q_ref[place] = dot(piece, wq).astype(BF16)
        k_ref[place] = dot(piece, wk).astype(BF16)
        v_ref[place] = dot(piece, wv).astype(BF16)
    length = len_ref[0]
    lse_ref[...] = jnp.zeros(lse_ref.shape, F32)
    scale = HEAD**-0.5
    for h in range(width // HEAD):
        lanes = slice(h * HEAD, (h + 1) * HEAD)
        q = q_ref[:, lanes] * jnp.asarray(scale, BF16)
        k = k_ref[:, lanes]
        vt = v_ref[:, lanes].T
        for first in range(0, rows, QROWS):
            n = first + QROWS
            s = dot_nt(k[:n], q[first:n])
            s = jnp.where(allowed_keys(n, first, QROWS, length), s, -jnp.inf)
            top = jnp.max(s, axis=0, keepdims=True)
            e = jnp.exp(s - top)
            total = jnp.sum(e, axis=0, keepdims=True)
            probs = (e * (1.0 / total)).astype(BF16)
            att_ref[lanes, first:n] = dot(vt[:, :n], probs).astype(BF16)
            lse_ref[h : h + 1, first:n] = top + jnp.log(total)
    wo = w_ref[:, 3 * width :]
    out = lax.dot_general(
        att_ref[...], wo, (((0,), (1,)), ((), ())), preferred_element_type=F32
    ).astype(BF16)
    quarter = a_ref.shape[0]
    first = core_ref[0] == 0
    for half in range(2):
        low = out[2 * half * quarter : (2 * half + 1) * quarter]
        high = out[(2 * half + 1) * quarter : (2 * half + 2) * quarter]
        keep_ref[half] = jnp.where(first, low, high)
        send_ref[half] = jnp.where(first, high, low)


def attn_forward_kernel(core, length, pieces, w):
    quarter, model = pieces[0].shape
    rows = 4 * quarter
    width = w.shape[1] // 4
    row_b = jax.ShapeDtypeStruct((rows, width), BF16)
    piece = jax.ShapeDtypeStruct((2, quarter, model), BF16)
    return pl.pallas_call(
        attn_fwd_body,
        in_specs=[SCALAR, SCALAR] + [WHOLE] * 5,
        out_shape=(
            piece, piece,
            jax.ShapeDtypeStruct((rows, model), BF16),
            row_b, row_b, row_b,
            jax.ShapeDtypeStruct((width, rows), BF16),
            jax.ShapeDtypeStruct((8, rows), F32),
        ),
        compiler_params=pltpu.CompilerParams(vmem_limit_bytes=VMEM_LIMIT),
        cost_estimate=cost(12),
        name="attn_forward",
    )(core, length, *pieces, w)


def attn_bwd_body(
    core_ref, len_ref, a_ref, b_ref, c_ref, d_ref, w_ref, q_ref, k_ref, v_ref, lse_ref,
    keep_ref, send_ref, g_ref, gp_ref, ga, gqt, acck, accv
):
    rows, width = q_ref.shape
    places = piece_rows(core_ref[0], a_ref.shape[0])
    wo = w_ref[:, 3 * width :]
    for piece_ref, place in zip((a_ref, b_ref, c_ref, d_ref), places):
        piece = piece_ref[...]
        g_ref[place] = piece
        ga[place] = dot(piece, wo).astype(BF16)
    length = len_ref[0]
    scale = HEAD**-0.5
    acck[...] = jnp.zeros(acck.shape, F32)
    accv[...] = jnp.zeros(accv.shape, F32)
    for h in range(width // HEAD):
        lanes = slice(h * HEAD, (h + 1) * HEAD)
        q = q_ref[:, lanes] * jnp.asarray(scale, BF16)
        k = k_ref[:, lanes]
        kt = k.T
        v = v_ref[:, lanes]
        g = ga[:, lanes]
        for first in range(0, rows, QROWS):
            n = first + QROWS
            s = dot_nt(k[:n], q[first:n])
            probs = jnp.where(
                allowed_keys(n, first, QROWS, length), jnp.exp(s - lse_ref[h : h + 1, first:n]), 0.0
            )
            gp = dot_nt(v[:n], g[first:n])
            inner = jnp.sum(probs * gp, axis=0, keepdims=True)
            gs = (probs * (gp - inner)).astype(BF16)
            gqt[lanes, first:n] = dot(kt[:, :n], gs) * scale
            acck[h, :n] += dot(gs, q[first:n])
            accv[h, :n] += dot(probs.astype(BF16), g[first:n])
        gp_ref[:, width + h * HEAD : width + (h + 1) * HEAD] = acck[h].astype(BF16)
        gp_ref[:, 2 * width + h * HEAD : 2 * width + (h + 1) * HEAD] = accv[h].astype(BF16)
    gp_ref[:, :width] = gqt[...].T.astype(BF16)
    wp = w_ref[:, : 3 * width]
    for i, place in enumerate(places):
        (keep_ref, send_ref)[i % 2][i // 2] = dot_nt(gp_ref[place], wp).astype(BF16)


def attn_backward_kernel(core, length, pieces, w, q, k, v, lse):
    quarter, model = pieces[0].shape
    rows, width = q.shape
    piece = jax.ShapeDtypeStruct((2, quarter, model), BF16)
    heads = width // HEAD
    return pl.pallas_call(
        attn_bwd_body,
        in_specs=[SCALAR, SCALAR] + [WHOLE] * 9,
        out_shape=(
            piece, piece,
            jax.ShapeDtypeStruct((rows, model), BF16),
            jax.ShapeDtypeStruct((rows, 3 * width), BF16),
        ),
        scratch_shapes=[
            pltpu.VMEM((rows, width), BF16),
            pltpu.VMEM((width, rows), F32),
            pltpu.VMEM((heads, rows, HEAD), F32),
            pltpu.VMEM((heads, rows, HEAD), F32),
        ],
        compiler_params=pltpu.CompilerParams(vmem_limit_bytes=VMEM_LIMIT),
        cost_estimate=cost(14),
        name="attn_backward",
    )(core, length, *pieces, w, q, k, v, lse)


EPSILON = 1e-05


def kernel_call(body, outs, name, us, scalars=0, scratch=()):
    def call(*args):
        return pl.pallas_call(
            body,
            in_specs=[SCALAR] * scalars + [WHOLE] * (len(args) - scalars),
            out_shape=outs,
            scratch_shapes=list(scratch),
            cost_estimate=cost(us),
            compiler_params=pltpu.CompilerParams(vmem_limit_bytes=VMEM_LIMIT),
            name=name,
        )(*args)

    return call


def shaped(shape, dtype):
    return jax.ShapeDtypeStruct(shape, dtype)


def statistics(h):
    average = jnp.mean(h, axis=1, keepdims=True)
    centred = h - average
    inverse = lax.rsqrt(jnp.mean(centred * centred, axis=1, keepdims=True) + EPSILON)
    return centred * inverse, inverse


def norm_gradient(grad_normed, h, gain):
    unit, inverse = statistics(h)
    scaled = grad_normed * gain
    first_mean = jnp.mean(scaled, axis=1, keepdims=True)
    second_mean = jnp.mean(scaled * unit, axis=1, keepdims=True)
    return inverse * (scaled - first_mean - unit * second_mean)


def first_norm_body(chip_ref, mine_ref, other_ref, gain_ref, h0_ref, n0_ref, h1_ref, n1_ref):
    mine = mine_ref[...].astype(F32)
    other = other_ref[...].astype(F32)
    first = chip_ref[0] == 0
    for h, h_ref, n_ref in (
        (jnp.where(first, mine, other), h0_ref, n0_ref),
        (jnp.where(first, other, mine), h1_ref, n1_ref),
    ):
        h_ref[...] = h
        unit, _ = statistics(h)
        n_ref[...] = (unit * gain_ref[...]).astype(BF16)


def first_norm(chip, mine, other, gain):
    state, normed = shaped(mine.shape, F32), shaped(mine.shape, BF16)
    outs = (state, normed, state, normed)
    return kernel_call(first_norm_body, outs, "first_norm", 2.5, 1)(chip, mine, other, gain)


def both(pair_ref, received_ref):
    return pair_ref[...].astype(F32) + received_ref[...].astype(F32)


def norm_body(h_ref, pair_ref, received_ref, gain_ref, state_ref, normed_ref):
    h = h_ref[...] + both(pair_ref, received_ref)
    state_ref[...] = h
    unit, _ = statistics(h)
    normed_ref[...] = (unit * gain_ref[...]).astype(BF16)


def norm_step(h, pair, received, gain):
    outs = (shaped(h.shape, F32), shaped(h.shape, BF16))
    return kernel_call(norm_body, outs, "norm_step", 1.5)(h, pair, received, gain)


def back_body(g_ref, pair_ref, received_ref, h_ref, gain_ref, grad_ref, low_ref):
    grad = g_ref[...].astype(F32) + norm_gradient(
        both(pair_ref, received_ref), h_ref[...], gain_ref[...]
    )
    grad_ref[...] = grad
    low_ref[...] = grad.astype(BF16)


def back_step(g, pair, received, h, gain):
    outs = (shaped(g.shape, F32), shaped(g.shape, BF16))
    return kernel_call(back_body, outs, "back_step", 2)(g, pair, received, h, gain)


def last_back_body(chip_ref, g0, h0, g1, h1, own_ref, received_ref, gain_ref, out_ref):
    first = chip_ref[0] == 0
    grad_normed = both(own_ref, received_ref)
    h = jnp.where(first, h0[...], h1[...])
    grad = jnp.where(first, g0[...], g1[...])
    out_ref[...] = (grad + norm_gradient(grad_normed, h, gain_ref[...])).astype(BF16)


def last_back(chip, grads, states, own, received, gain):
    outs = shaped(received.shape, BF16)
    return kernel_call(last_back_body, outs, "last_back", 2, 1)(
        chip, grads[0], states[0], grads[1], states[1], own, received, gain
    )


def own_half_body(chip_ref, keep_ref, received_ref, own_ref, send_ref):
    first = chip_ref[0] == 0
    low = keep_ref[0].astype(F32) + received_ref[0].astype(F32)
    high = keep_ref[1].astype(F32) + received_ref[1].astype(F32)
    own_ref[...] = jnp.where(first, low, high).astype(BF16)
    send_ref[...] = jnp.where(first, high, low).astype(BF16)


def own_half(chip, keep, received):
    piece = shaped(keep.shape[1:], BF16)
    return kernel_call(own_half_body, (piece, piece), "own_half", 2, 1)(chip, keep, received)


ROOT = 0.7978845608028654
CUBIC = 0.044715


def gelu(u):
    return 0.5 * u * (1.0 + jnp.tanh(ROOT * (u + CUBIC * u * u * u)))


def gelu_parts(u):
    square = u * u
    t = jnp.tanh(ROOT * (u + CUBIC * u * square))
    half = 0.5 * (1.0 + t)
    slope = half + 0.5 * u * (1.0 - t * t) * (ROOT * (1.0 + 3.0 * CUBIC * square))
    return u * half, slope


PIECE = 256


def unit_pieces(units, *refs):
    for i, ref in enumerate(refs):
        yield slice(i * units, (i + 1) * units), ref[:, :units], ref[:, units : 2 * units]


def ffn_fwd_body(
    h_ref, pair_ref, received_ref, gain_ref, own_ref, mate_ref, state_ref, n_ref, hidden_ref, out_ref
):
    units = mate_ref.shape[1] // 2
    h = h_ref[...] + both(pair_ref, received_ref)
    state_ref[...] = h
    unit, _ = statistics(h)
    n = (unit * gain_ref[...]).astype(BF16)
    n_ref[...] = n
    out = None
    for lanes, up, down in unit_pieces(units, own_ref, mate_ref):
        hidden = dot(n, up)
        hidden_ref[:, lanes] = hidden
        part = dot_nt(gelu(hidden).astype(BF16), down)
        out = part if out is None else out + part
    out_ref[...] = out.astype(BF16)


def ffn_forward(h, pair, received, gain, own, mate):
    piece = shaped(h.shape, BF16)
    hidden = shaped((h.shape[0], mate.shape[1]), F32)
    outs = (shaped(h.shape, F32), piece, hidden, piece)
    return kernel_call(ffn_fwd_body, outs, "ffn_forward", 50)(h, pair, received, gain, own, mate)


def ffn_both_body(
    h_ref, pair_ref, received_ref, gain_ref, g_ref, own_ref, mate_ref,
    state_ref, n_ref, grad_ref, active_ref, out_ref,
):
    units = mate_ref.shape[1] // 2
    h = h_ref[...] + both(pair_ref, received_ref)
    state_ref[...] = h
    unit, _ = statistics(h)
    n = (unit * gain_ref[...]).astype(BF16)
    n_ref[...] = n
    g = g_ref[...]
    out = None
    for lanes, up, down in unit_pieces(units, own_ref, mate_ref):
        active, slope = gelu_parts(dot(n, up))
        active_ref[:, lanes] = active.astype(BF16)
        grad = (dot(g, down) * slope).astype(BF16)
        grad_ref[:, lanes] = grad
        part = dot_nt(grad, up)
        out = part if out is None else out + part
    out_ref[...] = out.astype(BF16)


def ffn_both(h, pair, received, gain, g, own, mate):
    piece = shaped(h.shape, BF16)
    rows = shaped((h.shape[0], mate.shape[1]), BF16)
    outs = (shaped(h.shape, F32), piece, rows, rows, piece)
    return kernel_call(ffn_both_body, outs, "ffn_both", 60)(h, pair, received, gain, g, own, mate)


def ffn_bwd_body(
    g_ref, pair_ref, received_ref, h_ref, gain_ref, hidden_ref, own_ref, mate_ref,
    total_ref, low_ref, grad_ref, active_ref, out_ref,
):
    units = mate_ref.shape[1] // 2
    total = g_ref[...] + norm_gradient(both(pair_ref, received_ref), h_ref[...], gain_ref[...])
    total_ref[...] = total
    g = total.astype(BF16)
    low_ref[...] = g
    out = None
    for lanes, up, down in unit_pieces(units, own_ref, mate_ref):
        active, slope = gelu_parts(hidden_ref[:, lanes])
        active_ref[:, lanes] = active.astype(BF16)
        grad = (dot(g, down) * slope).astype(BF16)
        grad_ref[:, lanes] = grad
        part = dot_nt(grad, up)
        out = part if out is None else out + part
    out_ref[...] = out.astype(BF16)


def ffn_backward(g, pair, received, h, gain, hidden, own, mate):
    piece = shaped(h.shape, BF16)
    rows = shaped(hidden.shape, BF16)
    outs = (shaped(h.shape, F32), piece, rows, rows, piece)
    return kernel_call(ffn_bwd_body, outs, "ffn_backward", 60)(
        g, pair, received, h, gain, hidden, own, mate
    )


def ffn_out_body(chip_ref, a0_ref, a1_ref, own_ref, mate_ref, out_ref, send_ref):
    units = mate_ref.shape[1] // 2
    outs = []
    for a_ref in (a0_ref, a1_ref):
        out = None
        for lanes, _, down in unit_pieces(units, own_ref, mate_ref):
            part = dot_nt(a_ref[:, lanes], down)
            out = part if out is None else out + part
        outs.append(out)
    first = chip_ref[0] == 0
    out_ref[...] = jnp.where(first, outs[0], outs[1]).astype(BF16)
    send_ref[...] = jnp.where(first, outs[1], outs[0]).astype(BF16)


def ffn_out(chip, active0, active1, own, mate):
    piece = shaped((active0.shape[0], own.shape[0]), BF16)
    return kernel_call(ffn_out_body, (piece, piece), "ffn_out", 3, 1)(
        chip, active0, active1, own, mate
    )


def output_body(chip_ref, h0_ref, h1_ref, own_ref, received_ref, out_ref):
    h = jnp.where(chip_ref[0] == 0, h0_ref[...], h1_ref[...])
    out_ref[...] = (h + both(own_ref, received_ref)).astype(BF16)


def output_step(chip, states, own, received):
    outs = shaped(own.shape, BF16)
    return kernel_call(output_body, outs, "output_step", 2, 1)(chip, *states, own, received)


def ffn_grads_body(n0, n1, g0, g1, gh0, gh1, a0, a1, own_ref, *mate_refs):
    count = len(mate_refs) // 2
    units = count * PIECE
    for i in range(count):
        lanes = slice(units + i * PIECE, units + (i + 1) * PIECE)
        mate_refs[i][...] = (
            dot_tn(n0[...], gh0[:, lanes]) + dot_tn(n1[...], gh1[:, lanes])
        ).astype(BF16)
        mate_refs[count + i][...] = (
            dot_tn(g0[...], a0[:, lanes]) + dot_tn(g1[...], a1[:, lanes])
        ).astype(BF16)
    own_ref[:, :units] = (
        dot_tn(n0[...], gh0[:, :units]) + dot_tn(n1[...], gh1[:, :units])
    ).astype(BF16)
    own_ref[:, units:] = (
        dot_tn(g0[...], a0[:, :units]) + dot_tn(g1[...], a1[:, :units])
    ).astype(BF16)


def ffn_grads(n, g, grad_hidden, active):
    model, units = n[0].shape[1], active[0].shape[1]
    outs = (shaped((model, units), BF16),) + (shaped((model, PIECE), BF16),) * (units // PIECE)
    own, *mate = kernel_call(ffn_grads_body, outs, "ffn_grads", 6)(*n, *g, *grad_hidden, *active)
    return own, mate


def attn_grads_body(x_ref, gp_ref, g_ref, att_ref, own_ref, *refs):
    *mate_refs, out_ref = refs
    first = own_ref.shape[1]
    joined = first + gp_ref.shape[1]
    for i, mate_ref in enumerate(mate_refs):
        lanes = slice(i * PIECE, (i + 1) * PIECE)
        out_ref[:, lanes] = (own_ref[:, lanes].astype(F32) + mate_ref[...].astype(F32)).astype(BF16)
    out_ref[:, first:joined] = dot_tn(x_ref[...], gp_ref[...]).astype(BF16)
    out_ref[:, joined:] = lax.dot_general(
        g_ref[...], att_ref[...], (((0,), (1,)), ((), ())), preferred_element_type=F32
    ).astype(BF16)


def attn_grads(x, joined, g, attended_t, own, mate):
    columns = own.shape[1] + joined.shape[1] + attended_t.shape[0]
    outs = shaped((x.shape[1], columns), BF16)
    return kernel_call(attn_grads_body, outs, "attn_grads", 8)(
        x, joined, g, attended_t, own, *mate
    )


def halved(side, count, bit, rows_of, keep_ref, send_ref, lanes=slice(None)):
    block = keep_ref.shape[0] * 2 // count
    place = 0
    for j in range(count):
        if j & bit:
            continue
        low, high = rows_of(j * block, block), rows_of((j | bit) * block, block)
        here = slice(place, place + block)
        keep_ref[here, lanes] = jnp.where(side == 0, low, high).astype(BF16)
        send_ref[here, lanes] = jnp.where(side == 0, high, low).astype(BF16)
        place += block


def halves_of(rows, columns):
    return (shaped((rows // 2, columns), BF16),) * 2


def ffn_cut(side, own, mate, count, bit):
    def body(side_ref, own_ref, *refs):
        *mate_refs, keep_ref, send_ref = refs
        for i, mate_ref in enumerate(mate_refs):
            lanes = slice(i * PIECE, (i + 1) * PIECE)

            def rows_of(first, size, mate_ref=mate_ref, lanes=lanes):
                here = slice(first, first + size)
                return own_ref[here, lanes].astype(F32) + mate_ref[here].astype(F32)

            halved(side_ref[0], count, bit, rows_of, keep_ref, send_ref, lanes)

    return kernel_call(body, halves_of(*own.shape), "ffn_cut", 3, 1)(side, own, *mate)


def mixer_grads(side, x, joined, g, mixed, count, bit):
    model, columns = x.shape[1], joined.shape[1] + mixed.shape[1]

    def body(side_ref, x_ref, gp_ref, g_ref, mixed_ref, keep_ref, send_ref, total):
        total[:, : gp_ref.shape[1]] = dot_tn(x_ref[...], gp_ref[...])
        total[:, gp_ref.shape[1] :] = dot_tn(g_ref[...], mixed_ref[...])
        halved(
            side_ref[0], count, bit, lambda first, size: total[first : first + size], keep_ref, send_ref
        )

    return kernel_call(
        body, halves_of(model, columns), "mixer_grads", 6, 1, [pltpu.VMEM((model, columns), F32)]
    )(side, x, joined, g, mixed)


def scatter_step(side, keep, received, count, bit):
    def body(side_ref, kept_ref, received_ref, keep_ref, send_ref):
        def rows_of(first, size):
            here = slice(first, first + size)
            return kept_ref[here].astype(F32) + received_ref[here].astype(F32)

        halved(side_ref[0], count, bit, rows_of, keep_ref, send_ref)

    return kernel_call(body, halves_of(*keep.shape), "scatter_step", 2, 1)(side, keep, received)


def small_cut(side, taps, tiles, count, bit):
    width = taps.shape[1]
    starts = [0] * len(tiles)
    for i in range(1, len(tiles)):
        starts[i] = starts[i - 1] + tiles[i - 1][0].shape[1]

    def body(side_ref, taps_ref, *refs):
        *tile_refs, keep_ref, send_ref, total = refs
        total[:, :width] = taps_ref[...]
        for i, start in enumerate(starts):
            size = tile_refs[2 * i].shape[1]
            total[:, width + start : width + start + size] = tile_refs[2 * i][...]
            total[:, 2 * width + start : 2 * width + start + size] = tile_refs[2 * i + 1][...]
        halved(
            side_ref[0], count, bit, lambda first, size: total[first : first + size], keep_ref, send_ref
        )

    shape = (taps.shape[0], 3 * width)
    return kernel_call(
        body, halves_of(*shape), "small_cut", 2, 1, [pltpu.VMEM(shape, F32)]
    )(side, taps, *[x for tile in tiles for x in tile])


def summed(parts, lanes):
    total = parts[0][:, lanes].astype(F32)
    for part in parts[1:]:
        total = total + part[:, lanes].astype(F32)
    return total


def finish(parts, ffn_parts, first, ffn_first, weights, up, gain, ffn_gain):
    rows, width = weights[0].shape
    units = up.shape[1]
    count = len(parts)

    def body(wq_ref, wk_ref, wv_ref, up_ref, gain_ref, ffn_gain_ref, *refs):
        part_refs, ffn_refs = refs[:count], refs[count : 2 * count]
        q_ref, k_ref, v_ref, o_ref, up_grad_ref, down_ref, gain_grad_ref = refs[2 * count :]
        weighted = None
        for i, (w_ref, out_ref) in enumerate(((wq_ref, q_ref), (wk_ref, k_ref), (wv_ref, v_ref))):
            grad = summed(part_refs, slice(first + i * width, first + (i + 1) * width))
            out_ref[...] = grad
            grad = grad * w_ref[...].astype(F32)
            weighted = grad if weighted is None else weighted + grad
        o_ref[...] = summed(part_refs, slice(first + 3 * width, first + 4 * width)).T
        gain_grad_ref[:1] = jnp.sum(weighted.T, axis=0, keepdims=True) / gain_ref[...]
        grad = summed(ffn_refs, slice(ffn_first, ffn_first + units))
        up_grad_ref[...] = grad
        down_ref[...] = summed(ffn_refs, slice(ffn_first + units, ffn_first + 2 * units)).T
        weighted = grad * up_ref[...].astype(F32)
        gain_grad_ref[1:] = jnp.sum(weighted.T, axis=0, keepdims=True) / ffn_gain_ref[...]

    square = shaped((rows, width), F32)
    outs = (
        square, square, square, shaped((width, rows), F32),
        shaped((rows, units), F32), shaped((units, rows), F32), shaped((2, rows), F32),
    )
    return kernel_call(body, outs, "finish", 5)(*weights, up, gain, ffn_gain, *parts, *ffn_parts)


TENSOR = "tensor"
DATA = "dp"


def swap(x, bit):
    return lax.ppermute(x, TENSOR, [(i, i ^ bit) for i in range(4)])


def from_mate(x):
    return swap(x, 1)


def from_chip(x):
    return swap(x, 2)


def tie(*values):
    return lax.optimization_barrier(values)


def after(value, *others):
    return lax.optimization_barrier((value,) + others)[0]


def row_major(x):
    return with_layout_constraint(x, Layout(major_to_minor=tuple(range(x.ndim))))


def add_cores(keep, send):
    return (keep.astype(F32) + from_mate(send).astype(F32)).astype(BF16)


class Rows:
    def __init__(self):
        self.count = lax.axis_size(DATA)
        self.index = lax.axis_index(DATA)
        self.depth = self.count.bit_length() - 1
        self.bits = [1 << i for i in reversed(range(self.depth))]

    def swap(self, x, bit):
        return lax.ppermute(x, DATA, [(i, i ^ bit) for i in range(self.count)])

    def gather_send(self, x, step):
        return self.swap(x, self.bits[step])

    def gather_merge(self, x, other, step):
        upper = (self.index & self.bits[step]) != 0
        return jnp.stack([jnp.where(upper, other, x), jnp.where(upper, x, other)], axis=step)

    def gather_step(self, x, step):
        return self.gather_merge(x, self.gather_send(x, step), step)

    def gather(self, x, first=0, last=None):
        for step in range(first, self.depth if last is None else last):
            x = self.gather_step(x, step)
        return x

    def flat(self, x):
        return x.reshape(self.count * x.shape[-2], x.shape[-1])

    def parts(self, x):
        return x.reshape((2,) * self.depth + (x.shape[0] // self.count, x.shape[1]))

    def cut(self, x, step):
        side = ((self.index & self.bits[step]) != 0).astype(jnp.int32)
        keep = lax.dynamic_slice_in_dim(x, side, 1, step)
        send = lax.dynamic_slice_in_dim(x, 1 - side, 1, step)
        return keep, send.astype(BF16)

    def side(self, step):
        return ((self.index & self.bits[step]) != 0).astype(jnp.int32).reshape(1)

    def without(self, x, step):
        shape = [2] * self.depth
        shape[step] = 1
        return x.reshape(tuple(shape) + (x.shape[0] * 2 // self.count, x.shape[1]))

    def scatter(self, x, steps):
        for step in steps:
            keep, send = self.cut(x, step)
            x = keep.astype(F32) + self.swap(send, self.bits[step]).astype(F32)
        return x


def on_device(
    tokens, cotangent, seq_lengths,
    gain_mixer, mixer_query, mixer_key, mixer_value, shift_taps, ssm_decay, ssm_coef, mixer_out,
    gain_ffn1, ffn1_up, ffn1_down,
    gain_attn, attn_query, attn_key, attn_value, attn_out,
    gain_ffn2, ffn2_up, ffn2_down,
):
    place = lax.axis_index(TENSOR)
    chip = place >> 1
    core = (place & 1).astype(jnp.int32).reshape(1)
    chips = chip.astype(jnp.int32).reshape(1)
    rows = Rows()
    fwd, inv = spectral_tables()
    quarter, model = tokens.shape
    length = 4 * quarter
    block, width = mixer_query.shape
    units = ffn1_up.shape[1]
    unit_rows = shift_taps.shape[0]
    states = unit_rows * rows.count

    own_gains = jnp.stack([gain_mixer, gain_ffn1, gain_attn, gain_ffn2], axis=0)
    small = jnp.zeros((16, model), BF16)
    small = small.at[:unit_rows, : 3 * width].set(
        jnp.concatenate([shift_taps, ssm_decay.T, ssm_coef.T], axis=1)
    )
    small = small.at[12:16, :block].set(own_gains)
    mixer_own = jnp.concatenate([mixer_query, mixer_key, mixer_value, mixer_out.T], axis=1)
    ffn1_own = jnp.concatenate([ffn1_up, ffn1_down.T], axis=1)
    attn_own = jnp.concatenate([attn_query, attn_key, attn_value, attn_out.T], axis=1)
    ffn2_own = jnp.concatenate([ffn2_up, ffn2_down.T], axis=1)
    top = rows.depth - 1
    positions = place * quarter + jnp.arange(quarter)
    live = (positions < seq_lengths[0])[:, None]
    masked = jnp.where(live, cotangent, jnp.zeros_like(cotangent))
    small = rows.gather(small, 0, 1)
    mixer_w = rows.gather(mixer_own, 0, 1)
    there = from_chip(tokens)
    first_w = lax.all_gather(
        jnp.concatenate([ffn1_own, attn_own], axis=1), DATA, axis=0, tiled=True
    )
    small = rows.gather(small, 1, top)
    mixer_w = rows.gather(mixer_w, 1, top)
    small = rows.gather(small, top).reshape(rows.count, 16, model)
    small, mixer_w = tie(small, mixer_w)
    mixer_other = rows.gather_send(mixer_w, top)

    gains = small[:, 12:16, :block].transpose(1, 0, 2).reshape(4, 1, model).astype(F32)
    vectors = small[:, :unit_rows, : 3 * width].reshape(states, 3 * width).astype(F32)
    taps_w, decay_t, coef_t = (vectors[:, i * width : (i + 1) * width] for i in range(3))
    h0, n0, h1, n1 = first_norm(chips, tokens, there, gains[0])
    start = [h0, h1]
    grad_other = from_chip(after(masked, n0))
    spectra = kernel_spectra(after(decay_t, n0), coef_t, taps_w, fwd, length)
    pieces = [n0, from_mate(n0), n1, from_mate(n1)]
    mixer_other, grad_other = after((mixer_other, grad_other), spectra[0])
    mixer_w = rows.flat(rows.gather_merge(mixer_w, mixer_other, top))
    keep, send, x1, mixed, *saved = mixer_forward_kernel(
        core, pieces, mixer_w, spectra, fwd, inv
    )

    def core_sums(keep, send):
        other = from_mate(send)
        return [(keep[i].astype(F32) + other[i].astype(F32)).astype(BF16) for i in range(2)]

    def exchanged(keep, send):
        sums = core_sums(keep, send)
        return sums, [from_chip(p) for p in sums]

    pairs, received = exchanged(keep, send)
    first_w = after(first_w, pairs[1])
    ffn1_w, attn_w = first_w[:, : 2 * units], first_w[:, 2 * units :]
    ffn1_mate = from_mate(ffn1_w)
    ffn2_w = lax.all_gather(after(ffn2_own, pairs[1]), DATA, axis=0, tiled=True)
    ffn1_mate = after(ffn1_mate, received[0])
    after_mixer, n2, hidden1, nexts, arrived = [], [], [], [], []
    for half in range(2):
        wait = received[0] if half == 0 else after(received[1], nexts[0])
        h, n, hidden, out = ffn_forward(
            start[half], pairs[half], wait, gains[1], ffn1_w, ffn1_mate
        )
        after_mixer.append(h)
        n2.append(n)
        hidden1.append(hidden)
        nexts.append(out)
        arrived.append(from_chip(out))
    after_ffn1, pieces = [], []
    for half in range(2):
        wait = after(arrived[half], nexts[1]) if half == 0 else after(arrived[1], pieces[0])
        h, n = norm_step(after_mixer[half], nexts[half], wait, gains[2])
        after_ffn1.append(h)
        pieces += [n, from_mate(n)]
    attn_w, pieces[2] = tie(attn_w, pieces[2])
    keep, send, x3, q2, k2, v2, attended_t, log_total = attn_forward_kernel(
        core, seq_lengths, pieces, attn_w
    )
    pairs, received = exchanged(keep, send)
    ffn2_w = after(ffn2_w, pairs[1])

    ffn2_mate = from_mate(ffn2_w)
    grad = [jnp.where(chip == 0, masked, grad_other), jnp.where(chip == 0, grad_other, masked)]
    g4 = list(grad)
    ffn2_mate = after(ffn2_mate, received[0])
    after_attn, n4, gh, act, nexts, arrived = [], [], [], [], [], []
    for half in range(2):
        wait = received[0] if half == 0 else after(received[1], nexts[0])
        h, n, grad_hidden, active, out = ffn_both(
            after_ffn1[half], pairs[half], wait, gains[3], g4[half], ffn2_w, ffn2_mate
        )
        after_attn.append(h)
        n4.append(n)
        gh.append(grad_hidden)
        act.append(active)
        nexts.append(out)
        arrived.append(from_chip(out))
    lows = []
    wait = after(arrived[0], nexts[1])
    grad[0], low = back_step(grad[0], nexts[0], wait, after_attn[0], gains[3])
    lows.append(low)
    gh, act = after((gh, act), low)
    own, mate = ffn_grads(n4, g4, gh, act)
    wait = after(arrived[1], mate[-1])
    grad[1], low = back_step(grad[1], nexts[1], wait, after_attn[1], gains[3])
    lows.append(low)
    pieces = [lows[0], from_mate(after(lows[0], low)), lows[1], from_mate(lows[1])]
    ffn2_mate_g = [from_mate(x) for x in after(tuple(mate), pieces[1], pieces[3])]
    keep, send, g3, grad_joined = attn_backward_kernel(
        core, seq_lengths, pieces, attn_w, q2, k2, v2, log_total
    )
    pairs, received = exchanged(keep, send)
    own, ffn2_mate_g = after((own, ffn2_mate_g), pairs[1])
    second_p = attn_grads(x3, grad_joined, g3, attended_t, own, ffn2_mate_g)
    step = rows.depth - 1
    final_own, final_sent = ffn_out(chips, *after(tuple(act), second_p), ffn2_w, ffn2_mate)
    received = list(after(tuple(received), second_p, final_sent))

    g2, gh, act_b, nexts, arrived = [], [], [], [], []
    for half in range(2):
        wait = received[half]
        grad[half], low, grad_hidden, active, out = ffn_backward(
            grad[half].astype(F32), pairs[half], wait, after_ffn1[half], gains[2], hidden1[half],
            ffn1_w, ffn1_mate,
        )
        g2.append(low)
        gh.append(grad_hidden)
        act_b.append(active)
        nexts.append(out)
        arrived.append(from_chip(out))
    second_g = lax.psum_scatter(after(second_p, nexts[0]), DATA, scatter_dimension=0, tiled=True)
    lows = []
    wait = after(arrived[0], nexts[1])
    grad[0], low = back_step(grad[0], nexts[0], wait, after_mixer[0], gains[1])
    lows.append(low)
    gh, act_b = after((gh, act_b), low)
    own, mate = ffn_grads(n2, g2, gh, act_b)
    wait = after(arrived[1], mate[-1])
    grad[1], low = back_step(grad[1], nexts[1], wait, after_mixer[1], gains[1])
    lows.append(low)
    pieces = [lows[0], from_mate(lows[0]), lows[1], from_mate(lows[1])]
    mate_g = [from_mate(x) for x in after(tuple(mate), pieces[1], arrived[1])]
    mate_g, pieces[1], pieces[3] = tie(mate_g, pieces[1], pieces[3])
    ffn1_keep, ffn1_send = ffn_cut(rows.side(step), own, mate_g, rows.count, rows.bits[step])
    pieces[0], ffn1_send, final_sent = tie(pieces[0], ffn1_send, final_sent)
    final_received = from_chip(final_sent)
    ffn1_received = rows.swap(ffn1_send, rows.bits[step])
    keep, send, g1, grad_joined, grad_taps, *g_spectrum = mixer_backward_kernel(
        core, pieces, mixer_w, saved[:6], spectra, fwd, inv, states
    )
    output = output_step(chips, after_attn, final_own, after(final_received, keep))
    mixer_keep, mixer_send = mixer_grads(
        rows.side(step - 1), x1, grad_joined, g1, mixed, rows.count, rows.bits[step - 1]
    )
    mixer_received = rows.swap(mixer_send, rows.bits[step - 1])
    own, last_sent = own_half(chips, keep, from_mate(after(send, mixer_send)))
    last_received = from_chip(last_sent)
    g_spectrum = after(tuple(g_spectrum), last_sent)
    ssm = [ssm_grad_kernel(g_spectrum, saved[6:], decay_t, coef_t, inv, 0)]

    half, pair = rows.count // 2, rows.count // 4

    def send_on(arrays, step, *ready):
        return [rows.swap(x, rows.bits[step]) for x in arrays]

    ffn1_received = after(ffn1_received, ssm[0][0])
    ffn1_keep, ffn1_send = scatter_step(rows.side(step - 1), ffn1_keep, ffn1_received, half, 1)
    mixer_received = after(mixer_received, ffn1_send)
    mixer_keep, mixer_send = scatter_step(rows.side(step), mixer_keep, mixer_received, half, 1)
    ffn1_received = rows.swap(ffn1_send, rows.bits[step - 1])
    mixer_received = rows.swap(mixer_send, rows.bits[step])
    g_spectrum = after(g_spectrum, mixer_send)
    ssm += [
        ssm_grad_kernel(g_spectrum, saved[6:], decay_t, coef_t, inv, i)
        for i in range(1, len(channel_tiles(width)))
    ]
    small_keep, small_send = small_cut(
        rows.side(step), grad_taps, ssm, rows.count, rows.bits[step]
    )
    small_received = rows.swap(small_send, rows.bits[step])
    ffn1_received, mixer_received, last_received, small_received = tie(
        *after((ffn1_received, mixer_received, last_received, small_received), small_send)
    )
    ffn1_keep, ffn1_send = scatter_step(rows.side(step - 2), ffn1_keep, ffn1_received, pair, 1)
    mixer_received, small_received = after((mixer_received, small_received), ffn1_send)
    mixer_keep, mixer_send = scatter_step(rows.side(step - 2), mixer_keep, mixer_received, pair, 1)
    small_keep, small_send = scatter_step(
        rows.side(step - 1), small_keep, after(small_received, mixer_send), half, 1
    )
    ffn1_send, mixer_send, small_send = tie(ffn1_send, mixer_send, small_send)
    ffn1_received = rows.swap(ffn1_send, rows.bits[step - 2])
    mixer_received = rows.swap(mixer_send, rows.bits[step - 2])
    small_received = rows.swap(small_send, rows.bits[step - 1])
    input_grad = last_back(chips, grad, start, own, after(last_received, small_send), gains[0])
    small_keep, small_send = scatter_step(rows.side(step - 2), small_keep, small_received, pair, 1)
    small_received = rows.swap(small_send, rows.bits[step - 2])
    second_g = [after(second_g, small_send)]

    def column(gain):
        return gain.astype(F32)[None, :]

    aq, ak, av, ao, u2, d2, gains_second = finish(
        second_g, second_g, 2 * units, 0, (attn_query, attn_key, attn_value), ffn2_up,
        column(gain_attn), column(gain_ffn2),
    )
    ffn1_received, mixer_received, small_received = after(
        (ffn1_received, mixer_received, small_received), gains_second
    )
    level, tail = pair // 2, step - 3
    while tail >= 0:
        ffn1_keep, ffn1_send = scatter_step(rows.side(tail), ffn1_keep, ffn1_received, level, 1)
        mixer_keep, mixer_send = scatter_step(rows.side(tail), mixer_keep, mixer_received, level, 1)
        small_keep, small_send = scatter_step(rows.side(tail), small_keep, small_received, level, 1)
        ffn1_received = rows.swap(ffn1_send, rows.bits[tail])
        mixer_received = rows.swap(mixer_send, rows.bits[tail])
        small_received = rows.swap(small_send, rows.bits[tail])
        level, tail = level // 2, tail - 1
    mq, mk, mv, mo, u1, d1, gains_first = finish(
        [mixer_keep, mixer_received], [ffn1_keep, ffn1_received], 0, 0,
        (mixer_query, mixer_key, mixer_value), ffn1_up, column(gain_mixer), column(gain_ffn1),
    )
    small_g = small_keep.astype(F32) + small_received.astype(F32)
    gt, gd, gc = (small_g[:, i * width : (i + 1) * width] for i in range(3))
    first_gains, second_gains = (
        g + swap(g, 1) + (swap(g, 2) + swap(g, 3)) for g in (gains_first, gains_second)
    )
    return (
        output, input_grad,
        first_gains[0], mq, mk, mv, gt, gd.T, gc.T, mo,
        first_gains[1], u1, d1,
        second_gains[0], aq, ak, av, ao,
        second_gains[1], u2, d2,
    )


def solution(mesh):
    rows = P(("dp", "tensor"), None)
    up = P("dp", "tensor")
    down = P("tensor", "dp")
    vector = P("dp")
    mixer = (vector, up, up, up, up, down, down, down)
    ffn = (vector, up, down)
    attn = (vector, up, up, up, down)
    weights = mixer + ffn + attn + ffn
    return jax.shard_map(
        on_device,
        mesh=mesh,
        in_specs=(rows, rows, vector) + weights,
        out_specs=(rows, rows) + weights,
        check_vma=False,
    )
```

```python
import math
import numpy as np
import jax
import jax.numpy as jnp
from jax import lax
from jax.experimental import pallas as pl
from jax.experimental.pallas import tpu as pltpu
from jax.experimental.layout import Layout, with_layout_constraint
from jax.sharding import PartitionSpec as P

F32 = jnp.float32
BF16 = jnp.bfloat16
BLK = 128
GROUP = 8
UNROLL = 2
VMEM_LIMIT = 56 * 1024 * 1024


def cost(us):
    return pl.CostEstimate(
        flops=int(us * 1.1e8), transcendentals=0, bytes_accessed=int(us * 3.5e5)
    )


def dot(a, b):
    return jnp.dot(a, b, preferred_element_type=F32)


def dot_nt(a, b):
    return lax.dot_general(a, b, (((1,), (1,)), ((), ())), preferred_element_type=F32)


def split(x):
    high = x.astype(BF16)
    return high, (x - high.astype(F32)).astype(BF16)


def spectral_tables():
    j = np.arange(BLK)
    f = np.arange(BLK)
    angle = 2.0 * np.pi * np.outer(f, j) / (2 * BLK)
    alternating = (-1.0) ** j
    real = np.cos(angle)
    imag = -np.sin(angle)
    imag[0] = alternating
    forward = np.concatenate([real, imag], axis=0)
    weight = np.full((BLK, 1), 2.0)
    weight[0] = 1.0
    back_real = weight * real / (2 * BLK)
    back_imag = 2.0 * imag / (2 * BLK)
    back_imag[0] = alternating / (2 * BLK)
    inverse = np.concatenate([back_real, back_imag], axis=0).T

    def halves(table):
        high = table.astype(jnp.bfloat16)
        low = (table - high.astype(np.float64)).astype(jnp.bfloat16)
        return high, low

    fh, fl = halves(forward)
    ih, il = halves(inverse)
    fwd = np.concatenate([fh, fh, fl], axis=1)
    inv = np.concatenate([ih, il], axis=0)
    return jnp.asarray(fwd), jnp.asarray(inv)


def to_spectrum_exact(fwd_ref, x):
    high, low = split(x)
    return dot(fwd_ref[:, : 2 * BLK], jnp.concatenate([high, low], axis=0)) + dot(
        fwd_ref[:, 2 * BLK :], high
    )


def to_spectrum(fwd_ref, x):
    return dot(fwd_ref[:, :BLK], x.astype(BF16))


def from_spectrum(inv_ref, re, im):
    return dot(inv_ref[:BLK], jnp.concatenate([re.astype(BF16), im.astype(BF16)], axis=0))


def sign_rows(shape):
    row = lax.broadcasted_iota(jnp.int32, shape, 0)
    return jnp.where(row % 2 == 0, 1.0, -1.0).astype(F32)


def lane_tiles(width):
    return [(s, min(128, width - s)) for s in range(0, width, 128)]


def fix_first(tile, re, im):
    row = lax.broadcasted_iota(jnp.int32, re.shape, 0)
    special = (row == 0) & (tile == 0)
    return jnp.where(special, im, re), jnp.where(special, 0.0, im)


def channel_tiles(width):
    return [(s, min(128, width - s), 128 // min(128, width - s)) for s in range(0, width, 128)]


def side_by_side(x, start, size, copies):
    rows = x.shape[0] // copies
    parts = [x[i * rows : (i + 1) * rows, start : start + size] for i in range(copies)]
    return parts[0] if copies == 1 else jnp.concatenate(parts, axis=1)


def kgen_body(decay_ref, coef_ref, taps_ref, fwd_ref, kre_ref, kim_ref, tre_ref, tim_ref, rate, mixp, kern):
    states, width = decay_ref.shape
    blocks = kre_ref.shape[0]
    decay = decay_ref[...]
    mixing = jnp.sqrt(2.0 * decay) * coef_ref[...]
    for start, size, copies in channel_tiles(width):
        rows = states // copies
        tile_decay = side_by_side(decay, start, size, copies)
        tile_mixing = side_by_side(mixing, start, size, copies)
        rate[:rows] = -tile_decay
        for m in range(blocks):
            mixp[m, :rows] = tile_mixing * jnp.exp(tile_decay * (-float(BLK * m)))

        def per_tile(jt, _, start=start, size=size, copies=copies, rows=rows):
            steps = (lax.broadcasted_iota(jnp.int32, (8, 128), 0) + jt * 8).astype(F32)

            def per_states(ng, acc):
                here = pl.ds(pl.multiple_of(ng * 8, 8), 8)
                rates = rate[here]
                scales = [mixp[m, here] for m in range(blocks)]
                for i in range(8):
                    e = jnp.exp(rates[i : i + 1] * steps)
                    acc = tuple(a + e * s[i : i + 1] for a, s in zip(acc, scales))
                return acc

            acc = lax.fori_loop(
                0, rows // 8, per_states, tuple(jnp.zeros((8, 128), F32) for _ in range(blocks))
            )
            place = pl.ds(pl.multiple_of(jt * 8, 8), 8)
            for m in range(blocks):
                total = acc[m][:, :size]
                for i in range(1, copies):
                    total = total + acc[m][:, i * size : (i + 1) * size]
                kern[m, place, start : start + size] = total
            return 0

        lax.fori_loop(0, BLK // 8, per_tile, 0)
    for m in range(blocks):
        spec = to_spectrum_exact(fwd_ref, kern[m])
        kre_ref[m] = spec[:BLK]
        kim_ref[m] = spec[BLK:]
    taps = jnp.concatenate(
        [taps_ref[...], jnp.zeros((BLK - taps_ref.shape[0], width), F32)], axis=0
    )
    spec = to_spectrum_exact(fwd_ref, taps)
    tre_ref[...] = spec[:BLK]
    tim_ref[...] = spec[BLK:]


def kernel_spectra(decay_t, coef_t, taps, fwd, length):
    states, width = decay_t.shape
    blocks = length // BLK
    return pl.pallas_call(
        kgen_body,
        out_shape=(
            jax.ShapeDtypeStruct((blocks, BLK, width), F32),
            jax.ShapeDtypeStruct((blocks, BLK, width), F32),
            jax.ShapeDtypeStruct((BLK, width), F32),
            jax.ShapeDtypeStruct((BLK, width), F32),
        ),
        scratch_shapes=[
            pltpu.VMEM((states, 128), F32),
            pltpu.VMEM((blocks, states, 128), F32),
            pltpu.VMEM((blocks, BLK, width), F32),
        ],
        compiler_params=pltpu.CompilerParams(vmem_limit_bytes=VMEM_LIMIT),
        cost_estimate=cost(11),
        name="kernel_spectra",
    )(decay_t, coef_t, taps, fwd)


def conv_tiles(width, body):
    for start, size in lane_tiles(width):
        lanes = slice(start, start + size)

        def step(ft, _, lanes=lanes):
            body(ft, pl.ds(pl.multiple_of(ft * 8, 8), 8), lanes)
            return 0

        lax.fori_loop(0, BLK // 8, step, 0)


def piece_rows(core, quarter):
    places = []
    for half in range(2):
        for side in (core, 1 - core):
            places.append(pl.ds(pl.multiple_of((2 * half + side) * quarter, quarter), quarter))
    return places


def mixer_fwd_body(
    core_ref, a_ref, b_ref, c_ref, d_ref, w_ref, kre_ref, kim_ref, tre_ref, tim_ref, fwd_ref, inv_ref,
    keep_ref, send_ref,
    x_ref, mixed_ref, q_ref, v_ref, sh_ref, st_ref, sre_ref, sim_ref, ure_ref, uim_ref,
    zre, zim, keys, queries, values, ure, uim,
):
    length, width = q_ref.shape
    blocks = length // BLK
    sign = sign_rows((BLK, width))
    row0 = lax.broadcasted_iota(jnp.int32, (BLK, width), 0) == 0
    places = piece_rows(core_ref[0], a_ref.shape[0])
    wq = w_ref[:, :width]
    wk = w_ref[:, width : 2 * width]
    wv = w_ref[:, 2 * width : 3 * width]
    for piece_ref, place in zip((a_ref, b_ref, c_ref, d_ref), places):
        piece = piece_ref[...]
        x_ref[place] = piece
        queries[place] = dot(piece, wq)
        values[place] = dot(piece, wv)
        keys[place] = dot(piece, wk)
    q_ref[...] = queries[...].astype(BF16)
    v_ref[...] = values[...].astype(BF16)
    tre = tre_ref[...]
    tim = tim_ref[...]
    tre2 = jnp.where(row0, tim, tre)
    tim0 = jnp.where(row0, 0.0, tim)
    last = None
    for p in range(blocks):
        rows = slice(p * BLK, (p + 1) * BLK)
        spec = to_spectrum(fwd_ref, keys[rows])
        re, im = spec[:BLK], spec[BLK:]
        sre_ref[p] = re.astype(BF16)
        sim_ref[p] = im.astype(BF16)
        pr = re * tre - im * tim0
        pi = re * tim0 + im * tre2
        if last is None:
            z = (pr, pi)
        else:
            z = (pr + sign * last[0], pi + sign * last[1])
        last = (pr, pi)
        shifted = from_spectrum(inv_ref, *z)
        sh_ref[rows] = shifted.astype(BF16)
        spec = to_spectrum(fwd_ref, shifted * values[rows])
        ure[p] = spec[:BLK]
        uim[p] = spec[BLK:]
        ure_ref[p] = spec[:BLK].astype(BF16)
        uim_ref[p] = spec[BLK:].astype(BF16)

    def products(ft, fr, lanes):
        sgn = sign[:8, lanes]
        k = [(kre_ref[m, fr, lanes], kim_ref[m, fr, lanes]) for m in range(blocks)]
        k = [(a,) + fix_first(ft, a, b) for a, b in k]
        u = [(ure[m, fr, lanes], uim[m, fr, lanes]) for m in range(blocks)]
        prev = None
        for p in range(blocks):
            yr = yi = None
            for m in range(p + 1):
                ur, ui = u[m]
                kr, kr2, ki0 = k[p - m]
                a = ur * kr - ui * ki0
                b = ur * ki0 + ui * kr2
                yr = a if yr is None else yr + a
                yi = b if yi is None else yi + b
            if prev is None:
                zre[p, fr, lanes] = yr
                zim[p, fr, lanes] = yi
            else:
                zre[p, fr, lanes] = yr + sgn * prev[0]
                zim[p, fr, lanes] = yi + sgn * prev[1]
            prev = (yr, yi)

    conv_tiles(width, products)
    wo = w_ref[:, 3 * width :]
    for half in range(2):
        for p in range(half * blocks // 2, (half + 1) * blocks // 2):
            rows = slice(p * BLK, (p + 1) * BLK)
            state = from_spectrum(inv_ref, zre[p], zim[p])
            st_ref[rows] = state.astype(BF16)
            mixed_ref[rows] = (queries[rows] * state).astype(BF16)
        for out_ref, place in zip((keep_ref, send_ref), places[2 * half : 2 * half + 2]):
            out_ref[half] = dot_nt(mixed_ref[place], wo).astype(BF16)


SCALAR = pl.BlockSpec(memory_space=pltpu.SMEM)
WHOLE = pl.BlockSpec(memory_space=pltpu.VMEM)


def mixer_forward_kernel(core, pieces, w, spectra, fwd, inv):
    quarter, model = pieces[0].shape
    length = 4 * quarter
    width = w.shape[1] // 4
    blocks = length // BLK
    row_f = jax.ShapeDtypeStruct((length, width), BF16)
    spec_f = jax.ShapeDtypeStruct((blocks, BLK, width), BF16)
    piece = jax.ShapeDtypeStruct((2, quarter, model), BF16)
    return pl.pallas_call(
        mixer_fwd_body,
        in_specs=[SCALAR] + [WHOLE] * 11,
        out_shape=(
            piece, piece,
            jax.ShapeDtypeStruct((length, model), BF16),
            jax.ShapeDtypeStruct((length, width), BF16),
            row_f, row_f, row_f, row_f, spec_f, spec_f, spec_f, spec_f,
        ),
        scratch_shapes=[pltpu.VMEM((blocks, BLK, width), F32)] * 2
        + [pltpu.VMEM((length, width), F32)] * 3
        + [pltpu.VMEM((blocks, BLK, width), F32)] * 2,
        compiler_params=pltpu.CompilerParams(vmem_limit_bytes=VMEM_LIMIT),
        cost_estimate=cost(14),
        name="mixer_forward",
    )(core, *pieces, w, *spectra, fwd, inv)


def correlate_tiles(width, blocks, left, other, result):
    left_re, left_im = left
    other_re, other_im = other
    to_re, to_im = result
    sign = sign_rows((8, width))

    def products(ft, fr, lanes):
        sgn = sign[:, lanes]
        k = [(other_re[m, fr, lanes], other_im[m, fr, lanes]) for m in range(blocks)]
        k = [(a,) + fix_first(ft, a, b) for a, b in k]
        g = [(left_re[m, fr, lanes], left_im[m, fr, lanes]) for m in range(blocks)]
        after = None
        for p in reversed(range(blocks)):
            wr = wi = None
            for m in range(p, blocks):
                gr, gi = g[m]
                kr, kr2, ki0 = k[m - p]
                a = gr * kr + gi * ki0
                b = gi * kr2 - gr * ki0
                wr = a if wr is None else wr + a
                wi = b if wi is None else wi + b
            if after is None:
                to_re[p, fr, lanes] = wr
                to_im[p, fr, lanes] = wi
            else:
                to_re[p, fr, lanes] = wr + sgn * after[0]
                to_im[p, fr, lanes] = wi + sgn * after[1]
            after = (wr, wi)

    conv_tiles(width, products)


def mixer_bwd_body(
    core_ref, a_ref, b_ref, c_ref, d_ref, w_ref, q_ref, v_ref, sh_ref, st_ref, sre_ref, sim_ref,
    kre_ref, kim_ref, tre_ref, tim_ref, fwd_ref, inv_ref,
    keep_ref, send_ref, g_ref, gp_ref, taps_ref, gre_ref, gim_ref,
    wre, wim, gre, gim, grad_mixed,
):
    length, width = q_ref.shape
    blocks = length // BLK
    sign = sign_rows((BLK, width))
    row0 = lax.broadcasted_iota(jnp.int32, (BLK, width), 0) == 0
    places = piece_rows(core_ref[0], a_ref.shape[0])
    wo = w_ref[:, 3 * width :]
    for piece_ref, place in zip((a_ref, b_ref, c_ref, d_ref), places):
        piece = piece_ref[...]
        g_ref[place] = piece
        grad_mixed[place] = dot(piece, wo)
    for p in range(blocks):
        rows = slice(p * BLK, (p + 1) * BLK)
        gm = grad_mixed[rows]
        gp_ref[rows, :width] = (gm * st_ref[rows].astype(F32)).astype(BF16)
        spec = to_spectrum(fwd_ref, gm * q_ref[rows].astype(F32))
        gre[p] = spec[:BLK]
        gim[p] = spec[BLK:]
        gre_ref[p] = spec[:BLK].astype(BF16)
        gim_ref[p] = spec[BLK:].astype(BF16)
    correlate_tiles(width, blocks, (gre, gim), (kre_ref, kim_ref), (wre, wim))
    tre = tre_ref[...]
    tim = tim_ref[...]
    tre2 = jnp.where(row0, tim, tre)
    tim0 = jnp.where(row0, 0.0, tim)
    after = None
    next_gs = None
    zero = jnp.zeros((BLK, width), F32)
    corr = [zero, zero, zero, zero]
    for p in reversed(range(blocks)):
        rows = slice(p * BLK, (p + 1) * BLK)
        grad_u = from_spectrum(inv_ref, wre[p], wim[p])
        gp_ref[rows, 2 * width :] = (grad_u * sh_ref[rows].astype(F32)).astype(BF16)
        spec = to_spectrum(fwd_ref, grad_u * v_ref[rows].astype(F32))
        re, im = spec[:BLK], spec[BLK:]
        pr = re * tre + im * tim0
        pi = im * tre2 - re * tim0
        if after is None:
            z = (pr, pi)
        else:
            z = (pr + sign * after[0], pi + sign * after[1])
        after = (pr, pi)
        gp_ref[rows, width : 2 * width] = from_spectrum(inv_ref, *z).astype(BF16)
        sr, si = sre_ref[p].astype(F32), sim_ref[p].astype(F32)
        sr2 = jnp.where(row0, si, sr)
        si0 = jnp.where(row0, 0.0, si)
        corr[0] = corr[0] + (re * sr + im * si0)
        corr[1] = corr[1] + (im * sr2 - re * si0)
        if next_gs is not None:
            nr, ni = next_gs
            corr[2] = corr[2] + (nr * sr + ni * si0)
            corr[3] = corr[3] + (ni * sr2 - nr * si0)
        next_gs = (re, im)
    taps = from_spectrum(inv_ref, corr[0] + sign * corr[2], corr[1] + sign * corr[3])
    taps_ref[...] = taps[: taps_ref.shape[0]]
    wp = w_ref[:, : 3 * width]
    for i, place in enumerate(places):
        (keep_ref, send_ref)[i % 2][i // 2] = dot_nt(gp_ref[place], wp).astype(BF16)


def mixer_backward_kernel(core, pieces, w, saved, spectra, fwd, inv, taps):
    quarter, model = pieces[0].shape
    length = 4 * quarter
    width = w.shape[1] // 4
    blocks = length // BLK
    piece = jax.ShapeDtypeStruct((2, quarter, model), BF16)
    spec_f = jax.ShapeDtypeStruct((blocks, BLK, width), BF16)
    return pl.pallas_call(
        mixer_bwd_body,
        in_specs=[SCALAR] + [WHOLE] * 17,
        out_shape=(
            piece, piece,
            jax.ShapeDtypeStruct((length, model), BF16),
            jax.ShapeDtypeStruct((length, 3 * width), BF16),
            jax.ShapeDtypeStruct((taps, width), F32),
            spec_f, spec_f,
        ),
        scratch_shapes=[pltpu.VMEM((blocks, BLK, width), F32)] * 4
        + [pltpu.VMEM((length, width), F32)],
        compiler_params=pltpu.CompilerParams(vmem_limit_bytes=VMEM_LIMIT),
        cost_estimate=cost(15),
        name="mixer_backward",
    )(core, *pieces, w, *saved, *spectra, fwd, inv)


def ssm_grad_kernel(g_spectrum, u_spectrum, decay_t, coef_t, inv, tile):
    states, width = decay_t.shape
    blocks = g_spectrum[0].shape[0]
    start, size, copies = channel_tiles(width)[tile]
    lanes = slice(start, start + size)
    rows = states // copies
    group = GROUP

    def body(g_re, g_im, u_re, u_im, decay_ref, coef_ref, inv_ref, gd_ref, gc_ref,
             gre, gim, ure, uim, vre, vim, dk_ref, rate, sum_a, sum_b):
        for scratch, ref in ((gre, g_re), (gim, g_im), (ure, u_re), (uim, u_im)):
            scratch[...] = ref[:, :, lanes].astype(F32)
        correlate_tiles(size, blocks, (gre, gim), (ure, uim), (vre, vim))
        rate[:rows] = side_by_side(decay_ref[...], start, size, copies)
        for p in range(blocks):
            part = from_spectrum(inv_ref, vre[p], vim[p])
            dk_ref[p] = part if copies == 1 else jnp.concatenate([part] * copies, axis=1)
        base = lax.broadcasted_iota(jnp.int32, (8, 128), 0).astype(F32)

        def per_group(ng, _):
            here = pl.ds(pl.multiple_of(ng * 8, 8), 8)
            rates = rate[here]
            row_ids = lax.broadcasted_iota(jnp.int32, (8, 128), 0)
            sums_a = jnp.zeros((8, 128), F32)
            sums_b = jnp.zeros((8, 128), F32)
            for first in range(0, 8, group):
                d = [rates[first + i : first + i + 1] for i in range(group)]
                p = [jnp.broadcast_to(jnp.exp(-float(BLK) * x), (8, 128)) for x in d]
                step8 = [jnp.broadcast_to(jnp.exp(-8.0 * x), (8, 128)) for x in d]
                e0 = tuple(jnp.exp(-x * base) for x in d)
                zero = jnp.zeros((8, 128), F32)

                def per_tile(jt, carry, p=p, step8=step8):
                    e, a, b = carry
                    steps = base + (jt * 8).astype(F32)
                    place = pl.ds(pl.multiple_of(jt * 8, 8), 8)
                    dk = [dk_ref[m, place] for m in range(blocks)]
                    ne, na, nb = [], [], []
                    for i in range(group):
                        h = dk[blocks - 1]
                        s = None
                        for m in reversed(range(blocks - 1)):
                            s = h if s is None else s * p[i] + h
                            h = h * p[i] + dk[m]
                        na.append(a[i] + e[i] * h)
                        nb.append(b[i] + e[i] * (steps * h + float(BLK) * (s * p[i])))
                        ne.append(e[i] * step8[i])
                    return tuple(ne), tuple(na), tuple(nb)

                _, a, b = lax.fori_loop(
                    0, BLK // 8, per_tile, (e0, (zero,) * group, (zero,) * group), unroll=UNROLL
                )
                for i in range(group):
                    mine = row_ids == first + i
                    sums_a = jnp.where(mine, jnp.sum(a[i], axis=0, keepdims=True), sums_a)
                    sums_b = jnp.where(mine, jnp.sum(b[i], axis=0, keepdims=True), sums_b)
            sum_a[here] = sums_a
            sum_b[here] = sums_b
            return 0

        lax.fori_loop(0, rows // 8, per_group, 0)
        for i in range(copies):
            here = slice(i * rows, (i + 1) * rows)
            part = slice(i * size, (i + 1) * size)
            a, b = sum_a[:rows, part], sum_b[:rows, part]
            root = jnp.sqrt(2.0 * decay_ref[here, lanes])
            gc_ref[here] = root * a
            gd_ref[here] = coef_ref[here, lanes] * (a / root - root * b)

    out = jax.ShapeDtypeStruct((states, size), F32)
    return pl.pallas_call(
        body,
        out_shape=(out, out),
        scratch_shapes=[pltpu.VMEM((blocks, BLK, size), F32)] * 6
        + [pltpu.VMEM((blocks, BLK, 128), F32)]
        + [pltpu.VMEM((states, 128), F32)] * 3,
        cost_estimate=cost(10),
        compiler_params=pltpu.CompilerParams(vmem_limit_bytes=VMEM_LIMIT),
        name="ssm_grad",
    )(*g_spectrum, *u_spectrum, decay_t, coef_t, inv)


HEAD = 64
QROWS = 256


def dot_tn(a, b):
    return lax.dot_general(a, b, (((0,), (0,)), ((), ())), preferred_element_type=F32)


def allowed_keys(keys, first_query, queries, length):
    key = lax.broadcasted_iota(jnp.int32, (keys, queries), 0)
    query = lax.broadcasted_iota(jnp.int32, (keys, queries), 1) + first_query
    return (key <= query) & (key < length)


def attn_fwd_body(
    core_ref, len_ref, a_ref, b_ref, c_ref, d_ref, w_ref,
    keep_ref, send_ref, x_ref, q_ref, k_ref, v_ref, att_ref, lse_ref,
):
    rows, width = q_ref.shape
    places = piece_rows(core_ref[0], a_ref.shape[0])
    wq = w_ref[:, :width]
    wk = w_ref[:, width : 2 * width]
    wv = w_ref[:, 2 * width : 3 * width]
    for piece_ref, place in zip((a_ref, b_ref, c_ref, d_ref), places):
        piece = piece_ref[...]
        x_ref[place] = piece
        q_ref[place] = dot(piece, wq).astype(BF16)
        k_ref[place] = dot(piece, wk).astype(BF16)
        v_ref[place] = dot(piece, wv).astype(BF16)
    length = len_ref[0]
    lse_ref[...] = jnp.zeros(lse_ref.shape, F32)
    scale = HEAD**-0.5
    for h in range(width // HEAD):
        lanes = slice(h * HEAD, (h + 1) * HEAD)
        q = q_ref[:, lanes] * jnp.asarray(scale, BF16)
        k = k_ref[:, lanes]
        vt = v_ref[:, lanes].T
        for first in range(0, rows, QROWS):
            n = first + QROWS
            s = dot_nt(k[:n], q[first:n])
            s = jnp.where(allowed_keys(n, first, QROWS, length), s, -jnp.inf)
            top = jnp.max(s, axis=0, keepdims=True)
            e = jnp.exp(s - top)
            total = jnp.sum(e, axis=0, keepdims=True)
            probs = (e * (1.0 / total)).astype(BF16)
            att_ref[lanes, first:n] = dot(vt[:, :n], probs).astype(BF16)
            lse_ref[h : h + 1, first:n] = top + jnp.log(total)
    wo = w_ref[:, 3 * width :]
    out = lax.dot_general(
        att_ref[...], wo, (((0,), (1,)), ((), ())), preferred_element_type=F32
    ).astype(BF16)
    quarter = a_ref.shape[0]
    first = core_ref[0] == 0
    for half in range(2):
        low = out[2 * half * quarter : (2 * half + 1) * quarter]
        high = out[(2 * half + 1) * quarter : (2 * half + 2) * quarter]
        keep_ref[half] = jnp.where(first, low, high)
        send_ref[half] = jnp.where(first, high, low)


def attn_forward_kernel(core, length, pieces, w):
    quarter, model = pieces[0].shape
    rows = 4 * quarter
    width = w.shape[1] // 4
    row_b = jax.ShapeDtypeStruct((rows, width), BF16)
    piece = jax.ShapeDtypeStruct((2, quarter, model), BF16)
    return pl.pallas_call(
        attn_fwd_body,
        in_specs=[SCALAR, SCALAR] + [WHOLE] * 5,
        out_shape=(
            piece, piece,
            jax.ShapeDtypeStruct((rows, model), BF16),
            row_b, row_b, row_b,
            jax.ShapeDtypeStruct((width, rows), BF16),
            jax.ShapeDtypeStruct((8, rows), F32),
        ),
        compiler_params=pltpu.CompilerParams(vmem_limit_bytes=VMEM_LIMIT),
        cost_estimate=cost(12),
        name="attn_forward",
    )(core, length, *pieces, w)


def attn_bwd_body(
    core_ref, len_ref, a_ref, b_ref, c_ref, d_ref, w_ref, q_ref, k_ref, v_ref, lse_ref,
    keep_ref, send_ref, g_ref, gp_ref, ga, gqt, acck, accv
):
    rows, width = q_ref.shape
    places = piece_rows(core_ref[0], a_ref.shape[0])
    wo = w_ref[:, 3 * width :]
    for piece_ref, place in zip((a_ref, b_ref, c_ref, d_ref), places):
        piece = piece_ref[...]
        g_ref[place] = piece
        ga[place] = dot(piece, wo).astype(BF16)
    length = len_ref[0]
    scale = HEAD**-0.5
    acck[...] = jnp.zeros(acck.shape, F32)
    accv[...] = jnp.zeros(accv.shape, F32)
    for h in range(width // HEAD):
        lanes = slice(h * HEAD, (h + 1) * HEAD)
        q = q_ref[:, lanes] * jnp.asarray(scale, BF16)
        k = k_ref[:, lanes]
        kt = k.T
        v = v_ref[:, lanes]
        g = ga[:, lanes]
        for first in range(0, rows, QROWS):
            n = first + QROWS
            s = dot_nt(k[:n], q[first:n])
            probs = jnp.where(
                allowed_keys(n, first, QROWS, length), jnp.exp(s - lse_ref[h : h + 1, first:n]), 0.0
            )
            gp = dot_nt(v[:n], g[first:n])
            inner = jnp.sum(probs * gp, axis=0, keepdims=True)
            gs = (probs * (gp - inner)).astype(BF16)
            gqt[lanes, first:n] = dot(kt[:, :n], gs) * scale
            acck[h, :n] += dot(gs, q[first:n])
            accv[h, :n] += dot(probs.astype(BF16), g[first:n])
        gp_ref[:, width + h * HEAD : width + (h + 1) * HEAD] = acck[h].astype(BF16)
        gp_ref[:, 2 * width + h * HEAD : 2 * width + (h + 1) * HEAD] = accv[h].astype(BF16)
    gp_ref[:, :width] = gqt[...].T.astype(BF16)
    wp = w_ref[:, : 3 * width]
    for i, place in enumerate(places):
        (keep_ref, send_ref)[i % 2][i // 2] = dot_nt(gp_ref[place], wp).astype(BF16)


def attn_backward_kernel(core, length, pieces, w, q, k, v, lse):
    quarter, model = pieces[0].shape
    rows, width = q.shape
    piece = jax.ShapeDtypeStruct((2, quarter, model), BF16)
    heads = width // HEAD
    return pl.pallas_call(
        attn_bwd_body,
        in_specs=[SCALAR, SCALAR] + [WHOLE] * 9,
        out_shape=(
            piece, piece,
            jax.ShapeDtypeStruct((rows, model), BF16),
            jax.ShapeDtypeStruct((rows, 3 * width), BF16),
        ),
        scratch_shapes=[
            pltpu.VMEM((rows, width), BF16),
            pltpu.VMEM((width, rows), F32),
            pltpu.VMEM((heads, rows, HEAD), F32),
            pltpu.VMEM((heads, rows, HEAD), F32),
        ],
        compiler_params=pltpu.CompilerParams(vmem_limit_bytes=VMEM_LIMIT),
        cost_estimate=cost(14),
        name="attn_backward",
    )(core, length, *pieces, w, q, k, v, lse)


EPSILON = 1e-05


def kernel_call(body, outs, name, us, scalars=0, scratch=()):
    def call(*args):
        return pl.pallas_call(
            body,
            in_specs=[SCALAR] * scalars + [WHOLE] * (len(args) - scalars),
            out_shape=outs,
            scratch_shapes=list(scratch),
            cost_estimate=cost(us),
            compiler_params=pltpu.CompilerParams(vmem_limit_bytes=VMEM_LIMIT),
            name=name,
        )(*args)

    return call


def shaped(shape, dtype):
    return jax.ShapeDtypeStruct(shape, dtype)


def statistics(h):
    average = jnp.mean(h, axis=1, keepdims=True)
    centred = h - average
    inverse = lax.rsqrt(jnp.mean(centred * centred, axis=1, keepdims=True) + EPSILON)
    return centred * inverse, inverse


def norm_gradient(grad_normed, h, gain):
    unit, inverse = statistics(h)
    scaled = grad_normed * gain
    first_mean = jnp.mean(scaled, axis=1, keepdims=True)
    second_mean = jnp.mean(scaled * unit, axis=1, keepdims=True)
    gain_grad = jnp.sum(grad_normed * unit, axis=0, keepdims=True)
    return inverse * (scaled - first_mean - unit * second_mean), gain_grad


def first_norm_body(chip_ref, mine_ref, other_ref, gain_ref, h0_ref, n0_ref, h1_ref, n1_ref):
    mine = mine_ref[...].astype(F32)
    other = other_ref[...].astype(F32)
    first = chip_ref[0] == 0
    for h, h_ref, n_ref in (
        (jnp.where(first, mine, other), h0_ref, n0_ref),
        (jnp.where(first, other, mine), h1_ref, n1_ref),
    ):
        h_ref[...] = h
        unit, _ = statistics(h)
        n_ref[...] = (unit * gain_ref[...]).astype(BF16)


def first_norm(chip, mine, other, gain):
    state, normed = shaped(mine.shape, F32), shaped(mine.shape, BF16)
    outs = (state, normed, state, normed)
    return kernel_call(first_norm_body, outs, "first_norm", 2.5, 1)(chip, mine, other, gain)


def both(pair_ref, received_ref):
    return pair_ref[...].astype(F32) + received_ref[...].astype(F32)


def norm_body(h_ref, pair_ref, received_ref, gain_ref, state_ref, normed_ref):
    h = h_ref[...] + both(pair_ref, received_ref)
    state_ref[...] = h
    unit, _ = statistics(h)
    normed_ref[...] = (unit * gain_ref[...]).astype(BF16)


def norm_step(h, pair, received, gain):
    outs = (shaped(h.shape, F32), shaped(h.shape, BF16))
    return kernel_call(norm_body, outs, "norm_step", 1.5)(h, pair, received, gain)


def back_body(g_ref, pair_ref, received_ref, h_ref, gain_ref, grad_ref, low_ref, gain_grad_ref):
    grad, gain_grad_ref[...] = norm_gradient(
        both(pair_ref, received_ref), h_ref[...], gain_ref[...]
    )
    grad = g_ref[...].astype(F32) + grad
    grad_ref[...] = grad
    low_ref[...] = grad.astype(BF16)


def back_step(g, pair, received, h, gain):
    outs = (shaped(g.shape, F32), shaped(g.shape, BF16), shaped(gain.shape, F32))
    return kernel_call(back_body, outs, "back_step", 2)(g, pair, received, h, gain)


def last_back_body(chip_ref, g0, h0, g1, h1, own_ref, received_ref, gain_ref, out_ref):
    first = chip_ref[0] == 0
    grad_normed = both(own_ref, received_ref)
    h = jnp.where(first, h0[...], h1[...])
    grad = jnp.where(first, g0[...], g1[...])
    out_ref[...] = (grad + norm_gradient(grad_normed, h, gain_ref[...])[0]).astype(BF16)


def last_back(chip, grads, states, own, received, gain):
    outs = shaped(received.shape, BF16)
    return kernel_call(last_back_body, outs, "last_back", 2, 1)(
        chip, grads[0], states[0], grads[1], states[1], own, received, gain
    )


def own_half_body(chip_ref, keep_ref, received_ref, own_ref, send_ref):
    first = chip_ref[0] == 0
    low = keep_ref[0].astype(F32) + received_ref[0].astype(F32)
    high = keep_ref[1].astype(F32) + received_ref[1].astype(F32)
    own_ref[...] = jnp.where(first, low, high).astype(BF16)
    send_ref[...] = jnp.where(first, high, low).astype(BF16)


def own_half(chip, keep, received):
    piece = shaped(keep.shape[1:], BF16)
    return kernel_call(own_half_body, (piece, piece), "own_half", 2, 1)(chip, keep, received)


ROOT = 0.7978845608028654
CUBIC = 0.044715


def gelu(u):
    return 0.5 * u * (1.0 + jnp.tanh(ROOT * (u + CUBIC * u * u * u)))


def gelu_parts(u):
    square = u * u
    t = jnp.tanh(ROOT * (u + CUBIC * u * square))
    half = 0.5 * (1.0 + t)
    slope = half + 0.5 * u * (1.0 - t * t) * (ROOT * (1.0 + 3.0 * CUBIC * square))
    return u * half, slope


PIECE = 256


def unit_pieces(units, *refs):
    for i, ref in enumerate(refs):
        yield slice(i * units, (i + 1) * units), ref[:, :units], ref[:, units : 2 * units]


def ffn_fwd_body(
    h_ref, pair_ref, received_ref, gain_ref, own_ref, mate_ref, state_ref, n_ref, hidden_ref, out_ref
):
    units = mate_ref.shape[1] // 2
    h = h_ref[...] + both(pair_ref, received_ref)
    state_ref[...] = h
    unit, _ = statistics(h)
    n = (unit * gain_ref[...]).astype(BF16)
    n_ref[...] = n
    out = None
    for lanes, up, down in unit_pieces(units, own_ref, mate_ref):
        hidden = dot(n, up)
        hidden_ref[:, lanes] = hidden
        part = dot_nt(gelu(hidden).astype(BF16), down)
        out = part if out is None else out + part
    out_ref[...] = out.astype(BF16)


def ffn_forward(h, pair, received, gain, own, mate):
    piece = shaped(h.shape, BF16)
    hidden = shaped((h.shape[0], mate.shape[1]), F32)
    outs = (shaped(h.shape, F32), piece, hidden, piece)
    return kernel_call(ffn_fwd_body, outs, "ffn_forward", 50)(h, pair, received, gain, own, mate)


def ffn_both_body(
    h_ref, pair_ref, received_ref, gain_ref, g_ref, own_ref, mate_ref,
    state_ref, n_ref, grad_ref, active_ref, out_ref,
):
    units = mate_ref.shape[1] // 2
    h = h_ref[...] + both(pair_ref, received_ref)
    state_ref[...] = h
    unit, _ = statistics(h)
    n = (unit * gain_ref[...]).astype(BF16)
    n_ref[...] = n
    g = g_ref[...]
    out = None
    for lanes, up, down in unit_pieces(units, own_ref, mate_ref):
        active, slope = gelu_parts(dot(n, up))
        active_ref[:, lanes] = active.astype(BF16)
        grad = (dot(g, down) * slope).astype(BF16)
        grad_ref[:, lanes] = grad
        part = dot_nt(grad, up)
        out = part if out is None else out + part
    out_ref[...] = out.astype(BF16)


def ffn_both(h, pair, received, gain, g, own, mate):
    piece = shaped(h.shape, BF16)
    rows = shaped((h.shape[0], mate.shape[1]), BF16)
    outs = (shaped(h.shape, F32), piece, rows, rows, piece)
    return kernel_call(ffn_both_body, outs, "ffn_both", 60)(h, pair, received, gain, g, own, mate)


def ffn_bwd_body(
    g_ref, pair_ref, received_ref, h_ref, gain_ref, hidden_ref, own_ref, mate_ref,
    total_ref, low_ref, grad_ref, active_ref, out_ref, gain_grad_ref,
):
    units = mate_ref.shape[1] // 2
    total, gain_grad_ref[...] = norm_gradient(
        both(pair_ref, received_ref), h_ref[...], gain_ref[...]
    )
    total = g_ref[...] + total
    total_ref[...] = total
    g = total.astype(BF16)
    low_ref[...] = g
    out = None
    for lanes, up, down in unit_pieces(units, own_ref, mate_ref):
        active, slope = gelu_parts(hidden_ref[:, lanes])
        active_ref[:, lanes] = active.astype(BF16)
        grad = (dot(g, down) * slope).astype(BF16)
        grad_ref[:, lanes] = grad
        part = dot_nt(grad, up)
        out = part if out is None else out + part
    out_ref[...] = out.astype(BF16)


def ffn_backward(g, pair, received, h, gain, hidden, own, mate):
    piece = shaped(h.shape, BF16)
    rows = shaped(hidden.shape, BF16)
    outs = (shaped(h.shape, F32), piece, rows, rows, piece, shaped(gain.shape, F32))
    return kernel_call(ffn_bwd_body, outs, "ffn_backward", 60)(
        g, pair, received, h, gain, hidden, own, mate
    )


def ffn_out_body(chip_ref, a0_ref, a1_ref, own_ref, mate_ref, out_ref, send_ref):
    units = mate_ref.shape[1] // 2
    outs = []
    for a_ref in (a0_ref, a1_ref):
        out = None
        for lanes, _, down in unit_pieces(units, own_ref, mate_ref):
            part = dot_nt(a_ref[:, lanes], down)
            out = part if out is None else out + part
        outs.append(out)
    first = chip_ref[0] == 0
    out_ref[...] = jnp.where(first, outs[0], outs[1]).astype(BF16)
    send_ref[...] = jnp.where(first, outs[1], outs[0]).astype(BF16)


def ffn_out(chip, active0, active1, own, mate):
    piece = shaped((active0.shape[0], own.shape[0]), BF16)
    return kernel_call(ffn_out_body, (piece, piece), "ffn_out", 3, 1)(
        chip, active0, active1, own, mate
    )


def output_body(chip_ref, h0_ref, h1_ref, own_ref, received_ref, out_ref):
    h = jnp.where(chip_ref[0] == 0, h0_ref[...], h1_ref[...])
    out_ref[...] = (h + both(own_ref, received_ref)).astype(BF16)


def output_step(chip, states, own, received):
    outs = shaped(own.shape, BF16)
    return kernel_call(output_body, outs, "output_step", 2, 1)(chip, *states, own, received)


def ffn_grads_body(n0, n1, g0, g1, gh0, gh1, a0, a1, own_ref, *mate_refs):
    count = len(mate_refs) // 2
    units = count * PIECE
    for i in range(count):
        lanes = slice(units + i * PIECE, units + (i + 1) * PIECE)
        mate_refs[i][...] = (
            dot_tn(n0[...], gh0[:, lanes]) + dot_tn(n1[...], gh1[:, lanes])
        ).astype(BF16)
        mate_refs[count + i][...] = (
            dot_tn(g0[...], a0[:, lanes]) + dot_tn(g1[...], a1[:, lanes])
        ).astype(BF16)
    own_ref[:, :units] = (
        dot_tn(n0[...], gh0[:, :units]) + dot_tn(n1[...], gh1[:, :units])
    ).astype(BF16)
    own_ref[:, units:] = (
        dot_tn(g0[...], a0[:, :units]) + dot_tn(g1[...], a1[:, :units])
    ).astype(BF16)


def ffn_grads(n, g, grad_hidden, active):
    model, units = n[0].shape[1], active[0].shape[1]
    outs = (shaped((model, units), BF16),) + (shaped((model, PIECE), BF16),) * (units // PIECE)
    own, *mate = kernel_call(ffn_grads_body, outs, "ffn_grads", 6)(*n, *g, *grad_hidden, *active)
    return own, mate


def attn_grads_body(x_ref, gp_ref, g_ref, att_ref, own_ref, *refs):
    *mate_refs, out_ref = refs
    first = own_ref.shape[1]
    joined = first + gp_ref.shape[1]
    for i, mate_ref in enumerate(mate_refs):
        lanes = slice(i * PIECE, (i + 1) * PIECE)
        out_ref[:, lanes] = (own_ref[:, lanes].astype(F32) + mate_ref[...].astype(F32)).astype(BF16)
    out_ref[:, first:joined] = dot_tn(x_ref[...], gp_ref[...]).astype(BF16)
    out_ref[:, joined:] = lax.dot_general(
        g_ref[...], att_ref[...], (((0,), (1,)), ((), ())), preferred_element_type=F32
    ).astype(BF16)


def attn_grads(x, joined, g, attended_t, own, mate):
    columns = own.shape[1] + joined.shape[1] + attended_t.shape[0]
    outs = shaped((x.shape[1], columns), BF16)
    return kernel_call(attn_grads_body, outs, "attn_grads", 8)(
        x, joined, g, attended_t, own, *mate
    )


def halved(side, count, bit, rows_of, keep_ref, send_ref, lanes=slice(None)):
    block = keep_ref.shape[0] * 2 // count
    place = 0
    for j in range(count):
        if j & bit:
            continue
        low, high = rows_of(j * block, block), rows_of((j | bit) * block, block)
        here = slice(place, place + block)
        keep_ref[here, lanes] = jnp.where(side == 0, low, high).astype(BF16)
        send_ref[here, lanes] = jnp.where(side == 0, high, low).astype(BF16)
        place += block


def halves_of(rows, columns):
    return (shaped((rows // 2, columns), BF16),) * 2


def ffn_cut(side, own, mate, count, bit):
    def body(side_ref, own_ref, *refs):
        *mate_refs, keep_ref, send_ref = refs
        for i, mate_ref in enumerate(mate_refs):
            lanes = slice(i * PIECE, (i + 1) * PIECE)

            def rows_of(first, size, mate_ref=mate_ref, lanes=lanes):
                here = slice(first, first + size)
                return own_ref[here, lanes].astype(F32) + mate_ref[here].astype(F32)

            halved(side_ref[0], count, bit, rows_of, keep_ref, send_ref, lanes)

    return kernel_call(body, halves_of(*own.shape), "ffn_cut", 3, 1)(side, own, *mate)


def mixer_grads(side, x, joined, g, mixed, w, count, bit):
    model, columns = x.shape[1], joined.shape[1] + mixed.shape[1]
    inputs = joined.shape[1]

    def body(side_ref, x_ref, gp_ref, g_ref, mixed_ref, w_ref, keep_ref, send_ref, gain_ref, total):
        total[:, :inputs] = dot_tn(x_ref[...], gp_ref[...])
        total[:, inputs:] = dot_tn(g_ref[...], mixed_ref[...])
        halved(
            side_ref[0], count, bit, lambda first, size: total[first : first + size], keep_ref, send_ref
        )
        weighted = total[:, :inputs] * w_ref[:, :inputs].astype(F32)
        high, low = split(weighted)
        ones = jnp.ones((8, inputs), BF16)
        gain_ref[...] = (dot_nt(ones, high) + dot_nt(ones, low))[:1]

    outs = halves_of(model, columns) + (shaped((1, model), F32),)
    return kernel_call(body, outs, "mixer_grads", 6, 1, [pltpu.VMEM((model, columns), F32)])(
        side, x, joined, g, mixed, w
    )


def scatter_step(side, keep, received, count, bit):
    def body(side_ref, kept_ref, received_ref, keep_ref, send_ref):
        def rows_of(first, size):
            here = slice(first, first + size)
            return kept_ref[here].astype(F32) + received_ref[here].astype(F32)

        halved(side_ref[0], count, bit, rows_of, keep_ref, send_ref)

    return kernel_call(body, halves_of(*keep.shape), "scatter_step", 2, 1)(side, keep, received)


def gain_places(count, rows, model, gains):
    block = model // count
    lanes = gains * block // rows
    step = math.gcd(block, lanes)
    places = []
    for j in range(count):
        for i in range(gains):
            for first in range(0, block, step):
                flat = i * block + first
                places.append((i, j * block + first, step, j * rows + flat // lanes, flat % lanes))
    return places, lanes


def small_cut(side, taps, tiles, gains, count, bit):
    width = taps.shape[1]
    starts = [0] * len(tiles)
    for i in range(1, len(tiles)):
        starts[i] = starts[i - 1] + tiles[i - 1][0].shape[1]
    places, lanes = gain_places(count, taps.shape[0] // count, gains.shape[1], gains.shape[0])

    def body(side_ref, taps_ref, gains_ref, *refs):
        *tile_refs, keep_ref, send_ref, total = refs
        total[:, :width] = taps_ref[...]
        for i, start in enumerate(starts):
            size = tile_refs[2 * i].shape[1]
            total[:, width + start : width + start + size] = tile_refs[2 * i][...]
            total[:, 2 * width + start : 2 * width + start + size] = tile_refs[2 * i + 1][...]
        for i, first, size, row, lane in places:
            here = slice(3 * width + lane, 3 * width + lane + size)
            total[row : row + 1, here] = gains_ref[i : i + 1, first : first + size]
        halved(
            side_ref[0], count, bit, lambda first, size: total[first : first + size], keep_ref, send_ref
        )

    shape = (taps.shape[0], 3 * width + lanes)
    return kernel_call(
        body, halves_of(*shape), "small_cut", 2, 1, [pltpu.VMEM(shape, F32)]
    )(side, taps, gains, *[x for tile in tiles for x in tile])


def finish_small(keep, received, gains, width):
    rows = keep.shape[0]
    count, block = gains.shape
    places, _ = gain_places(1, rows, block, count)

    def body(keep_ref, received_ref, gains_ref, taps_ref, decay_ref, coef_ref, gain_grad_ref):
        total = keep_ref[...].astype(F32) + received_ref[...].astype(F32)
        taps_ref[...] = total[:, :width]
        decay_ref[...] = total[:, width : 2 * width]
        coef_ref[...] = total[:, 2 * width : 3 * width]
        for i, first, size, row, lane in places:
            lanes = slice(3 * width + lane, 3 * width + lane + size)
            part = total[row : row + 1, lanes]
            if i == 0:
                part = part / gains_ref[:1, first : first + size]
            gain_grad_ref[i : i + 1, first : first + size] = part

    outs = (
        shaped((rows, width), F32), shaped((rows, width), F32), shaped((rows, width), F32),
        shaped((count, block), F32),
    )
    return kernel_call(body, outs, "finish_small", 2)(keep, received, gains)


def summed(parts, lanes):
    total = parts[0][:, lanes].astype(F32)
    for part in parts[1:]:
        total = total + part[:, lanes].astype(F32)
    return total


def finish(parts, ffn_parts, first, ffn_first, width, units):
    rows = parts[0].shape[0]
    count = len(parts)

    def body(*refs):
        part_refs, ffn_refs = refs[:count], refs[count : 2 * count]
        q_ref, k_ref, v_ref, o_ref, up_ref, down_ref = refs[2 * count :]
        for i, out_ref in enumerate((q_ref, k_ref, v_ref)):
            out_ref[...] = summed(part_refs, slice(first + i * width, first + (i + 1) * width))
        o_ref[...] = summed(part_refs, slice(first + 3 * width, first + 4 * width)).T
        up_ref[...] = summed(ffn_refs, slice(ffn_first, ffn_first + units))
        down_ref[...] = summed(ffn_refs, slice(ffn_first + units, ffn_first + 2 * units))

    square = shaped((rows, width), F32)
    outs = (
        square, square, square, shaped((width, rows), F32),
        shaped((rows, units), F32), shaped((rows, units), F32),
    )
    return kernel_call(body, outs, "finish", 5)(*parts, *ffn_parts)


TENSOR = "tensor"
DATA = "dp"


def swap(x, bit):
    return lax.ppermute(x, TENSOR, [(i, i ^ bit) for i in range(4)])


def from_mate(x):
    return swap(x, 1)


def from_chip(x):
    return swap(x, 2)


def tie(*values):
    return lax.optimization_barrier(values)


def after(value, *others):
    return lax.optimization_barrier((value,) + others)[0]


def row_major(x):
    return with_layout_constraint(x, Layout(major_to_minor=tuple(range(x.ndim))))


def add_cores(keep, send):
    return (keep.astype(F32) + from_mate(send).astype(F32)).astype(BF16)


class Rows:
    def __init__(self):
        self.count = lax.axis_size(DATA)
        self.index = lax.axis_index(DATA)
        self.depth = self.count.bit_length() - 1
        self.bits = [1 << i for i in reversed(range(self.depth))]

    def swap(self, x, bit):
        return lax.ppermute(x, DATA, [(i, i ^ bit) for i in range(self.count)])

    def gather_send(self, x, step):
        return self.swap(x, self.bits[step])

    def gather_merge(self, x, other, step):
        upper = (self.index & self.bits[step]) != 0
        return jnp.stack([jnp.where(upper, other, x), jnp.where(upper, x, other)], axis=step)

    def gather_step(self, x, step):
        return self.gather_merge(x, self.gather_send(x, step), step)

    def gather(self, x, first=0, last=None):
        for step in range(first, self.depth if last is None else last):
            x = self.gather_step(x, step)
        return x

    def flat(self, x):
        return x.reshape(self.count * x.shape[-2], x.shape[-1])

    def parts(self, x):
        return x.reshape((2,) * self.depth + (x.shape[0] // self.count, x.shape[1]))

    def cut(self, x, step):
        side = ((self.index & self.bits[step]) != 0).astype(jnp.int32)
        keep = lax.dynamic_slice_in_dim(x, side, 1, step)
        send = lax.dynamic_slice_in_dim(x, 1 - side, 1, step)
        return keep, send.astype(BF16)

    def side(self, step):
        return ((self.index & self.bits[step]) != 0).astype(jnp.int32).reshape(1)

    def without(self, x, step):
        shape = [2] * self.depth
        shape[step] = 1
        return x.reshape(tuple(shape) + (x.shape[0] * 2 // self.count, x.shape[1]))

    def scatter(self, x, steps):
        for step in steps:
            keep, send = self.cut(x, step)
            x = keep.astype(F32) + self.swap(send, self.bits[step]).astype(F32)
        return x


def on_device(
    tokens, cotangent, seq_lengths,
    gain_mixer, mixer_query, mixer_key, mixer_value, shift_taps, ssm_decay, ssm_coef, mixer_out,
    gain_ffn1, ffn1_up, ffn1_down,
    gain_attn, attn_query, attn_key, attn_value, attn_out,
    gain_ffn2, ffn2_up, ffn2_down,
):
    place = lax.axis_index(TENSOR)
    chip = place >> 1
    core = (place & 1).astype(jnp.int32).reshape(1)
    chips = chip.astype(jnp.int32).reshape(1)
    rows = Rows()
    fwd, inv = spectral_tables()
    quarter, model = tokens.shape
    length = 4 * quarter
    block, width = mixer_query.shape
    units = ffn1_up.shape[1]
    unit_rows = shift_taps.shape[0]
    states = unit_rows * rows.count

    own_gains = jnp.stack([gain_mixer, gain_ffn1, gain_attn, gain_ffn2], axis=0)
    small = jnp.zeros((16, model), BF16)
    small = small.at[:unit_rows, : 3 * width].set(
        jnp.concatenate([shift_taps, ssm_decay.T, ssm_coef.T], axis=1)
    )
    small = small.at[12:16, :block].set(own_gains)
    mixer_own = jnp.concatenate([mixer_query, mixer_key, mixer_value, mixer_out.T], axis=1)
    ffn1_own = jnp.concatenate([ffn1_up, ffn1_down.T], axis=1)
    attn_own = jnp.concatenate([attn_query, attn_key, attn_value, attn_out.T], axis=1)
    ffn2_own = jnp.concatenate([ffn2_up, ffn2_down.T], axis=1)
    top = rows.depth - 1
    positions = place * quarter + jnp.arange(quarter)
    live = (positions < seq_lengths[0])[:, None]
    masked = jnp.where(live, cotangent, jnp.zeros_like(cotangent))
    small = rows.gather(small, 0, 1)
    mixer_w = rows.gather(mixer_own, 0, 1)
    there = from_chip(tokens)
    first_w = lax.all_gather(
        jnp.concatenate([ffn1_own, attn_own], axis=1), DATA, axis=0, tiled=True
    )
    small = rows.gather(small, 1, top)
    mixer_w = rows.gather(mixer_w, 1, top)
    small = rows.gather(small, top).reshape(rows.count, 16, model)
    small, mixer_w = tie(small, mixer_w)
    mixer_other = rows.gather_send(mixer_w, top)

    gains = small[:, 12:16, :block].transpose(1, 0, 2).reshape(4, 1, model).astype(F32)
    vectors = small[:, :unit_rows, : 3 * width].reshape(states, 3 * width).astype(F32)
    taps_w, decay_t, coef_t = (vectors[:, i * width : (i + 1) * width] for i in range(3))
    h0, n0, h1, n1 = first_norm(chips, tokens, there, gains[0])
    start = [h0, h1]
    grad_other = from_chip(after(masked, n0))
    spectra = kernel_spectra(after(decay_t, n0), coef_t, taps_w, fwd, length)
    pieces = [n0, from_mate(n0), n1, from_mate(n1)]
    mixer_other, grad_other = after((mixer_other, grad_other), spectra[0])
    mixer_w = rows.flat(rows.gather_merge(mixer_w, mixer_other, top))
    keep, send, x1, mixed, *saved = mixer_forward_kernel(
        core, pieces, mixer_w, spectra, fwd, inv
    )

    def core_sums(keep, send):
        other = from_mate(send)
        return [(keep[i].astype(F32) + other[i].astype(F32)).astype(BF16) for i in range(2)]

    def exchanged(keep, send):
        sums = core_sums(keep, send)
        return sums, [from_chip(p) for p in sums]

    pairs, received = exchanged(keep, send)
    first_w = after(first_w, pairs[1])
    ffn1_w, attn_w = first_w[:, : 2 * units], first_w[:, 2 * units :]
    received[0], attn_w = tie(received[0], attn_w)
    ffn1_mate = from_mate(ffn1_w)
    ffn2_w = lax.all_gather(after(ffn2_own, pairs[1]), DATA, axis=0, tiled=True)
    ffn1_mate = after(ffn1_mate, received[0])
    after_mixer, n2, hidden1, nexts, arrived = [], [], [], [], []
    for half in range(2):
        wait = received[0] if half == 0 else after(received[1], nexts[0])
        h, n, hidden, out = ffn_forward(
            start[half], pairs[half], wait, gains[1], ffn1_w, ffn1_mate
        )
        after_mixer.append(h)
        n2.append(n)
        hidden1.append(hidden)
        nexts.append(out)
        arrived.append(from_chip(out))
    after_ffn1, pieces = [], []
    for half in range(2):
        wait = after(arrived[half], nexts[1]) if half == 0 else after(arrived[1], pieces[0])
        h, n = norm_step(after_mixer[half], nexts[half], wait, gains[2])
        after_ffn1.append(h)
        pieces += [n, from_mate(n)]
    keep, send, x3, q2, k2, v2, attended_t, log_total = attn_forward_kernel(
        core, seq_lengths, pieces, attn_w
    )
    pairs, received = exchanged(keep, send)
    ffn2_w = after(ffn2_w, pairs[1])

    ffn2_mate = from_mate(ffn2_w)
    grad = [jnp.where(chip == 0, masked, grad_other), jnp.where(chip == 0, grad_other, masked)]
    g4 = list(grad)
    ffn2_mate = after(ffn2_mate, received[0])
    after_attn, n4, gh, act, nexts, arrived = [], [], [], [], [], []
    for half in range(2):
        wait = received[0] if half == 0 else after(received[1], nexts[0])
        h, n, grad_hidden, active, out = ffn_both(
            after_ffn1[half], pairs[half], wait, gains[3], g4[half], ffn2_w, ffn2_mate
        )
        after_attn.append(h)
        n4.append(n)
        gh.append(grad_hidden)
        act.append(active)
        nexts.append(out)
        arrived.append(from_chip(out))
    lows, ffn2_gain = [], []
    wait = after(arrived[0], nexts[1])
    grad[0], low, part = back_step(grad[0], nexts[0], wait, after_attn[0], gains[3])
    ffn2_gain.append(part)
    lows.append(low)
    gh, act = after((gh, act), low)
    own, mate = ffn_grads(n4, g4, gh, act)
    wait = after(arrived[1], mate[-1])
    grad[1], low, part = back_step(grad[1], nexts[1], wait, after_attn[1], gains[3])
    ffn2_gain.append(part)
    lows.append(low)
    pieces = [lows[0], from_mate(after(lows[0], low)), lows[1], from_mate(lows[1])]
    ffn2_mate_g = [from_mate(x) for x in after(tuple(mate), pieces[1], pieces[3])]
    keep, send, g3, grad_joined = attn_backward_kernel(
        core, seq_lengths, pieces, attn_w, q2, k2, v2, log_total
    )
    pairs, received = exchanged(keep, send)
    own, ffn2_mate_g = after((own, ffn2_mate_g), pairs[1])
    second_p = attn_grads(x3, grad_joined, g3, attended_t, own, ffn2_mate_g)
    step = rows.depth - 1
    final_own, final_sent = ffn_out(chips, *after(tuple(act), second_p), ffn2_w, ffn2_mate)
    received = list(after(tuple(received), second_p, final_sent))

    g2, gh, act_b, nexts, arrived, attn_gain = [], [], [], [], [], []
    for half in range(2):
        wait = received[half]
        grad[half], low, grad_hidden, active, out, part = ffn_backward(
            grad[half].astype(F32), pairs[half], wait, after_ffn1[half], gains[2], hidden1[half],
            ffn1_w, ffn1_mate,
        )
        g2.append(low)
        attn_gain.append(part)
        gh.append(grad_hidden)
        act_b.append(active)
        nexts.append(out)
        arrived.append(from_chip(out))
    second_g = lax.psum_scatter(after(second_p, nexts[0]), DATA, scatter_dimension=0, tiled=True)
    lows, ffn1_gain = [], []
    wait = after(arrived[0], nexts[1])
    grad[0], low, part = back_step(grad[0], nexts[0], wait, after_mixer[0], gains[1])
    ffn1_gain.append(part)
    lows.append(low)
    gh, act_b = after((gh, act_b), low)
    own, mate = ffn_grads(n2, g2, gh, act_b)
    wait = after(arrived[1], mate[-1])
    grad[1], low, part = back_step(grad[1], nexts[1], wait, after_mixer[1], gains[1])
    ffn1_gain.append(part)
    lows.append(low)
    pieces = [lows[0], from_mate(lows[0]), lows[1], from_mate(lows[1])]
    mate_g = [from_mate(x) for x in after(tuple(mate), pieces[1], arrived[1])]
    mate_g, pieces[1], pieces[3] = tie(mate_g, pieces[1], pieces[3])
    ffn1_keep, ffn1_send = ffn_cut(rows.side(step), own, mate_g, rows.count, rows.bits[step])
    pieces[0], ffn1_send, final_sent = tie(pieces[0], ffn1_send, final_sent)
    final_received = from_chip(final_sent)
    ffn1_received = rows.swap(ffn1_send, rows.bits[step])
    keep, send, g1, grad_joined, grad_taps, *g_spectrum = mixer_backward_kernel(
        core, pieces, mixer_w, saved[:6], spectra, fwd, inv, states
    )
    mixer_keep, mixer_send, mixer_gain = mixer_grads(
        rows.side(step - 1), x1, grad_joined, g1, mixed, mixer_w, rows.count, rows.bits[step - 1]
    )
    gain_rows = jnp.concatenate(
        [mixer_gain] + [0.5 * (p[0] + p[1]) for p in (ffn1_gain, attn_gain, ffn2_gain)], axis=0
    )
    gain_rows = gain_rows + from_mate(gain_rows)
    gain_rows = gain_rows + from_chip(gain_rows)
    mixer_received = rows.swap(mixer_send, rows.bits[step - 1])
    own, last_sent = own_half(chips, keep, from_mate(after(send, mixer_send)))
    last_received = from_chip(last_sent)
    g_spectrum = after(tuple(g_spectrum), last_sent)
    ssm = [ssm_grad_kernel(g_spectrum, saved[6:], decay_t, coef_t, inv, 0)]

    half, pair = rows.count // 2, rows.count // 4

    def send_on(arrays, step, *ready):
        return [rows.swap(x, rows.bits[step]) for x in arrays]

    ffn1_received = after(ffn1_received, ssm[0][0])
    ffn1_keep, ffn1_send = scatter_step(rows.side(step - 1), ffn1_keep, ffn1_received, half, 1)
    mixer_received = after(mixer_received, ffn1_send)
    mixer_keep, mixer_send = scatter_step(rows.side(step), mixer_keep, mixer_received, half, 1)
    ffn1_received = rows.swap(ffn1_send, rows.bits[step - 1])
    mixer_received = rows.swap(mixer_send, rows.bits[step])
    g_spectrum = after(g_spectrum, mixer_send)
    ssm += [
        ssm_grad_kernel(g_spectrum, saved[6:], decay_t, coef_t, inv, i)
        for i in range(1, len(channel_tiles(width)))
    ]
    small_keep, small_send = small_cut(
        rows.side(step), grad_taps, ssm, gain_rows, rows.count, rows.bits[step]
    )
    small_received = rows.swap(small_send, rows.bits[step])
    small_received = after(small_received, small_send)
    small_keep, small_send = scatter_step(rows.side(step - 1), small_keep, small_received, half, 1)
    small_received = rows.swap(small_send, rows.bits[step - 1])
    ffn1_received, mixer_received, last_received = tie(
        *after((ffn1_received, mixer_received, last_received), small_send)
    )
    ffn1_keep, ffn1_send = scatter_step(rows.side(step - 2), ffn1_keep, ffn1_received, pair, 1)
    mixer_received = after(mixer_received, ffn1_send)
    mixer_keep, mixer_send = scatter_step(rows.side(step - 2), mixer_keep, mixer_received, pair, 1)
    last_received, final_received = after((last_received, final_received), mixer_send)
    input_grad = last_back(chips, grad, start, own, last_received, gains[0])
    output = output_step(chips, after_attn, final_own, final_received)
    small_received = after(small_received, input_grad, output)
    small_keep, small_send = scatter_step(rows.side(step - 2), small_keep, small_received, pair, 1)

    ffn1_received = rows.swap(ffn1_send, rows.bits[step - 2])
    mixer_received = rows.swap(mixer_send, rows.bits[step - 2])
    small_received = rows.swap(small_send, rows.bits[step - 2])
    second_g = [after(second_g, small_send)]

    aq, ak, av, ao, u2, d2 = finish(second_g, second_g, 2 * units, 0, width, units)
    ffn1_received, mixer_received, small_received = after(
        (ffn1_received, mixer_received, small_received), aq, input_grad, output
    )
    level, tail = pair // 2, step - 3
    while tail >= 0:
        ffn1_keep, ffn1_send = scatter_step(rows.side(tail), ffn1_keep, ffn1_received, level, 1)
        mixer_keep, mixer_send = scatter_step(rows.side(tail), mixer_keep, mixer_received, level, 1)
        small_keep, small_send = scatter_step(rows.side(tail), small_keep, small_received, level, 1)
        ffn1_received = rows.swap(ffn1_send, rows.bits[tail])
        mixer_received = rows.swap(mixer_send, rows.bits[tail])
        small_received = rows.swap(small_send, rows.bits[tail])
        level, tail = level // 2, tail - 1
    mq, mk, mv, mo, u1, d1 = finish(
        [mixer_keep, mixer_received], [ffn1_keep, ffn1_received], 0, 0, width, units
    )
    gt, gd, gc, gain_grads = finish_small(
        small_keep, after(small_received, mq), own_gains.astype(F32), width
    )
    return (
        output, input_grad,
        gain_grads[0], mq, mk, mv, gt, gd.T, gc.T, mo,
        gain_grads[1], u1, d1.T,
        gain_grads[2], aq, ak, av, ao,
        gain_grads[3], u2, d2.T,
    )


def solution(mesh):
    rows = P(("dp", "tensor"), None)
    up = P("dp", "tensor")
    down = P("tensor", "dp")
    vector = P("dp")
    mixer = (vector, up, up, up, up, down, down, down)
    ffn = (vector, up, down)
    attn = (vector, up, up, up, down)
    weights = mixer + ffn + attn + ffn
    return jax.shard_map(
        on_device,
        mesh=mesh,
        in_specs=(rows, rows, vector) + weights,
        out_specs=(rows, rows) + weights,
        check_vma=False,
    )
```

```python
import math
import numpy as np
import jax
import jax.numpy as jnp
from jax import lax
from jax.experimental import pallas as pl
from jax.experimental.pallas import tpu as pltpu
from jax.experimental.layout import Layout, with_layout_constraint
from jax.sharding import PartitionSpec as P

F32 = jnp.float32
BF16 = jnp.bfloat16
BLK = 128
GROUP = 8
UNROLL = 2
VMEM_LIMIT = 56 * 1024 * 1024


def cost(us):
    return pl.CostEstimate(
        flops=int(us * 1.1e8), transcendentals=0, bytes_accessed=int(us * 3.5e5)
    )


def dot(a, b):
    return jnp.dot(a, b, preferred_element_type=F32)


def dot_nt(a, b):
    return lax.dot_general(a, b, (((1,), (1,)), ((), ())), preferred_element_type=F32)


def split(x):
    high = x.astype(BF16)
    return high, (x - high.astype(F32)).astype(BF16)


def spectral_tables():
    j = np.arange(BLK)
    f = np.arange(BLK)
    angle = 2.0 * np.pi * np.outer(f, j) / (2 * BLK)
    alternating = (-1.0) ** j
    real = np.cos(angle)
    imag = -np.sin(angle)
    imag[0] = alternating
    forward = np.concatenate([real, imag], axis=0)
    weight = np.full((BLK, 1), 2.0)
    weight[0] = 1.0
    back_real = weight * real / (2 * BLK)
    back_imag = 2.0 * imag / (2 * BLK)
    back_imag[0] = alternating / (2 * BLK)
    inverse = np.concatenate([back_real, back_imag], axis=0).T

    def halves(table):
        high = table.astype(jnp.bfloat16)
        low = (table - high.astype(np.float64)).astype(jnp.bfloat16)
        return high, low

    fh, fl = halves(forward)
    ih, il = halves(inverse)
    fwd = np.concatenate([fh, fh, fl], axis=1)
    inv = np.concatenate([ih, il], axis=0)
    return jnp.asarray(fwd), jnp.asarray(inv)


def to_spectrum_exact(fwd_ref, x):
    high, low = split(x)
    return dot(fwd_ref[:, : 2 * BLK], jnp.concatenate([high, low], axis=0)) + dot(
        fwd_ref[:, 2 * BLK :], high
    )


def to_spectrum(fwd_ref, x):
    return dot(fwd_ref[:, :BLK], x.astype(BF16))


def from_spectrum(inv_ref, re, im):
    return dot(inv_ref[:BLK], jnp.concatenate([re.astype(BF16), im.astype(BF16)], axis=0))


def sign_rows(shape):
    row = lax.broadcasted_iota(jnp.int32, shape, 0)
    return jnp.where(row % 2 == 0, 1.0, -1.0).astype(F32)


def lane_tiles(width):
    return [(s, min(128, width - s)) for s in range(0, width, 128)]


def fix_first(tile, re, im):
    row = lax.broadcasted_iota(jnp.int32, re.shape, 0)
    special = (row == 0) & (tile == 0)
    return jnp.where(special, im, re), jnp.where(special, 0.0, im)


def channel_tiles(width):
    return [(s, min(128, width - s), 128 // min(128, width - s)) for s in range(0, width, 128)]


def side_by_side(x, start, size, copies):
    rows = x.shape[0] // copies
    parts = [x[i * rows : (i + 1) * rows, start : start + size] for i in range(copies)]
    return parts[0] if copies == 1 else jnp.concatenate(parts, axis=1)


def kgen_body(decay_ref, coef_ref, taps_ref, fwd_ref, kre_ref, kim_ref, tre_ref, tim_ref, rate, mixp, kern):
    states, width = decay_ref.shape
    blocks = kre_ref.shape[0]
    decay = decay_ref[...]
    mixing = jnp.sqrt(2.0 * decay) * coef_ref[...]
    for start, size, copies in channel_tiles(width):
        rows = states // copies
        tile_decay = side_by_side(decay, start, size, copies)
        tile_mixing = side_by_side(mixing, start, size, copies)
        rate[:rows] = -tile_decay
        for m in range(blocks):
            mixp[m, :rows] = tile_mixing * jnp.exp(tile_decay * (-float(BLK * m)))

        def per_tile(jt, _, start=start, size=size, copies=copies, rows=rows):
            steps = (lax.broadcasted_iota(jnp.int32, (8, 128), 0) + jt * 8).astype(F32)

            def per_states(ng, acc):
                here = pl.ds(pl.multiple_of(ng * 8, 8), 8)
                rates = rate[here]
                scales = [mixp[m, here] for m in range(blocks)]
                for i in range(8):
                    e = jnp.exp(rates[i : i + 1] * steps)
                    acc = tuple(a + e * s[i : i + 1] for a, s in zip(acc, scales))
                return acc

            acc = lax.fori_loop(
                0, rows // 8, per_states, tuple(jnp.zeros((8, 128), F32) for _ in range(blocks))
            )
            place = pl.ds(pl.multiple_of(jt * 8, 8), 8)
            for m in range(blocks):
                total = acc[m][:, :size]
                for i in range(1, copies):
                    total = total + acc[m][:, i * size : (i + 1) * size]
                kern[m, place, start : start + size] = total
            return 0

        lax.fori_loop(0, BLK // 8, per_tile, 0)
    for m in range(blocks):
        spec = to_spectrum_exact(fwd_ref, kern[m])
        kre_ref[m] = spec[:BLK]
        kim_ref[m] = spec[BLK:]
    taps = jnp.concatenate(
        [taps_ref[...], jnp.zeros((BLK - taps_ref.shape[0], width), F32)], axis=0
    )
    spec = to_spectrum_exact(fwd_ref, taps)
    tre_ref[...] = spec[:BLK]
    tim_ref[...] = spec[BLK:]


def kernel_spectra(decay_t, coef_t, taps, fwd, length):
    states, width = decay_t.shape
    blocks = length // BLK
    return pl.pallas_call(
        kgen_body,
        out_shape=(
            jax.ShapeDtypeStruct((blocks, BLK, width), F32),
            jax.ShapeDtypeStruct((blocks, BLK, width), F32),
            jax.ShapeDtypeStruct((BLK, width), F32),
            jax.ShapeDtypeStruct((BLK, width), F32),
        ),
        scratch_shapes=[
            pltpu.VMEM((states, 128), F32),
            pltpu.VMEM((blocks, states, 128), F32),
            pltpu.VMEM((blocks, BLK, width), F32),
        ],
        compiler_params=pltpu.CompilerParams(vmem_limit_bytes=VMEM_LIMIT),
        cost_estimate=cost(11),
        name="kernel_spectra",
    )(decay_t, coef_t, taps, fwd)


def conv_tiles(width, body):
    for start, size in lane_tiles(width):
        lanes = slice(start, start + size)

        def step(ft, _, lanes=lanes):
            body(ft, pl.ds(pl.multiple_of(ft * 8, 8), 8), lanes)
            return 0

        lax.fori_loop(0, BLK // 8, step, 0)


def piece_rows(core, quarter):
    places = []
    for half in range(2):
        for side in (core, 1 - core):
            places.append(pl.ds(pl.multiple_of((2 * half + side) * quarter, quarter), quarter))
    return places


def mixer_fwd_body(
    core_ref, a_ref, b_ref, c_ref, d_ref, w_ref, kre_ref, kim_ref, tre_ref, tim_ref, fwd_ref, inv_ref,
    keep_ref, send_ref,
    x_ref, mixed_ref, q_ref, v_ref, sh_ref, st_ref, sre_ref, sim_ref, ure_ref, uim_ref,
    zre, zim, keys, queries, values, ure, uim,
):
    length, width = q_ref.shape
    blocks = length // BLK
    sign = sign_rows((BLK, width))
    row0 = lax.broadcasted_iota(jnp.int32, (BLK, width), 0) == 0
    places = piece_rows(core_ref[0], a_ref.shape[0])
    wq = w_ref[:, :width]
    wk = w_ref[:, width : 2 * width]
    wv = w_ref[:, 2 * width : 3 * width]
    for piece_ref, place in zip((a_ref, b_ref, c_ref, d_ref), places):
        piece = piece_ref[...]
        x_ref[place] = piece
        queries[place] = dot(piece, wq)
        values[place] = dot(piece, wv)
        keys[place] = dot(piece, wk)
    q_ref[...] = queries[...].astype(BF16)
    v_ref[...] = values[...].astype(BF16)
    tre = tre_ref[...]
    tim = tim_ref[...]
    tre2 = jnp.where(row0, tim, tre)
    tim0 = jnp.where(row0, 0.0, tim)
    last = None
    for p in range(blocks):
        rows = slice(p * BLK, (p + 1) * BLK)
        spec = to_spectrum(fwd_ref, keys[rows])
        re, im = spec[:BLK], spec[BLK:]
        sre_ref[p] = re.astype(BF16)
        sim_ref[p] = im.astype(BF16)
        pr = re * tre - im * tim0
        pi = re * tim0 + im * tre2
        if last is None:
            z = (pr, pi)
        else:
            z = (pr + sign * last[0], pi + sign * last[1])
        last = (pr, pi)
        shifted = from_spectrum(inv_ref, *z)
        sh_ref[rows] = shifted.astype(BF16)
        spec = to_spectrum(fwd_ref, shifted * values[rows])
        ure[p] = spec[:BLK]
        uim[p] = spec[BLK:]
        ure_ref[p] = spec[:BLK].astype(BF16)
        uim_ref[p] = spec[BLK:].astype(BF16)

    def products(ft, fr, lanes):
        sgn = sign[:8, lanes]
        k = [(kre_ref[m, fr, lanes], kim_ref[m, fr, lanes]) for m in range(blocks)]
        k = [(a,) + fix_first(ft, a, b) for a, b in k]
        u = [(ure[m, fr, lanes], uim[m, fr, lanes]) for m in range(blocks)]
        prev = None
        for p in range(blocks):
            yr = yi = None
            for m in range(p + 1):
                ur, ui = u[m]
                kr, kr2, ki0 = k[p - m]
                a = ur * kr - ui * ki0
                b = ur * ki0 + ui * kr2
                yr = a if yr is None else yr + a
                yi = b if yi is None else yi + b
            if prev is None:
                zre[p, fr, lanes] = yr
                zim[p, fr, lanes] = yi
            else:
                zre[p, fr, lanes] = yr + sgn * prev[0]
                zim[p, fr, lanes] = yi + sgn * prev[1]
            prev = (yr, yi)

    conv_tiles(width, products)
    wo = w_ref[:, 3 * width :]
    for half in range(2):
        for p in range(half * blocks // 2, (half + 1) * blocks // 2):
            rows = slice(p * BLK, (p + 1) * BLK)
            state = from_spectrum(inv_ref, zre[p], zim[p])
            st_ref[rows] = state.astype(BF16)
            mixed_ref[rows] = (queries[rows] * state).astype(BF16)
        for out_ref, place in zip((keep_ref, send_ref), places[2 * half : 2 * half + 2]):
            out_ref[half] = dot_nt(mixed_ref[place], wo).astype(BF16)


SCALAR = pl.BlockSpec(memory_space=pltpu.SMEM)
WHOLE = pl.BlockSpec(memory_space=pltpu.VMEM)


def mixer_forward_kernel(core, pieces, w, spectra, fwd, inv):
    quarter, model = pieces[0].shape
    length = 4 * quarter
    width = w.shape[1] // 4
    blocks = length // BLK
    row_f = jax.ShapeDtypeStruct((length, width), BF16)
    spec_f = jax.ShapeDtypeStruct((blocks, BLK, width), BF16)
    piece = jax.ShapeDtypeStruct((2, quarter, model), BF16)
    return pl.pallas_call(
        mixer_fwd_body,
        in_specs=[SCALAR] + [WHOLE] * 11,
        out_shape=(
            piece, piece,
            jax.ShapeDtypeStruct((length, model), BF16),
            jax.ShapeDtypeStruct((length, width), BF16),
            row_f, row_f, row_f, row_f, spec_f, spec_f, spec_f, spec_f,
        ),
        scratch_shapes=[pltpu.VMEM((blocks, BLK, width), F32)] * 2
        + [pltpu.VMEM((length, width), F32)] * 3
        + [pltpu.VMEM((blocks, BLK, width), F32)] * 2,
        compiler_params=pltpu.CompilerParams(vmem_limit_bytes=VMEM_LIMIT),
        cost_estimate=cost(14),
        name="mixer_forward",
    )(core, *pieces, w, *spectra, fwd, inv)


def correlate_tiles(width, blocks, left, other, result):
    left_re, left_im = left
    other_re, other_im = other
    to_re, to_im = result
    sign = sign_rows((8, width))

    def products(ft, fr, lanes):
        sgn = sign[:, lanes]
        k = [(other_re[m, fr, lanes], other_im[m, fr, lanes]) for m in range(blocks)]
        k = [(a,) + fix_first(ft, a, b) for a, b in k]
        g = [(left_re[m, fr, lanes], left_im[m, fr, lanes]) for m in range(blocks)]
        after = None
        for p in reversed(range(blocks)):
            wr = wi = None
            for m in range(p, blocks):
                gr, gi = g[m]
                kr, kr2, ki0 = k[m - p]
                a = gr * kr + gi * ki0
                b = gi * kr2 - gr * ki0
                wr = a if wr is None else wr + a
                wi = b if wi is None else wi + b
            if after is None:
                to_re[p, fr, lanes] = wr
                to_im[p, fr, lanes] = wi
            else:
                to_re[p, fr, lanes] = wr + sgn * after[0]
                to_im[p, fr, lanes] = wi + sgn * after[1]
            after = (wr, wi)

    conv_tiles(width, products)


def mixer_bwd_body(
    core_ref, a_ref, b_ref, c_ref, d_ref, w_ref, q_ref, v_ref, sh_ref, st_ref, sre_ref, sim_ref,
    kre_ref, kim_ref, tre_ref, tim_ref, fwd_ref, inv_ref,
    keep_ref, send_ref, g_ref, gp_ref, taps_ref, gre_ref, gim_ref,
    wre, wim, gre, gim, grad_mixed,
):
    length, width = q_ref.shape
    blocks = length // BLK
    sign = sign_rows((BLK, width))
    row0 = lax.broadcasted_iota(jnp.int32, (BLK, width), 0) == 0
    places = piece_rows(core_ref[0], a_ref.shape[0])
    wo = w_ref[:, 3 * width :]
    for piece_ref, place in zip((a_ref, b_ref, c_ref, d_ref), places):
        piece = piece_ref[...]
        g_ref[place] = piece
        grad_mixed[place] = dot(piece, wo)
    for p in range(blocks):
        rows = slice(p * BLK, (p + 1) * BLK)
        gm = grad_mixed[rows]
        gp_ref[rows, :width] = (gm * st_ref[rows].astype(F32)).astype(BF16)
        spec = to_spectrum(fwd_ref, gm * q_ref[rows].astype(F32))
        gre[p] = spec[:BLK]
        gim[p] = spec[BLK:]
        gre_ref[p] = spec[:BLK].astype(BF16)
        gim_ref[p] = spec[BLK:].astype(BF16)
    correlate_tiles(width, blocks, (gre, gim), (kre_ref, kim_ref), (wre, wim))
    tre = tre_ref[...]
    tim = tim_ref[...]
    tre2 = jnp.where(row0, tim, tre)
    tim0 = jnp.where(row0, 0.0, tim)
    after = None
    next_gs = None
    zero = jnp.zeros((BLK, width), F32)
    corr = [zero, zero, zero, zero]
    for p in reversed(range(blocks)):
        rows = slice(p * BLK, (p + 1) * BLK)
        grad_u = from_spectrum(inv_ref, wre[p], wim[p])
        gp_ref[rows, 2 * width :] = (grad_u * sh_ref[rows].astype(F32)).astype(BF16)
        spec = to_spectrum(fwd_ref, grad_u * v_ref[rows].astype(F32))
        re, im = spec[:BLK], spec[BLK:]
        pr = re * tre + im * tim0
        pi = im * tre2 - re * tim0
        if after is None:
            z = (pr, pi)
        else:
            z = (pr + sign * after[0], pi + sign * after[1])
        after = (pr, pi)
        gp_ref[rows, width : 2 * width] = from_spectrum(inv_ref, *z).astype(BF16)
        sr, si = sre_ref[p].astype(F32), sim_ref[p].astype(F32)
        sr2 = jnp.where(row0, si, sr)
        si0 = jnp.where(row0, 0.0, si)
        corr[0] = corr[0] + (re * sr + im * si0)
        corr[1] = corr[1] + (im * sr2 - re * si0)
        if next_gs is not None:
            nr, ni = next_gs
            corr[2] = corr[2] + (nr * sr + ni * si0)
            corr[3] = corr[3] + (ni * sr2 - nr * si0)
        next_gs = (re, im)
    taps = from_spectrum(inv_ref, corr[0] + sign * corr[2], corr[1] + sign * corr[3])
    taps_ref[...] = taps[: taps_ref.shape[0]]
    wp = w_ref[:, : 3 * width]
    for i, place in enumerate(places):
        (keep_ref, send_ref)[i % 2][i // 2] = dot_nt(gp_ref[place], wp).astype(BF16)


def mixer_backward_kernel(core, pieces, w, saved, spectra, fwd, inv, taps):
    quarter, model = pieces[0].shape
    length = 4 * quarter
    width = w.shape[1] // 4
    blocks = length // BLK
    piece = jax.ShapeDtypeStruct((2, quarter, model), BF16)
    spec_f = jax.ShapeDtypeStruct((blocks, BLK, width), BF16)
    return pl.pallas_call(
        mixer_bwd_body,
        in_specs=[SCALAR] + [WHOLE] * 17,
        out_shape=(
            piece, piece,
            jax.ShapeDtypeStruct((length, model), BF16),
            jax.ShapeDtypeStruct((length, 3 * width), BF16),
            jax.ShapeDtypeStruct((taps, width), F32),
            spec_f, spec_f,
        ),
        scratch_shapes=[pltpu.VMEM((blocks, BLK, width), F32)] * 4
        + [pltpu.VMEM((length, width), F32)],
        compiler_params=pltpu.CompilerParams(vmem_limit_bytes=VMEM_LIMIT),
        cost_estimate=cost(15),
        name="mixer_backward",
    )(core, *pieces, w, *saved, *spectra, fwd, inv)


def ssm_grad_kernel(g_spectrum, u_spectrum, decay_t, coef_t, inv, tile):
    states, width = decay_t.shape
    blocks = g_spectrum[0].shape[0]
    start, size, copies = channel_tiles(width)[tile]
    lanes = slice(start, start + size)
    rows = states // copies
    group = GROUP

    def body(g_re, g_im, u_re, u_im, decay_ref, coef_ref, inv_ref, gd_ref, gc_ref,
             gre, gim, ure, uim, vre, vim, dk_ref, rate, sum_a, sum_b):
        for scratch, ref in ((gre, g_re), (gim, g_im), (ure, u_re), (uim, u_im)):
            scratch[...] = ref[:, :, lanes].astype(F32)
        correlate_tiles(size, blocks, (gre, gim), (ure, uim), (vre, vim))
        rate[:rows] = side_by_side(decay_ref[...], start, size, copies)
        for p in range(blocks):
            part = from_spectrum(inv_ref, vre[p], vim[p])
            dk_ref[p] = part if copies == 1 else jnp.concatenate([part] * copies, axis=1)
        base = lax.broadcasted_iota(jnp.int32, (8, 128), 0).astype(F32)

        def per_group(ng, _):
            here = pl.ds(pl.multiple_of(ng * 8, 8), 8)
            rates = rate[here]
            row_ids = lax.broadcasted_iota(jnp.int32, (8, 128), 0)
            sums_a = jnp.zeros((8, 128), F32)
            sums_b = jnp.zeros((8, 128), F32)
            for first in range(0, 8, group):
                d = [rates[first + i : first + i + 1] for i in range(group)]
                p = [jnp.broadcast_to(jnp.exp(-float(BLK) * x), (8, 128)) for x in d]
                step8 = [jnp.broadcast_to(jnp.exp(-8.0 * x), (8, 128)) for x in d]
                e0 = tuple(jnp.exp(-x * base) for x in d)
                zero = jnp.zeros((8, 128), F32)

                def per_tile(jt, carry, p=p, step8=step8):
                    e, a, b = carry
                    steps = base + (jt * 8).astype(F32)
                    place = pl.ds(pl.multiple_of(jt * 8, 8), 8)
                    dk = [dk_ref[m, place] for m in range(blocks)]
                    ne, na, nb = [], [], []
                    for i in range(group):
                        h = dk[blocks - 1]
                        s = None
                        for m in reversed(range(blocks - 1)):
                            s = h if s is None else s * p[i] + h
                            h = h * p[i] + dk[m]
                        na.append(a[i] + e[i] * h)
                        nb.append(b[i] + e[i] * (steps * h + float(BLK) * (s * p[i])))
                        ne.append(e[i] * step8[i])
                    return tuple(ne), tuple(na), tuple(nb)

                _, a, b = lax.fori_loop(
                    0, BLK // 8, per_tile, (e0, (zero,) * group, (zero,) * group), unroll=UNROLL
                )
                for i in range(group):
                    mine = row_ids == first + i
                    sums_a = jnp.where(mine, jnp.sum(a[i], axis=0, keepdims=True), sums_a)
                    sums_b = jnp.where(mine, jnp.sum(b[i], axis=0, keepdims=True), sums_b)
            sum_a[here] = sums_a
            sum_b[here] = sums_b
            return 0

        lax.fori_loop(0, rows // 8, per_group, 0)
        for i in range(copies):
            here = slice(i * rows, (i + 1) * rows)
            part = slice(i * size, (i + 1) * size)
            a, b = sum_a[:rows, part], sum_b[:rows, part]
            root = jnp.sqrt(2.0 * decay_ref[here, lanes])
            gc_ref[here] = root * a
            gd_ref[here] = coef_ref[here, lanes] * (a / root - root * b)

    out = jax.ShapeDtypeStruct((states, size), F32)
    return pl.pallas_call(
        body,
        out_shape=(out, out),
        scratch_shapes=[pltpu.VMEM((blocks, BLK, size), F32)] * 6
        + [pltpu.VMEM((blocks, BLK, 128), F32)]
        + [pltpu.VMEM((states, 128), F32)] * 3,
        cost_estimate=cost(10),
        compiler_params=pltpu.CompilerParams(vmem_limit_bytes=VMEM_LIMIT),
        name="ssm_grad",
    )(*g_spectrum, *u_spectrum, decay_t, coef_t, inv)


HEAD = 64
QROWS = 256


def dot_tn(a, b):
    return lax.dot_general(a, b, (((0,), (0,)), ((), ())), preferred_element_type=F32)


def allowed_keys(keys, first_query, queries, length):
    key = lax.broadcasted_iota(jnp.int32, (keys, queries), 0)
    query = lax.broadcasted_iota(jnp.int32, (keys, queries), 1) + first_query
    return (key <= query) & (key < length)


def attn_fwd_body(
    core_ref, len_ref, a_ref, b_ref, c_ref, d_ref, w_ref,
    keep_ref, send_ref, x_ref, q_ref, k_ref, v_ref, att_ref, lse_ref,
):
    rows, width = q_ref.shape
    places = piece_rows(core_ref[0], a_ref.shape[0])
    wq = w_ref[:, :width]
    wk = w_ref[:, width : 2 * width]
    wv = w_ref[:, 2 * width : 3 * width]
    for piece_ref, place in zip((a_ref, b_ref, c_ref, d_ref), places):
        piece = piece_ref[...]
        x_ref[place] = piece
        q_ref[place] = dot(piece, wq).astype(BF16)
        k_ref[place] = dot(piece, wk).astype(BF16)
        v_ref[place] = dot(piece, wv).astype(BF16)
    length = len_ref[0]
    lse_ref[...] = jnp.zeros(lse_ref.shape, F32)
    scale = HEAD**-0.5
    for h in range(width // HEAD):
        lanes = slice(h * HEAD, (h + 1) * HEAD)
        q = q_ref[:, lanes] * jnp.asarray(scale, BF16)
        k = k_ref[:, lanes]
        vt = v_ref[:, lanes].T
        for first in range(0, rows, QROWS):
            n = first + QROWS
            s = dot_nt(k[:n], q[first:n])
            s = jnp.where(allowed_keys(n, first, QROWS, length), s, -jnp.inf)
            top = jnp.max(s, axis=0, keepdims=True)
            e = jnp.exp(s - top)
            total = jnp.sum(e, axis=0, keepdims=True)
            probs = (e * (1.0 / total)).astype(BF16)
            att_ref[lanes, first:n] = dot(vt[:, :n], probs).astype(BF16)
            lse_ref[h : h + 1, first:n] = top + jnp.log(total)
    wo = w_ref[:, 3 * width :]
    out = lax.dot_general(
        att_ref[...], wo, (((0,), (1,)), ((), ())), preferred_element_type=F32
    ).astype(BF16)
    quarter = a_ref.shape[0]
    first = core_ref[0] == 0
    for half in range(2):
        low = out[2 * half * quarter : (2 * half + 1) * quarter]
        high = out[(2 * half + 1) * quarter : (2 * half + 2) * quarter]
        keep_ref[half] = jnp.where(first, low, high)
        send_ref[half] = jnp.where(first, high, low)


def attn_forward_kernel(core, length, pieces, w):
    quarter, model = pieces[0].shape
    rows = 4 * quarter
    width = w.shape[1] // 4
    row_b = jax.ShapeDtypeStruct((rows, width), BF16)
    piece = jax.ShapeDtypeStruct((2, quarter, model), BF16)
    return pl.pallas_call(
        attn_fwd_body,
        in_specs=[SCALAR, SCALAR] + [WHOLE] * 5,
        out_shape=(
            piece, piece,
            jax.ShapeDtypeStruct((rows, model), BF16),
            row_b, row_b, row_b,
            jax.ShapeDtypeStruct((width, rows), BF16),
            jax.ShapeDtypeStruct((8, rows), F32),
        ),
        compiler_params=pltpu.CompilerParams(vmem_limit_bytes=VMEM_LIMIT),
        cost_estimate=cost(12),
        name="attn_forward",
    )(core, length, *pieces, w)


def attn_bwd_body(
    core_ref, len_ref, a_ref, b_ref, c_ref, d_ref, w_ref, q_ref, k_ref, v_ref, lse_ref,
    keep_ref, send_ref, g_ref, gp_ref, ga, gqt, acck, accv
):
    rows, width = q_ref.shape
    places = piece_rows(core_ref[0], a_ref.shape[0])
    wo = w_ref[:, 3 * width :]
    for piece_ref, place in zip((a_ref, b_ref, c_ref, d_ref), places):
        piece = piece_ref[...]
        g_ref[place] = piece
        ga[place] = dot(piece, wo).astype(BF16)
    length = len_ref[0]
    scale = HEAD**-0.5
    acck[...] = jnp.zeros(acck.shape, F32)
    accv[...] = jnp.zeros(accv.shape, F32)
    for h in range(width // HEAD):
        lanes = slice(h * HEAD, (h + 1) * HEAD)
        q = q_ref[:, lanes] * jnp.asarray(scale, BF16)
        k = k_ref[:, lanes]
        kt = k.T
        v = v_ref[:, lanes]
        g = ga[:, lanes]
        for first in range(0, rows, QROWS):
            n = first + QROWS
            s = dot_nt(k[:n], q[first:n])
            probs = jnp.where(
                allowed_keys(n, first, QROWS, length), jnp.exp(s - lse_ref[h : h + 1, first:n]), 0.0
            )
            gp = dot_nt(v[:n], g[first:n])
            inner = jnp.sum(probs * gp, axis=0, keepdims=True)
            gs = (probs * (gp - inner)).astype(BF16)
            gqt[lanes, first:n] = dot(kt[:, :n], gs) * scale
            acck[h, :n] += dot(gs, q[first:n])
            accv[h, :n] += dot(probs.astype(BF16), g[first:n])
        gp_ref[:, width + h * HEAD : width + (h + 1) * HEAD] = acck[h].astype(BF16)
        gp_ref[:, 2 * width + h * HEAD : 2 * width + (h + 1) * HEAD] = accv[h].astype(BF16)
    gp_ref[:, :width] = gqt[...].T.astype(BF16)
    wp = w_ref[:, : 3 * width]
    for i, place in enumerate(places):
        (keep_ref, send_ref)[i % 2][i // 2] = dot_nt(gp_ref[place], wp).astype(BF16)


def attn_backward_kernel(core, length, pieces, w, q, k, v, lse):
    quarter, model = pieces[0].shape
    rows, width = q.shape
    piece = jax.ShapeDtypeStruct((2, quarter, model), BF16)
    heads = width // HEAD
    return pl.pallas_call(
        attn_bwd_body,
        in_specs=[SCALAR, SCALAR] + [WHOLE] * 9,
        out_shape=(
            piece, piece,
            jax.ShapeDtypeStruct((rows, model), BF16),
            jax.ShapeDtypeStruct((rows, 3 * width), BF16),
        ),
        scratch_shapes=[
            pltpu.VMEM((rows, width), BF16),
            pltpu.VMEM((width, rows), F32),
            pltpu.VMEM((heads, rows, HEAD), F32),
            pltpu.VMEM((heads, rows, HEAD), F32),
        ],
        compiler_params=pltpu.CompilerParams(vmem_limit_bytes=VMEM_LIMIT),
        cost_estimate=cost(14),
        name="attn_backward",
    )(core, length, *pieces, w, q, k, v, lse)


EPSILON = 1e-05


def kernel_call(body, outs, name, us, scalars=0, scratch=()):
    def call(*args):
        return pl.pallas_call(
            body,
            in_specs=[SCALAR] * scalars + [WHOLE] * (len(args) - scalars),
            out_shape=outs,
            scratch_shapes=list(scratch),
            cost_estimate=cost(us),
            compiler_params=pltpu.CompilerParams(vmem_limit_bytes=VMEM_LIMIT),
            name=name,
        )(*args)

    return call


def shaped(shape, dtype):
    return jax.ShapeDtypeStruct(shape, dtype)


def statistics(h):
    average = jnp.mean(h, axis=1, keepdims=True)
    centred = h - average
    inverse = lax.rsqrt(jnp.mean(centred * centred, axis=1, keepdims=True) + EPSILON)
    return centred * inverse, inverse


def norm_gradient(grad_normed, h, gain):
    unit, inverse = statistics(h)
    scaled = grad_normed * gain
    first_mean = jnp.mean(scaled, axis=1, keepdims=True)
    second_mean = jnp.mean(scaled * unit, axis=1, keepdims=True)
    gain_grad = jnp.sum(grad_normed * unit, axis=0, keepdims=True)
    return inverse * (scaled - first_mean - unit * second_mean), gain_grad


def first_norm_body(chip_ref, mine_ref, other_ref, gain_ref, h0_ref, n0_ref, h1_ref, n1_ref):
    mine = mine_ref[...].astype(F32)
    other = other_ref[...].astype(F32)
    first = chip_ref[0] == 0
    for h, h_ref, n_ref in (
        (jnp.where(first, mine, other), h0_ref, n0_ref),
        (jnp.where(first, other, mine), h1_ref, n1_ref),
    ):
        h_ref[...] = h
        unit, _ = statistics(h)
        n_ref[...] = (unit * gain_ref[...]).astype(BF16)


def first_norm(chip, mine, other, gain):
    state, normed = shaped(mine.shape, F32), shaped(mine.shape, BF16)
    outs = (state, normed, state, normed)
    return kernel_call(first_norm_body, outs, "first_norm", 2.5, 1)(chip, mine, other, gain)


def both(pair_ref, received_ref):
    return pair_ref[...].astype(F32) + received_ref[...].astype(F32)


def norm_body(h_ref, pair_ref, received_ref, gain_ref, state_ref, normed_ref):
    h = h_ref[...] + both(pair_ref, received_ref)
    state_ref[...] = h
    unit, _ = statistics(h)
    normed_ref[...] = (unit * gain_ref[...]).astype(BF16)


def norm_step(h, pair, received, gain):
    outs = (shaped(h.shape, F32), shaped(h.shape, BF16))
    return kernel_call(norm_body, outs, "norm_step", 1.5)(h, pair, received, gain)


def back_body(g_ref, pair_ref, received_ref, h_ref, gain_ref, grad_ref, low_ref, gain_grad_ref):
    grad, gain_grad_ref[...] = norm_gradient(
        both(pair_ref, received_ref), h_ref[...], gain_ref[...]
    )
    grad = g_ref[...].astype(F32) + grad
    grad_ref[...] = grad
    low_ref[...] = grad.astype(BF16)


def back_step(g, pair, received, h, gain):
    outs = (shaped(g.shape, F32), shaped(g.shape, BF16), shaped(gain.shape, F32))
    return kernel_call(back_body, outs, "back_step", 2)(g, pair, received, h, gain)


def last_back_body(chip_ref, g0, h0, g1, h1, own_ref, received_ref, gain_ref, out_ref):
    first = chip_ref[0] == 0
    grad_normed = both(own_ref, received_ref)
    h = jnp.where(first, h0[...], h1[...])
    grad = jnp.where(first, g0[...], g1[...])
    out_ref[...] = (grad + norm_gradient(grad_normed, h, gain_ref[...])[0]).astype(BF16)


def last_back(chip, grads, states, own, received, gain):
    outs = shaped(received.shape, BF16)
    return kernel_call(last_back_body, outs, "last_back", 2, 1)(
        chip, grads[0], states[0], grads[1], states[1], own, received, gain
    )


def own_half_body(chip_ref, keep_ref, received_ref, own_ref, send_ref):
    first = chip_ref[0] == 0
    low = keep_ref[0].astype(F32) + received_ref[0].astype(F32)
    high = keep_ref[1].astype(F32) + received_ref[1].astype(F32)
    own_ref[...] = jnp.where(first, low, high).astype(BF16)
    send_ref[...] = jnp.where(first, high, low).astype(BF16)


def own_half(chip, keep, received):
    piece = shaped(keep.shape[1:], BF16)
    return kernel_call(own_half_body, (piece, piece), "own_half", 2, 1)(chip, keep, received)


ROOT = 0.7978845608028654
CUBIC = 0.044715


def gelu(u):
    return 0.5 * u * (1.0 + jnp.tanh(ROOT * (u + CUBIC * u * u * u)))


def gelu_parts(u):
    square = u * u
    t = jnp.tanh(ROOT * (u + CUBIC * u * square))
    half = 0.5 * (1.0 + t)
    slope = half + 0.5 * u * (1.0 - t * t) * (ROOT * (1.0 + 3.0 * CUBIC * square))
    return u * half, slope


PIECE = 768


def unit_pieces(units, *refs):
    for i, ref in enumerate(refs):
        yield slice(i * units, (i + 1) * units), ref[:, :units], ref[:, units : 2 * units]


def ffn_fwd_body(
    h_ref, pair_ref, received_ref, gain_ref, own_ref, mate_ref, state_ref, n_ref, hidden_ref, out_ref
):
    units = mate_ref.shape[1] // 2
    h = h_ref[...] + both(pair_ref, received_ref)
    state_ref[...] = h
    unit, _ = statistics(h)
    n = (unit * gain_ref[...]).astype(BF16)
    n_ref[...] = n
    out = None
    for lanes, up, down in unit_pieces(units, own_ref, mate_ref):
        hidden = dot(n, up)
        hidden_ref[:, lanes] = hidden
        part = dot_nt(gelu(hidden).astype(BF16), down)
        out = part if out is None else out + part
    out_ref[...] = out.astype(BF16)


def ffn_forward(h, pair, received, gain, own, mate):
    piece = shaped(h.shape, BF16)
    hidden = shaped((h.shape[0], mate.shape[1]), F32)
    outs = (shaped(h.shape, F32), piece, hidden, piece)
    return kernel_call(ffn_fwd_body, outs, "ffn_forward", 50)(h, pair, received, gain, own, mate)


def ffn_both_body(
    h_ref, pair_ref, received_ref, gain_ref, g_ref, own_ref, mate_ref,
    state_ref, n_ref, grad_ref, active_ref, out_ref,
):
    units = mate_ref.shape[1] // 2
    h = h_ref[...] + both(pair_ref, received_ref)
    state_ref[...] = h
    unit, _ = statistics(h)
    n = (unit * gain_ref[...]).astype(BF16)
    n_ref[...] = n
    g = g_ref[...]
    out = None
    for lanes, up, down in unit_pieces(units, own_ref, mate_ref):
        active, slope = gelu_parts(dot(n, up))
        active_ref[:, lanes] = active.astype(BF16)
        grad = (dot(g, down) * slope).astype(BF16)
        grad_ref[:, lanes] = grad
        part = dot_nt(grad, up)
        out = part if out is None else out + part
    out_ref[...] = out.astype(BF16)


def ffn_both(h, pair, received, gain, g, own, mate):
    piece = shaped(h.shape, BF16)
    rows = shaped((h.shape[0], mate.shape[1]), BF16)
    outs = (shaped(h.shape, F32), piece, rows, rows, piece)
    return kernel_call(ffn_both_body, outs, "ffn_both", 60)(h, pair, received, gain, g, own, mate)


def ffn_bwd_body(
    g_ref, pair_ref, received_ref, h_ref, gain_ref, hidden_ref, own_ref, mate_ref,
    total_ref, low_ref, grad_ref, active_ref, out_ref, gain_grad_ref,
):
    units = mate_ref.shape[1] // 2
    total, gain_grad_ref[...] = norm_gradient(
        both(pair_ref, received_ref), h_ref[...], gain_ref[...]
    )
    total = g_ref[...] + total
    total_ref[...] = total
    g = total.astype(BF16)
    low_ref[...] = g
    out = None
    for lanes, up, down in unit_pieces(units, own_ref, mate_ref):
        active, slope = gelu_parts(hidden_ref[:, lanes])
        active_ref[:, lanes] = active.astype(BF16)
        grad = (dot(g, down) * slope).astype(BF16)
        grad_ref[:, lanes] = grad
        part = dot_nt(grad, up)
        out = part if out is None else out + part
    out_ref[...] = out.astype(BF16)


def ffn_backward(g, pair, received, h, gain, hidden, own, mate):
    piece = shaped(h.shape, BF16)
    rows = shaped(hidden.shape, BF16)
    outs = (shaped(h.shape, F32), piece, rows, rows, piece, shaped(gain.shape, F32))
    return kernel_call(ffn_bwd_body, outs, "ffn_backward", 60)(
        g, pair, received, h, gain, hidden, own, mate
    )


def ffn_out_body(chip_ref, a0_ref, a1_ref, own_ref, mate_ref, out_ref, send_ref):
    units = mate_ref.shape[1] // 2
    outs = []
    for a_ref in (a0_ref, a1_ref):
        out = None
        for lanes, _, down in unit_pieces(units, own_ref, mate_ref):
            part = dot_nt(a_ref[:, lanes], down)
            out = part if out is None else out + part
        outs.append(out)
    first = chip_ref[0] == 0
    out_ref[...] = jnp.where(first, outs[0], outs[1]).astype(BF16)
    send_ref[...] = jnp.where(first, outs[1], outs[0]).astype(BF16)


def ffn_out(chip, active0, active1, own, mate):
    piece = shaped((active0.shape[0], own.shape[0]), BF16)
    return kernel_call(ffn_out_body, (piece, piece), "ffn_out", 3, 1)(
        chip, active0, active1, own, mate
    )


def output_body(chip_ref, h0_ref, h1_ref, own_ref, received_ref, out_ref):
    h = jnp.where(chip_ref[0] == 0, h0_ref[...], h1_ref[...])
    out_ref[...] = (h + both(own_ref, received_ref)).astype(BF16)


def output_step(chip, states, own, received):
    outs = shaped(own.shape, BF16)
    return kernel_call(output_body, outs, "output_step", 2, 1)(chip, *states, own, received)


def ffn_grads_body(n0, n1, g0, g1, gh0, gh1, a0, a1, own_ref, *mate_refs):
    count = len(mate_refs) // 2
    units = count * PIECE
    for i in range(count):
        lanes = slice(units + i * PIECE, units + (i + 1) * PIECE)
        mate_refs[i][...] = (
            dot_tn(n0[...], gh0[:, lanes]) + dot_tn(n1[...], gh1[:, lanes])
        ).astype(BF16)
        mate_refs[count + i][...] = (
            dot_tn(g0[...], a0[:, lanes]) + dot_tn(g1[...], a1[:, lanes])
        ).astype(BF16)
    own_ref[:, :units] = (
        dot_tn(n0[...], gh0[:, :units]) + dot_tn(n1[...], gh1[:, :units])
    ).astype(BF16)
    own_ref[:, units:] = (
        dot_tn(g0[...], a0[:, :units]) + dot_tn(g1[...], a1[:, :units])
    ).astype(BF16)


def ffn_grads(n, g, grad_hidden, active):
    model, units = n[0].shape[1], active[0].shape[1]
    outs = (shaped((model, units), BF16),) + (shaped((model, PIECE), BF16),) * (units // PIECE)
    own, *mate = kernel_call(ffn_grads_body, outs, "ffn_grads", 6)(*n, *g, *grad_hidden, *active)
    return own, mate


def attn_grads_body(x_ref, gp_ref, g_ref, att_ref, own_ref, *refs):
    *mate_refs, out_ref = refs
    first = own_ref.shape[1]
    joined = first + gp_ref.shape[1]
    for i, mate_ref in enumerate(mate_refs):
        lanes = slice(i * PIECE, (i + 1) * PIECE)
        out_ref[:, lanes] = (own_ref[:, lanes].astype(F32) + mate_ref[...].astype(F32)).astype(BF16)
    out_ref[:, first:joined] = dot_tn(x_ref[...], gp_ref[...]).astype(BF16)
    out_ref[:, joined:] = lax.dot_general(
        g_ref[...], att_ref[...], (((0,), (1,)), ((), ())), preferred_element_type=F32
    ).astype(BF16)


def attn_grads(x, joined, g, attended_t, own, mate):
    columns = own.shape[1] + joined.shape[1] + attended_t.shape[0]
    outs = shaped((x.shape[1], columns), BF16)
    return kernel_call(attn_grads_body, outs, "attn_grads", 8)(
        x, joined, g, attended_t, own, *mate
    )


def halved(side, count, bit, rows_of, keep_ref, send_ref, lanes=slice(None)):
    block = keep_ref.shape[0] * 2 // count
    place = 0
    for j in range(count):
        if j & bit:
            continue
        low, high = rows_of(j * block, block), rows_of((j | bit) * block, block)
        here = slice(place, place + block)
        keep_ref[here, lanes] = jnp.where(side == 0, low, high).astype(BF16)
        send_ref[here, lanes] = jnp.where(side == 0, high, low).astype(BF16)
        place += block


def halves_of(rows, columns):
    return (shaped((rows // 2, columns), BF16),) * 2


def ffn_cut(side, own, mate, count, bit):
    def body(side_ref, own_ref, *refs):
        *mate_refs, keep_ref, send_ref = refs
        for i, mate_ref in enumerate(mate_refs):
            lanes = slice(i * PIECE, (i + 1) * PIECE)

            def rows_of(first, size, mate_ref=mate_ref, lanes=lanes):
                here = slice(first, first + size)
                return own_ref[here, lanes].astype(F32) + mate_ref[here].astype(F32)

            halved(side_ref[0], count, bit, rows_of, keep_ref, send_ref, lanes)

    return kernel_call(body, halves_of(*own.shape), "ffn_cut", 3, 1)(side, own, *mate)


def mixer_grads(side, x, joined, g, mixed, w, count, bit):
    model, columns = x.shape[1], joined.shape[1] + mixed.shape[1]
    inputs = joined.shape[1]

    def body(side_ref, x_ref, gp_ref, g_ref, mixed_ref, w_ref, keep_ref, send_ref, gain_ref, total):
        total[:, :inputs] = dot_tn(x_ref[...], gp_ref[...])
        total[:, inputs:] = dot_tn(g_ref[...], mixed_ref[...])
        halved(
            side_ref[0], count, bit, lambda first, size: total[first : first + size], keep_ref, send_ref
        )
        weighted = total[:, :inputs] * w_ref[:, :inputs].astype(F32)
        high, low = split(weighted)
        ones = jnp.ones((8, inputs), BF16)
        gain_ref[...] = (dot_nt(ones, high) + dot_nt(ones, low))[:1]

    outs = halves_of(model, columns) + (shaped((1, model), F32),)
    return kernel_call(body, outs, "mixer_grads", 6, 1, [pltpu.VMEM((model, columns), F32)])(
        side, x, joined, g, mixed, w
    )


def scatter_step(side, keep, received, count, bit):
    def body(side_ref, kept_ref, received_ref, keep_ref, send_ref):
        def rows_of(first, size):
            here = slice(first, first + size)
            return kept_ref[here].astype(F32) + received_ref[here].astype(F32)

        halved(side_ref[0], count, bit, rows_of, keep_ref, send_ref)

    return kernel_call(body, halves_of(*keep.shape), "scatter_step", 2, 1)(side, keep, received)


def gain_places(count, rows, model, gains):
    block = model // count
    lanes = gains * block // rows
    step = math.gcd(block, lanes)
    places = []
    for j in range(count):
        for i in range(gains):
            for first in range(0, block, step):
                flat = i * block + first
                places.append((i, j * block + first, step, j * rows + flat // lanes, flat % lanes))
    return places, lanes


def small_cut(side, taps, tiles, gains, count, bit):
    width = taps.shape[1]
    starts = [0] * len(tiles)
    for i in range(1, len(tiles)):
        starts[i] = starts[i - 1] + tiles[i - 1][0].shape[1]
    places, lanes = gain_places(count, taps.shape[0] // count, gains.shape[1], gains.shape[0])

    def body(side_ref, taps_ref, gains_ref, *refs):
        *tile_refs, keep_ref, send_ref, total = refs
        total[:, :width] = taps_ref[...]
        for i, start in enumerate(starts):
            size = tile_refs[2 * i].shape[1]
            total[:, width + start : width + start + size] = tile_refs[2 * i][...]
            total[:, 2 * width + start : 2 * width + start + size] = tile_refs[2 * i + 1][...]
        for i, first, size, row, lane in places:
            here = slice(3 * width + lane, 3 * width + lane + size)
            total[row : row + 1, here] = gains_ref[i : i + 1, first : first + size]
        halved(
            side_ref[0], count, bit, lambda first, size: total[first : first + size], keep_ref, send_ref
        )

    shape = (taps.shape[0], 3 * width + lanes)
    return kernel_call(
        body, halves_of(*shape), "small_cut", 2, 1, [pltpu.VMEM(shape, F32)]
    )(side, taps, gains, *[x for tile in tiles for x in tile])


def finish_small(keep, received, gains, width):
    rows = keep.shape[0]
    count, block = gains.shape
    places, _ = gain_places(1, rows, block, count)

    def body(keep_ref, received_ref, gains_ref, taps_ref, decay_ref, coef_ref, gain_grad_ref):
        total = keep_ref[...].astype(F32) + received_ref[...].astype(F32)
        taps_ref[...] = total[:, :width]
        decay_ref[...] = total[:, width : 2 * width]
        coef_ref[...] = total[:, 2 * width : 3 * width]
        for i, first, size, row, lane in places:
            lanes = slice(3 * width + lane, 3 * width + lane + size)
            part = total[row : row + 1, lanes]
            if i == 0:
                part = part / gains_ref[:1, first : first + size]
            gain_grad_ref[i : i + 1, first : first + size] = part

    outs = (
        shaped((rows, width), F32), shaped((rows, width), F32), shaped((rows, width), F32),
        shaped((count, block), F32),
    )
    return kernel_call(body, outs, "finish_small", 2)(keep, received, gains)


def summed(parts, lanes):
    total = parts[0][:, lanes].astype(F32)
    for part in parts[1:]:
        total = total + part[:, lanes].astype(F32)
    return total


def finish(parts, ffn_parts, first, ffn_first, width, units):
    rows = parts[0].shape[0]
    count = len(parts)

    def body(*refs):
        part_refs, ffn_refs = refs[:count], refs[count : 2 * count]
        q_ref, k_ref, v_ref, o_ref, up_ref, down_ref = refs[2 * count :]
        for i, out_ref in enumerate((q_ref, k_ref, v_ref)):
            out_ref[...] = summed(part_refs, slice(first + i * width, first + (i + 1) * width))
        o_ref[...] = summed(part_refs, slice(first + 3 * width, first + 4 * width)).T
        up_ref[...] = summed(ffn_refs, slice(ffn_first, ffn_first + units))
        down_ref[...] = summed(ffn_refs, slice(ffn_first + units, ffn_first + 2 * units))

    square = shaped((rows, width), F32)
    outs = (
        square, square, square, shaped((width, rows), F32),
        shaped((rows, units), F32), shaped((rows, units), F32),
    )
    return kernel_call(body, outs, "finish", 5)(*parts, *ffn_parts)


TENSOR = "tensor"
DATA = "dp"


def swap(x, bit):
    return lax.ppermute(x, TENSOR, [(i, i ^ bit) for i in range(4)])


def from_mate(x):
    return swap(x, 1)


def from_chip(x):
    return swap(x, 2)


def tie(*values):
    return lax.optimization_barrier(values)


def after(value, *others):
    return lax.optimization_barrier((value,) + others)[0]


def row_major(x):
    return with_layout_constraint(x, Layout(major_to_minor=tuple(range(x.ndim))))


def add_cores(keep, send):
    return (keep.astype(F32) + from_mate(send).astype(F32)).astype(BF16)


class Rows:
    def __init__(self):
        self.count = lax.axis_size(DATA)
        self.index = lax.axis_index(DATA)
        self.depth = self.count.bit_length() - 1
        self.bits = [1 << i for i in reversed(range(self.depth))]

    def swap(self, x, bit):
        return lax.ppermute(x, DATA, [(i, i ^ bit) for i in range(self.count)])

    def gather_send(self, x, step):
        return self.swap(x, self.bits[step])

    def gather_merge(self, x, other, step):
        upper = (self.index & self.bits[step]) != 0
        return jnp.stack([jnp.where(upper, other, x), jnp.where(upper, x, other)], axis=step)

    def gather_step(self, x, step):
        return self.gather_merge(x, self.gather_send(x, step), step)

    def gather(self, x, first=0, last=None):
        for step in range(first, self.depth if last is None else last):
            x = self.gather_step(x, step)
        return x

    def flat(self, x):
        return x.reshape(self.count * x.shape[-2], x.shape[-1])

    def parts(self, x):
        return x.reshape((2,) * self.depth + (x.shape[0] // self.count, x.shape[1]))

    def cut(self, x, step):
        side = ((self.index & self.bits[step]) != 0).astype(jnp.int32)
        keep = lax.dynamic_slice_in_dim(x, side, 1, step)
        send = lax.dynamic_slice_in_dim(x, 1 - side, 1, step)
        return keep, send.astype(BF16)

    def side(self, step):
        return ((self.index & self.bits[step]) != 0).astype(jnp.int32).reshape(1)

    def without(self, x, step):
        shape = [2] * self.depth
        shape[step] = 1
        return x.reshape(tuple(shape) + (x.shape[0] * 2 // self.count, x.shape[1]))

    def scatter(self, x, steps):
        for step in steps:
            keep, send = self.cut(x, step)
            x = keep.astype(F32) + self.swap(send, self.bits[step]).astype(F32)
        return x


def on_device(
    tokens, cotangent, seq_lengths,
    gain_mixer, mixer_query, mixer_key, mixer_value, shift_taps, ssm_decay, ssm_coef, mixer_out,
    gain_ffn1, ffn1_up, ffn1_down,
    gain_attn, attn_query, attn_key, attn_value, attn_out,
    gain_ffn2, ffn2_up, ffn2_down,
):
    place = lax.axis_index(TENSOR)
    chip = place >> 1
    core = (place & 1).astype(jnp.int32).reshape(1)
    chips = chip.astype(jnp.int32).reshape(1)
    rows = Rows()
    fwd, inv = spectral_tables()
    quarter, model = tokens.shape
    length = 4 * quarter
    block, width = mixer_query.shape
    units = ffn1_up.shape[1]
    unit_rows = shift_taps.shape[0]
    states = unit_rows * rows.count

    own_gains = jnp.stack([gain_mixer, gain_ffn1, gain_attn, gain_ffn2], axis=0)
    small = jnp.zeros((16, model), BF16)
    small = small.at[:unit_rows, : 3 * width].set(
        jnp.concatenate([shift_taps, ssm_decay.T, ssm_coef.T], axis=1)
    )
    small = small.at[12:16, :block].set(own_gains)
    mixer_own = jnp.concatenate([mixer_query, mixer_key, mixer_value, mixer_out.T], axis=1)
    ffn1_own = jnp.concatenate([ffn1_up, ffn1_down.T], axis=1)
    attn_own = jnp.concatenate([attn_query, attn_key, attn_value, attn_out.T], axis=1)
    ffn2_own = jnp.concatenate([ffn2_up, ffn2_down.T], axis=1)
    top = rows.depth - 1
    positions = place * quarter + jnp.arange(quarter)
    live = (positions < seq_lengths[0])[:, None]
    masked = jnp.where(live, cotangent, jnp.zeros_like(cotangent))
    small = rows.gather(small, 0, 1)
    mixer_w = rows.gather(mixer_own, 0, 1)
    there = from_chip(tokens)
    first_w = lax.all_gather(
        jnp.concatenate([ffn1_own, attn_own], axis=1), DATA, axis=0, tiled=True
    )
    small = rows.gather(small, 1, top)
    mixer_w = rows.gather(mixer_w, 1, top)
    small = rows.gather(small, top).reshape(rows.count, 16, model)
    small, mixer_w = tie(small, mixer_w)
    mixer_other = rows.gather_send(mixer_w, top)

    gains = small[:, 12:16, :block].transpose(1, 0, 2).reshape(4, 1, model).astype(F32)
    vectors = small[:, :unit_rows, : 3 * width].reshape(states, 3 * width).astype(F32)
    taps_w, decay_t, coef_t = (vectors[:, i * width : (i + 1) * width] for i in range(3))
    h0, n0, h1, n1 = first_norm(chips, tokens, there, gains[0])
    start = [h0, h1]
    grad_other = from_chip(after(masked, n0))
    spectra = kernel_spectra(after(decay_t, n0), coef_t, taps_w, fwd, length)
    pieces = [n0, from_mate(n0), n1, from_mate(n1)]
    mixer_other, grad_other = after((mixer_other, grad_other), spectra[0])
    mixer_w = rows.flat(rows.gather_merge(mixer_w, mixer_other, top))
    keep, send, x1, mixed, *saved = mixer_forward_kernel(
        core, pieces, mixer_w, spectra, fwd, inv
    )

    def core_sums(keep, send):
        other = from_mate(send)
        return [(keep[i].astype(F32) + other[i].astype(F32)).astype(BF16) for i in range(2)]

    def exchanged(keep, send):
        sums = core_sums(keep, send)
        return sums, [from_chip(p) for p in sums]

    pairs, received = exchanged(keep, send)
    first_w = after(first_w, pairs[1])
    ffn1_w, attn_w = first_w[:, : 2 * units], first_w[:, 2 * units :]
    grad = [jnp.where(chip == 0, masked, grad_other), jnp.where(chip == 0, grad_other, masked)]
    received[0], attn_w, *grad = tie(received[0], attn_w, *grad)
    ffn1_mate = from_mate(ffn1_w)
    ffn2_w = lax.all_gather(after(ffn2_own, pairs[1]), DATA, axis=0, tiled=True)
    ffn1_mate = after(ffn1_mate, received[0])
    after_mixer, n2, hidden1, nexts, arrived = [], [], [], [], []
    for half in range(2):
        wait = received[0] if half == 0 else after(received[1], nexts[0])
        h, n, hidden, out = ffn_forward(
            start[half], pairs[half], wait, gains[1], ffn1_w, ffn1_mate
        )
        after_mixer.append(h)
        n2.append(n)
        hidden1.append(hidden)
        nexts.append(out)
        arrived.append(from_chip(out))
    after_ffn1, pieces = [], []
    for half in range(2):
        wait = after(arrived[half], nexts[1]) if half == 0 else after(arrived[1], pieces[0])
        h, n = norm_step(after_mixer[half], nexts[half], wait, gains[2])
        after_ffn1.append(h)
        pieces += [n, from_mate(n)]
    keep, send, x3, q2, k2, v2, attended_t, log_total = attn_forward_kernel(
        core, seq_lengths, pieces, attn_w
    )
    pairs, received = exchanged(keep, send)
    ffn2_w = after(ffn2_w, pairs[1])

    ffn2_mate = from_mate(ffn2_w)
    g4 = list(grad)
    ffn2_mate = after(ffn2_mate, received[0])
    after_attn, n4, gh, act, nexts, arrived = [], [], [], [], [], []
    for half in range(2):
        wait = received[0] if half == 0 else after(received[1], nexts[0])
        h, n, grad_hidden, active, out = ffn_both(
            after_ffn1[half], pairs[half], wait, gains[3], g4[half], ffn2_w, ffn2_mate
        )
        after_attn.append(h)
        n4.append(n)
        gh.append(grad_hidden)
        act.append(active)
        nexts.append(out)
        arrived.append(from_chip(out))
    lows, ffn2_gain = [], []
    wait = after(arrived[0], nexts[1])
    grad[0], low, part = back_step(grad[0], nexts[0], wait, after_attn[0], gains[3])
    ffn2_gain.append(part)
    lows.append(low)
    gh, act = after((gh, act), low)
    own, mate = ffn_grads(n4, g4, gh, act)
    wait = after(arrived[1], mate[-1])
    grad[1], low, part = back_step(grad[1], nexts[1], wait, after_attn[1], gains[3])
    ffn2_gain.append(part)
    lows.append(low)
    pieces = [lows[0], from_mate(after(lows[0], low)), lows[1], from_mate(lows[1])]
    ffn2_mate_g = [from_mate(x) for x in after(tuple(mate), pieces[1], pieces[3])]
    keep, send, g3, grad_joined = attn_backward_kernel(
        core, seq_lengths, pieces, attn_w, q2, k2, v2, log_total
    )
    pairs, received = exchanged(keep, send)
    own, ffn2_mate_g = after((own, ffn2_mate_g), pairs[1])
    second_p = attn_grads(x3, grad_joined, g3, attended_t, own, ffn2_mate_g)
    step = rows.depth - 1
    final_own, final_sent = ffn_out(chips, *after(tuple(act), second_p), ffn2_w, ffn2_mate)
    received = list(after(tuple(received), second_p, final_sent))

    g2, gh, act_b, nexts, arrived, attn_gain = [], [], [], [], [], []
    for half in range(2):
        wait = received[half]
        grad[half], low, grad_hidden, active, out, part = ffn_backward(
            grad[half].astype(F32), pairs[half], wait, after_ffn1[half], gains[2], hidden1[half],
            ffn1_w, ffn1_mate,
        )
        g2.append(low)
        attn_gain.append(part)
        gh.append(grad_hidden)
        act_b.append(active)
        nexts.append(out)
        arrived.append(from_chip(out))
    second_g = lax.psum_scatter(after(second_p, nexts[0]), DATA, scatter_dimension=0, tiled=True)
    lows, ffn1_gain = [], []
    wait = after(arrived[0], nexts[1])
    grad[0], low, part = back_step(grad[0], nexts[0], wait, after_mixer[0], gains[1])
    ffn1_gain.append(part)
    lows.append(low)
    gh, act_b = after((gh, act_b), low)
    own, mate = ffn_grads(n2, g2, gh, act_b)
    wait = after(arrived[1], mate[-1])
    grad[1], low, part = back_step(grad[1], nexts[1], wait, after_mixer[1], gains[1])
    ffn1_gain.append(part)
    lows.append(low)
    pieces = [lows[0], from_mate(lows[0]), lows[1], from_mate(lows[1])]
    mate_g = [from_mate(x) for x in after(tuple(mate), pieces[1], arrived[1])]
    mate_g, pieces[1], pieces[3] = tie(mate_g, pieces[1], pieces[3])
    ffn1_keep, ffn1_send = ffn_cut(rows.side(step), own, mate_g, rows.count, rows.bits[step])
    pieces[0], ffn1_send, final_sent = tie(pieces[0], ffn1_send, final_sent)
    final_received = from_chip(final_sent)
    ffn1_received = rows.swap(ffn1_send, rows.bits[step])
    keep, send, g1, grad_joined, grad_taps, *g_spectrum = mixer_backward_kernel(
        core, pieces, mixer_w, saved[:6], spectra, fwd, inv, states
    )
    mixer_keep, mixer_send, mixer_gain = mixer_grads(
        rows.side(step - 1), x1, grad_joined, g1, mixed, mixer_w, rows.count, rows.bits[step - 1]
    )
    gain_rows = jnp.concatenate(
        [mixer_gain] + [0.5 * (p[0] + p[1]) for p in (ffn1_gain, attn_gain, ffn2_gain)], axis=0
    )
    gain_rows = gain_rows + from_mate(gain_rows)
    gain_rows = gain_rows + from_chip(gain_rows)
    mixer_received = rows.swap(mixer_send, rows.bits[step - 1])
    own, last_sent = own_half(chips, keep, from_mate(after(send, mixer_send)))
    last_received = from_chip(last_sent)
    g_spectrum = after(tuple(g_spectrum), last_sent)
    ssm = [ssm_grad_kernel(g_spectrum, saved[6:], decay_t, coef_t, inv, 0)]

    half, pair = rows.count // 2, rows.count // 4

    def send_on(arrays, step, *ready):
        return [rows.swap(x, rows.bits[step]) for x in arrays]

    ffn1_received = after(ffn1_received, ssm[0][0])
    ffn1_keep, ffn1_send = scatter_step(rows.side(step - 1), ffn1_keep, ffn1_received, half, 1)
    mixer_received = after(mixer_received, ffn1_send)
    mixer_keep, mixer_send = scatter_step(rows.side(step), mixer_keep, mixer_received, half, 1)
    ffn1_received = rows.swap(ffn1_send, rows.bits[step - 1])
    mixer_received = rows.swap(mixer_send, rows.bits[step])
    g_spectrum = after(g_spectrum, mixer_send)
    ssm += [
        ssm_grad_kernel(g_spectrum, saved[6:], decay_t, coef_t, inv, i)
        for i in range(1, len(channel_tiles(width)))
    ]
    small_keep, small_send = small_cut(
        rows.side(step), grad_taps, ssm, gain_rows, rows.count, rows.bits[step]
    )
    small_received = rows.swap(small_send, rows.bits[step])
    small_received = after(small_received, small_send)
    small_keep, small_send = scatter_step(rows.side(step - 1), small_keep, small_received, half, 1)
    small_received = rows.swap(small_send, rows.bits[step - 1])
    ffn1_received, mixer_received, last_received = tie(
        *after((ffn1_received, mixer_received, last_received), small_send)
    )
    ffn1_keep, ffn1_send = scatter_step(rows.side(step - 2), ffn1_keep, ffn1_received, pair, 1)
    mixer_received = after(mixer_received, ffn1_send)
    mixer_keep, mixer_send = scatter_step(rows.side(step - 2), mixer_keep, mixer_received, pair, 1)
    last_received, final_received = after((last_received, final_received), mixer_send)
    input_grad = last_back(chips, grad, start, own, last_received, gains[0])
    output = output_step(chips, after_attn, final_own, final_received)
    small_received = after(small_received, input_grad, output)
    small_keep, small_send = scatter_step(rows.side(step - 2), small_keep, small_received, pair, 1)

    ffn1_received = rows.swap(ffn1_send, rows.bits[step - 2])
    mixer_received = rows.swap(mixer_send, rows.bits[step - 2])
    small_received = rows.swap(small_send, rows.bits[step - 2])
    second_g = [after(second_g, small_send)]

    aq, ak, av, ao, u2, d2 = finish(second_g, second_g, 2 * units, 0, width, units)
    ffn1_received, mixer_received, small_received = after(
        (ffn1_received, mixer_received, small_received), aq, input_grad, output
    )
    level, tail = pair // 2, step - 3
    while tail >= 0:
        ffn1_keep, ffn1_send = scatter_step(rows.side(tail), ffn1_keep, ffn1_received, level, 1)
        mixer_keep, mixer_send = scatter_step(rows.side(tail), mixer_keep, mixer_received, level, 1)
        small_keep, small_send = scatter_step(rows.side(tail), small_keep, small_received, level, 1)
        ffn1_received = rows.swap(ffn1_send, rows.bits[tail])
        mixer_received = rows.swap(mixer_send, rows.bits[tail])
        small_received = rows.swap(small_send, rows.bits[tail])
        level, tail = level // 2, tail - 1
    mq, mk, mv, mo, u1, d1 = finish(
        [mixer_keep, mixer_received], [ffn1_keep, ffn1_received], 0, 0, width, units
    )
    gt, gd, gc, gain_grads = finish_small(
        small_keep, after(small_received, mq), own_gains.astype(F32), width
    )
    return (
        output, input_grad,
        gain_grads[0], mq, mk, mv, gt, gd.T, gc.T, mo,
        gain_grads[1], u1, d1.T,
        gain_grads[2], aq, ak, av, ao,
        gain_grads[3], u2, d2.T,
    )


def solution(mesh):
    rows = P(("dp", "tensor"), None)
    up = P("dp", "tensor")
    down = P("tensor", "dp")
    vector = P("dp")
    mixer = (vector, up, up, up, up, down, down, down)
    ffn = (vector, up, down)
    attn = (vector, up, up, up, down)
    weights = mixer + ffn + attn + ffn
    return jax.shard_map(
        on_device,
        mesh=mesh,
        in_specs=(rows, rows, vector) + weights,
        out_specs=(rows, rows) + weights,
        check_vma=False,
    )
```

```python
import math
import numpy as np
import jax
import jax.numpy as jnp
from jax import lax
from jax.experimental import pallas as pl
from jax.experimental.pallas import tpu as pltpu
from jax.experimental.layout import Layout, with_layout_constraint
from jax.sharding import PartitionSpec as P

F32 = jnp.float32
BF16 = jnp.bfloat16
BLK = 128
GROUP = 8
UNROLL = 2
VMEM_LIMIT = 56 * 1024 * 1024


def cost(us):
    return pl.CostEstimate(
        flops=int(us * 1.1e8), transcendentals=0, bytes_accessed=int(us * 3.5e5)
    )


def dot(a, b):
    return jnp.dot(a, b, preferred_element_type=F32)


def dot_nt(a, b):
    return lax.dot_general(a, b, (((1,), (1,)), ((), ())), preferred_element_type=F32)


def split(x):
    high = x.astype(BF16)
    return high, (x - high.astype(F32)).astype(BF16)


def spectral_tables():
    j = np.arange(BLK)
    f = np.arange(BLK)
    angle = 2.0 * np.pi * np.outer(f, j) / (2 * BLK)
    alternating = (-1.0) ** j
    real = np.cos(angle)
    imag = -np.sin(angle)
    imag[0] = alternating
    forward = np.concatenate([real, imag], axis=0)
    weight = np.full((BLK, 1), 2.0)
    weight[0] = 1.0
    back_real = weight * real / (2 * BLK)
    back_imag = 2.0 * imag / (2 * BLK)
    back_imag[0] = alternating / (2 * BLK)
    inverse = np.concatenate([back_real, back_imag], axis=0).T

    def halves(table):
        high = table.astype(jnp.bfloat16)
        low = (table - high.astype(np.float64)).astype(jnp.bfloat16)
        return high, low

    fh, fl = halves(forward)
    ih, il = halves(inverse)
    fwd = np.concatenate([fh, fh, fl], axis=1)
    inv = np.concatenate([ih, il], axis=0)
    return jnp.asarray(fwd), jnp.asarray(inv)


def to_spectrum_exact(fwd_ref, x):
    high, low = split(x)
    return dot(fwd_ref[:, : 2 * BLK], jnp.concatenate([high, low], axis=0)) + dot(
        fwd_ref[:, 2 * BLK :], high
    )


def to_spectrum(fwd_ref, x):
    return dot(fwd_ref[:, :BLK], x.astype(BF16))


def from_spectrum(inv_ref, re, im):
    return dot(inv_ref[:BLK], jnp.concatenate([re.astype(BF16), im.astype(BF16)], axis=0))


def sign_rows(shape):
    row = lax.broadcasted_iota(jnp.int32, shape, 0)
    return jnp.where(row % 2 == 0, 1.0, -1.0).astype(F32)


def lane_tiles(width):
    return [(s, min(128, width - s)) for s in range(0, width, 128)]


def fix_first(tile, re, im):
    row = lax.broadcasted_iota(jnp.int32, re.shape, 0)
    special = (row == 0) & (tile == 0)
    return jnp.where(special, im, re), jnp.where(special, 0.0, im)


def channel_tiles(width):
    return [(s, min(128, width - s), 128 // min(128, width - s)) for s in range(0, width, 128)]


def side_by_side(x, start, size, copies):
    rows = x.shape[0] // copies
    parts = [x[i * rows : (i + 1) * rows, start : start + size] for i in range(copies)]
    return parts[0] if copies == 1 else jnp.concatenate(parts, axis=1)


def kgen_body(decay_ref, coef_ref, taps_ref, fwd_ref, kre_ref, kim_ref, tre_ref, tim_ref, rate, mixp, kern):
    states, width = decay_ref.shape
    blocks = kre_ref.shape[0]
    decay = decay_ref[...]
    mixing = jnp.sqrt(2.0 * decay) * coef_ref[...]
    for start, size, copies in channel_tiles(width):
        rows = states // copies
        tile_decay = side_by_side(decay, start, size, copies)
        tile_mixing = side_by_side(mixing, start, size, copies)
        rate[:rows] = -tile_decay
        for m in range(blocks):
            mixp[m, :rows] = tile_mixing * jnp.exp(tile_decay * (-float(BLK * m)))

        def per_tile(jt, _, start=start, size=size, copies=copies, rows=rows):
            steps = (lax.broadcasted_iota(jnp.int32, (8, 128), 0) + jt * 8).astype(F32)

            def per_states(ng, acc):
                here = pl.ds(pl.multiple_of(ng * 8, 8), 8)
                rates = rate[here]
                scales = [mixp[m, here] for m in range(blocks)]
                for i in range(8):
                    e = jnp.exp(rates[i : i + 1] * steps)
                    acc = tuple(a + e * s[i : i + 1] for a, s in zip(acc, scales))
                return acc

            acc = lax.fori_loop(
                0, rows // 8, per_states, tuple(jnp.zeros((8, 128), F32) for _ in range(blocks))
            )
            place = pl.ds(pl.multiple_of(jt * 8, 8), 8)
            for m in range(blocks):
                total = acc[m][:, :size]
                for i in range(1, copies):
                    total = total + acc[m][:, i * size : (i + 1) * size]
                kern[m, place, start : start + size] = total
            return 0

        lax.fori_loop(0, BLK // 8, per_tile, 0)
    for m in range(blocks):
        spec = to_spectrum_exact(fwd_ref, kern[m])
        kre_ref[m] = spec[:BLK]
        kim_ref[m] = spec[BLK:]
    taps = jnp.concatenate(
        [taps_ref[...], jnp.zeros((BLK - taps_ref.shape[0], width), F32)], axis=0
    )
    spec = to_spectrum_exact(fwd_ref, taps)
    tre_ref[...] = spec[:BLK]
    tim_ref[...] = spec[BLK:]


def kernel_spectra(decay_t, coef_t, taps, fwd, length):
    states, width = decay_t.shape
    blocks = length // BLK
    return pl.pallas_call(
        kgen_body,
        out_shape=(
            jax.ShapeDtypeStruct((blocks, BLK, width), F32),
            jax.ShapeDtypeStruct((blocks, BLK, width), F32),
            jax.ShapeDtypeStruct((BLK, width), F32),
            jax.ShapeDtypeStruct((BLK, width), F32),
        ),
        scratch_shapes=[
            pltpu.VMEM((states, 128), F32),
            pltpu.VMEM((blocks, states, 128), F32),
            pltpu.VMEM((blocks, BLK, width), F32),
        ],
        compiler_params=pltpu.CompilerParams(vmem_limit_bytes=VMEM_LIMIT),
        cost_estimate=cost(11),
        name="kernel_spectra",
    )(decay_t, coef_t, taps, fwd)


def conv_tiles(width, body):
    for start, size in lane_tiles(width):
        lanes = slice(start, start + size)

        def step(ft, _, lanes=lanes):
            body(ft, pl.ds(pl.multiple_of(ft * 8, 8), 8), lanes)
            return 0

        lax.fori_loop(0, BLK // 8, step, 0)


def piece_rows(core, quarter):
    places = []
    for half in range(2):
        for side in (core, 1 - core):
            places.append(pl.ds(pl.multiple_of((2 * half + side) * quarter, quarter), quarter))
    return places


def mixer_fwd_body(
    core_ref, a_ref, b_ref, c_ref, d_ref, w_ref, kre_ref, kim_ref, tre_ref, tim_ref, fwd_ref, inv_ref,
    keep_ref, send_ref,
    x_ref, mixed_ref, q_ref, v_ref, sh_ref, st_ref, sre_ref, sim_ref, ure_ref, uim_ref,
    zre, zim, keys, queries, values, ure, uim,
):
    length, width = q_ref.shape
    blocks = length // BLK
    sign = sign_rows((BLK, width))
    row0 = lax.broadcasted_iota(jnp.int32, (BLK, width), 0) == 0
    places = piece_rows(core_ref[0], a_ref.shape[0])
    wq = w_ref[:, :width]
    wk = w_ref[:, width : 2 * width]
    wv = w_ref[:, 2 * width : 3 * width]
    for piece_ref, place in zip((a_ref, b_ref, c_ref, d_ref), places):
        piece = piece_ref[...]
        x_ref[place] = piece
        queries[place] = dot(piece, wq)
        values[place] = dot(piece, wv)
        keys[place] = dot(piece, wk)
    q_ref[...] = queries[...].astype(BF16)
    v_ref[...] = values[...].astype(BF16)
    tre = tre_ref[...]
    tim = tim_ref[...]
    tre2 = jnp.where(row0, tim, tre)
    tim0 = jnp.where(row0, 0.0, tim)
    last = None
    for p in range(blocks):
        rows = slice(p * BLK, (p + 1) * BLK)
        spec = to_spectrum(fwd_ref, keys[rows])
        re, im = spec[:BLK], spec[BLK:]
        sre_ref[p] = re.astype(BF16)
        sim_ref[p] = im.astype(BF16)
        pr = re * tre - im * tim0
        pi = re * tim0 + im * tre2
        if last is None:
            z = (pr, pi)
        else:
            z = (pr + sign * last[0], pi + sign * last[1])
        last = (pr, pi)
        shifted = from_spectrum(inv_ref, *z)
        sh_ref[rows] = shifted.astype(BF16)
        spec = to_spectrum(fwd_ref, shifted * values[rows])
        ure[p] = spec[:BLK]
        uim[p] = spec[BLK:]
        ure_ref[p] = spec[:BLK].astype(BF16)
        uim_ref[p] = spec[BLK:].astype(BF16)

    def products(ft, fr, lanes):
        sgn = sign[:8, lanes]
        k = [(kre_ref[m, fr, lanes], kim_ref[m, fr, lanes]) for m in range(blocks)]
        k = [(a,) + fix_first(ft, a, b) for a, b in k]
        u = [(ure[m, fr, lanes], uim[m, fr, lanes]) for m in range(blocks)]
        prev = None
        for p in range(blocks):
            yr = yi = None
            for m in range(p + 1):
                ur, ui = u[m]
                kr, kr2, ki0 = k[p - m]
                a = ur * kr - ui * ki0
                b = ur * ki0 + ui * kr2
                yr = a if yr is None else yr + a
                yi = b if yi is None else yi + b
            if prev is None:
                zre[p, fr, lanes] = yr
                zim[p, fr, lanes] = yi
            else:
                zre[p, fr, lanes] = yr + sgn * prev[0]
                zim[p, fr, lanes] = yi + sgn * prev[1]
            prev = (yr, yi)

    conv_tiles(width, products)
    wo = w_ref[:, 3 * width :]
    for half in range(2):
        for p in range(half * blocks // 2, (half + 1) * blocks // 2):
            rows = slice(p * BLK, (p + 1) * BLK)
            state = from_spectrum(inv_ref, zre[p], zim[p])
            st_ref[rows] = state.astype(BF16)
            mixed_ref[rows] = (queries[rows] * state).astype(BF16)
        for out_ref, place in zip((keep_ref, send_ref), places[2 * half : 2 * half + 2]):
            out_ref[half] = dot_nt(mixed_ref[place], wo).astype(BF16)


SCALAR = pl.BlockSpec(memory_space=pltpu.SMEM)
WHOLE = pl.BlockSpec(memory_space=pltpu.VMEM)


def mixer_forward_kernel(core, pieces, w, spectra, fwd, inv):
    quarter, model = pieces[0].shape
    length = 4 * quarter
    width = w.shape[1] // 4
    blocks = length // BLK
    row_f = jax.ShapeDtypeStruct((length, width), BF16)
    spec_f = jax.ShapeDtypeStruct((blocks, BLK, width), BF16)
    piece = jax.ShapeDtypeStruct((2, quarter, model), BF16)
    return pl.pallas_call(
        mixer_fwd_body,
        in_specs=[SCALAR] + [WHOLE] * 11,
        out_shape=(
            piece, piece,
            jax.ShapeDtypeStruct((length, model), BF16),
            jax.ShapeDtypeStruct((length, width), BF16),
            row_f, row_f, row_f, row_f, spec_f, spec_f, spec_f, spec_f,
        ),
        scratch_shapes=[pltpu.VMEM((blocks, BLK, width), F32)] * 2
        + [pltpu.VMEM((length, width), F32)] * 3
        + [pltpu.VMEM((blocks, BLK, width), F32)] * 2,
        compiler_params=pltpu.CompilerParams(vmem_limit_bytes=VMEM_LIMIT),
        cost_estimate=cost(14),
        name="mixer_forward",
    )(core, *pieces, w, *spectra, fwd, inv)


def correlate_tiles(width, blocks, left, other, result):
    left_re, left_im = left
    other_re, other_im = other
    to_re, to_im = result
    sign = sign_rows((8, width))

    def products(ft, fr, lanes):
        sgn = sign[:, lanes]
        k = [(other_re[m, fr, lanes], other_im[m, fr, lanes]) for m in range(blocks)]
        k = [(a,) + fix_first(ft, a, b) for a, b in k]
        g = [(left_re[m, fr, lanes], left_im[m, fr, lanes]) for m in range(blocks)]
        after = None
        for p in reversed(range(blocks)):
            wr = wi = None
            for m in range(p, blocks):
                gr, gi = g[m]
                kr, kr2, ki0 = k[m - p]
                a = gr * kr + gi * ki0
                b = gi * kr2 - gr * ki0
                wr = a if wr is None else wr + a
                wi = b if wi is None else wi + b
            if after is None:
                to_re[p, fr, lanes] = wr
                to_im[p, fr, lanes] = wi
            else:
                to_re[p, fr, lanes] = wr + sgn * after[0]
                to_im[p, fr, lanes] = wi + sgn * after[1]
            after = (wr, wi)

    conv_tiles(width, products)


def mixer_bwd_body(
    core_ref, a_ref, b_ref, c_ref, d_ref, w_ref, q_ref, v_ref, sh_ref, st_ref, sre_ref, sim_ref,
    kre_ref, kim_ref, tre_ref, tim_ref, fwd_ref, inv_ref,
    keep_ref, send_ref, g_ref, gp_ref, taps_ref, gre_ref, gim_ref,
    wre, wim, gre, gim, grad_mixed,
):
    length, width = q_ref.shape
    blocks = length // BLK
    sign = sign_rows((BLK, width))
    row0 = lax.broadcasted_iota(jnp.int32, (BLK, width), 0) == 0
    places = piece_rows(core_ref[0], a_ref.shape[0])
    wo = w_ref[:, 3 * width :]
    for piece_ref, place in zip((a_ref, b_ref, c_ref, d_ref), places):
        piece = piece_ref[...]
        g_ref[place] = piece
        grad_mixed[place] = dot(piece, wo)
    for p in range(blocks):
        rows = slice(p * BLK, (p + 1) * BLK)
        gm = grad_mixed[rows]
        gp_ref[rows, :width] = (gm * st_ref[rows].astype(F32)).astype(BF16)
        spec = to_spectrum(fwd_ref, gm * q_ref[rows].astype(F32))
        gre[p] = spec[:BLK]
        gim[p] = spec[BLK:]
        gre_ref[p] = spec[:BLK].astype(BF16)
        gim_ref[p] = spec[BLK:].astype(BF16)
    correlate_tiles(width, blocks, (gre, gim), (kre_ref, kim_ref), (wre, wim))
    tre = tre_ref[...]
    tim = tim_ref[...]
    tre2 = jnp.where(row0, tim, tre)
    tim0 = jnp.where(row0, 0.0, tim)
    after = None
    next_gs = None
    zero = jnp.zeros((BLK, width), F32)
    corr = [zero, zero, zero, zero]
    for p in reversed(range(blocks)):
        rows = slice(p * BLK, (p + 1) * BLK)
        grad_u = from_spectrum(inv_ref, wre[p], wim[p])
        gp_ref[rows, 2 * width :] = (grad_u * sh_ref[rows].astype(F32)).astype(BF16)
        spec = to_spectrum(fwd_ref, grad_u * v_ref[rows].astype(F32))
        re, im = spec[:BLK], spec[BLK:]
        pr = re * tre + im * tim0
        pi = im * tre2 - re * tim0
        if after is None:
            z = (pr, pi)
        else:
            z = (pr + sign * after[0], pi + sign * after[1])
        after = (pr, pi)
        gp_ref[rows, width : 2 * width] = from_spectrum(inv_ref, *z).astype(BF16)
        sr, si = sre_ref[p].astype(F32), sim_ref[p].astype(F32)
        sr2 = jnp.where(row0, si, sr)
        si0 = jnp.where(row0, 0.0, si)
        corr[0] = corr[0] + (re * sr + im * si0)
        corr[1] = corr[1] + (im * sr2 - re * si0)
        if next_gs is not None:
            nr, ni = next_gs
            corr[2] = corr[2] + (nr * sr + ni * si0)
            corr[3] = corr[3] + (ni * sr2 - nr * si0)
        next_gs = (re, im)
    taps = from_spectrum(inv_ref, corr[0] + sign * corr[2], corr[1] + sign * corr[3])
    taps_ref[...] = taps[: taps_ref.shape[0]]
    wp = w_ref[:, : 3 * width]
    for i, place in enumerate(places):
        (keep_ref, send_ref)[i % 2][i // 2] = dot_nt(gp_ref[place], wp).astype(BF16)


def mixer_backward_kernel(core, pieces, w, saved, spectra, fwd, inv, taps):
    quarter, model = pieces[0].shape
    length = 4 * quarter
    width = w.shape[1] // 4
    blocks = length // BLK
    piece = jax.ShapeDtypeStruct((2, quarter, model), BF16)
    spec_f = jax.ShapeDtypeStruct((blocks, BLK, width), BF16)
    return pl.pallas_call(
        mixer_bwd_body,
        in_specs=[SCALAR] + [WHOLE] * 17,
        out_shape=(
            piece, piece,
            jax.ShapeDtypeStruct((length, model), BF16),
            jax.ShapeDtypeStruct((length, 3 * width), BF16),
            jax.ShapeDtypeStruct((taps, width), F32),
            spec_f, spec_f,
        ),
        scratch_shapes=[pltpu.VMEM((blocks, BLK, width), F32)] * 4
        + [pltpu.VMEM((length, width), F32)],
        compiler_params=pltpu.CompilerParams(vmem_limit_bytes=VMEM_LIMIT),
        cost_estimate=cost(15),
        name="mixer_backward",
    )(core, *pieces, w, *saved, *spectra, fwd, inv)


def ssm_grad_kernel(g_spectrum, u_spectrum, decay_t, coef_t, inv, tile):
    states, width = decay_t.shape
    blocks = g_spectrum[0].shape[0]
    start, size, copies = channel_tiles(width)[tile]
    lanes = slice(start, start + size)
    rows = states // copies
    group = GROUP

    def body(g_re, g_im, u_re, u_im, decay_ref, coef_ref, inv_ref, gd_ref, gc_ref,
             gre, gim, ure, uim, vre, vim, dk_ref, rate, sum_a, sum_b):
        for scratch, ref in ((gre, g_re), (gim, g_im), (ure, u_re), (uim, u_im)):
            scratch[...] = ref[:, :, lanes].astype(F32)
        correlate_tiles(size, blocks, (gre, gim), (ure, uim), (vre, vim))
        rate[:rows] = side_by_side(decay_ref[...], start, size, copies)
        for p in range(blocks):
            part = from_spectrum(inv_ref, vre[p], vim[p])
            dk_ref[p] = part if copies == 1 else jnp.concatenate([part] * copies, axis=1)
        base = lax.broadcasted_iota(jnp.int32, (8, 128), 0).astype(F32)

        def per_group(ng, _):
            here = pl.ds(pl.multiple_of(ng * 8, 8), 8)
            rates = rate[here]
            row_ids = lax.broadcasted_iota(jnp.int32, (8, 128), 0)
            sums_a = jnp.zeros((8, 128), F32)
            sums_b = jnp.zeros((8, 128), F32)
            for first in range(0, 8, group):
                d = [rates[first + i : first + i + 1] for i in range(group)]
                p = [jnp.broadcast_to(jnp.exp(-float(BLK) * x), (8, 128)) for x in d]
                step8 = [jnp.broadcast_to(jnp.exp(-8.0 * x), (8, 128)) for x in d]
                e0 = tuple(jnp.exp(-x * base) for x in d)
                zero = jnp.zeros((8, 128), F32)

                def per_tile(jt, carry, p=p, step8=step8):
                    e, a, b = carry
                    steps = base + (jt * 8).astype(F32)
                    place = pl.ds(pl.multiple_of(jt * 8, 8), 8)
                    dk = [dk_ref[m, place] for m in range(blocks)]
                    ne, na, nb = [], [], []
                    for i in range(group):
                        h = dk[blocks - 1]
                        s = None
                        for m in reversed(range(blocks - 1)):
                            s = h if s is None else s * p[i] + h
                            h = h * p[i] + dk[m]
                        na.append(a[i] + e[i] * h)
                        nb.append(b[i] + e[i] * (steps * h + float(BLK) * (s * p[i])))
                        ne.append(e[i] * step8[i])
                    return tuple(ne), tuple(na), tuple(nb)

                _, a, b = lax.fori_loop(
                    0, BLK // 8, per_tile, (e0, (zero,) * group, (zero,) * group), unroll=UNROLL
                )
                for i in range(group):
                    mine = row_ids == first + i
                    sums_a = jnp.where(mine, jnp.sum(a[i], axis=0, keepdims=True), sums_a)
                    sums_b = jnp.where(mine, jnp.sum(b[i], axis=0, keepdims=True), sums_b)
            sum_a[here] = sums_a
            sum_b[here] = sums_b
            return 0

        lax.fori_loop(0, rows // 8, per_group, 0)
        for i in range(copies):
            here = slice(i * rows, (i + 1) * rows)
            part = slice(i * size, (i + 1) * size)
            a, b = sum_a[:rows, part], sum_b[:rows, part]
            root = jnp.sqrt(2.0 * decay_ref[here, lanes])
            gc_ref[here] = root * a
            gd_ref[here] = coef_ref[here, lanes] * (a / root - root * b)

    out = jax.ShapeDtypeStruct((states, size), F32)
    return pl.pallas_call(
        body,
        out_shape=(out, out),
        scratch_shapes=[pltpu.VMEM((blocks, BLK, size), F32)] * 6
        + [pltpu.VMEM((blocks, BLK, 128), F32)]
        + [pltpu.VMEM((states, 128), F32)] * 3,
        cost_estimate=cost(10),
        compiler_params=pltpu.CompilerParams(vmem_limit_bytes=VMEM_LIMIT),
        name="ssm_grad",
    )(*g_spectrum, *u_spectrum, decay_t, coef_t, inv)


HEAD = 64
QROWS = 256
LIVE = 512


def dot_tn(a, b):
    return lax.dot_general(a, b, (((0,), (0,)), ((), ())), preferred_element_type=F32)


def masked(s, first, length):
    key = lax.broadcasted_iota(jnp.int32, (QROWS, QROWS), 0)
    query = lax.broadcasted_iota(jnp.int32, (QROWS, QROWS), 1)
    parts = []
    for start in range(0, first + QROWS, QROWS):
        part = s[start : start + QROWS]
        allowed = None
        if start == first:
            allowed = key <= query
        if start >= LIVE:
            short = key < length - start
            allowed = short if allowed is None else allowed & short
        parts.append(part if allowed is None else jnp.where(allowed, part, -jnp.inf))
    return parts[0] if len(parts) == 1 else jnp.concatenate(parts, axis=0)


def attn_fwd_body(
    core_ref, len_ref, a_ref, b_ref, c_ref, d_ref, w_ref,
    keep_ref, send_ref, x_ref, q_ref, k_ref, v_ref, att_ref, lse_ref,
):
    rows, width = q_ref.shape
    places = piece_rows(core_ref[0], a_ref.shape[0])
    wq = w_ref[:, :width]
    wk = w_ref[:, width : 2 * width]
    wv = w_ref[:, 2 * width : 3 * width]
    for piece_ref, place in zip((a_ref, b_ref, c_ref, d_ref), places):
        piece = piece_ref[...]
        x_ref[place] = piece
        q_ref[place] = dot(piece, wq).astype(BF16)
        k_ref[place] = dot(piece, wk).astype(BF16)
        v_ref[place] = dot(piece, wv).astype(BF16)
    length = len_ref[0]
    lse_ref[...] = jnp.zeros(lse_ref.shape, F32)
    scale = HEAD**-0.5
    for h in range(width // HEAD):
        lanes = slice(h * HEAD, (h + 1) * HEAD)
        q = q_ref[:, lanes] * jnp.asarray(scale, BF16)
        k = k_ref[:, lanes]
        vt = v_ref[:, lanes].T
        for first in range(0, rows, QROWS):
            n = first + QROWS
            s = dot_nt(k[:n], q[first:n])
            s = masked(s, first, length)
            top = jnp.max(s, axis=0, keepdims=True)
            e = jnp.exp(s - top)
            total = jnp.sum(e, axis=0, keepdims=True)
            probs = (e * (1.0 / total)).astype(BF16)
            att_ref[lanes, first:n] = dot(vt[:, :n], probs).astype(BF16)
            lse_ref[h : h + 1, first:n] = top + jnp.log(total)
    wo = w_ref[:, 3 * width :]
    out = lax.dot_general(
        att_ref[...], wo, (((0,), (1,)), ((), ())), preferred_element_type=F32
    ).astype(BF16)
    quarter = a_ref.shape[0]
    first = core_ref[0] == 0
    for half in range(2):
        low = out[2 * half * quarter : (2 * half + 1) * quarter]
        high = out[(2 * half + 1) * quarter : (2 * half + 2) * quarter]
        keep_ref[half] = jnp.where(first, low, high)
        send_ref[half] = jnp.where(first, high, low)


def attn_forward_kernel(core, length, pieces, w):
    quarter, model = pieces[0].shape
    rows = 4 * quarter
    width = w.shape[1] // 4
    row_b = jax.ShapeDtypeStruct((rows, width), BF16)
    piece = jax.ShapeDtypeStruct((2, quarter, model), BF16)
    return pl.pallas_call(
        attn_fwd_body,
        in_specs=[SCALAR, SCALAR] + [WHOLE] * 5,
        out_shape=(
            piece, piece,
            jax.ShapeDtypeStruct((rows, model), BF16),
            row_b, row_b, row_b,
            jax.ShapeDtypeStruct((width, rows), BF16),
            jax.ShapeDtypeStruct((8, rows), F32),
        ),
        compiler_params=pltpu.CompilerParams(vmem_limit_bytes=VMEM_LIMIT),
        cost_estimate=cost(12),
        name="attn_forward",
    )(core, length, *pieces, w)


def attn_bwd_body(
    core_ref, len_ref, a_ref, b_ref, c_ref, d_ref, w_ref, q_ref, k_ref, v_ref, lse_ref,
    keep_ref, send_ref, g_ref, gp_ref, ga, gqt, acck, accv
):
    rows, width = q_ref.shape
    places = piece_rows(core_ref[0], a_ref.shape[0])
    wo = w_ref[:, 3 * width :]
    for piece_ref, place in zip((a_ref, b_ref, c_ref, d_ref), places):
        piece = piece_ref[...]
        g_ref[place] = piece
        ga[place] = dot(piece, wo).astype(BF16)
    length = len_ref[0]
    scale = HEAD**-0.5
    acck[...] = jnp.zeros(acck.shape, F32)
    accv[...] = jnp.zeros(accv.shape, F32)
    for h in range(width // HEAD):
        lanes = slice(h * HEAD, (h + 1) * HEAD)
        q = q_ref[:, lanes] * jnp.asarray(scale, BF16)
        k = k_ref[:, lanes]
        kt = k.T
        v = v_ref[:, lanes]
        g = ga[:, lanes]
        for first in range(0, rows, QROWS):
            n = first + QROWS
            s = dot_nt(k[:n], q[first:n])
            probs = jnp.exp(masked(s, first, length) - lse_ref[h : h + 1, first:n])
            gp = dot_nt(v[:n], g[first:n])
            inner = jnp.sum(probs * gp, axis=0, keepdims=True)
            gs = (probs * (gp - inner)).astype(BF16)
            gqt[lanes, first:n] = dot(kt[:, :n], gs) * scale
            acck[h, :n] += dot(gs, q[first:n])
            accv[h, :n] += dot(probs.astype(BF16), g[first:n])
        gp_ref[:, width + h * HEAD : width + (h + 1) * HEAD] = acck[h].astype(BF16)
        gp_ref[:, 2 * width + h * HEAD : 2 * width + (h + 1) * HEAD] = accv[h].astype(BF16)
    gp_ref[:, :width] = gqt[...].T.astype(BF16)
    wp = w_ref[:, : 3 * width]
    for i, place in enumerate(places):
        (keep_ref, send_ref)[i % 2][i // 2] = dot_nt(gp_ref[place], wp).astype(BF16)


def attn_backward_kernel(core, length, pieces, w, q, k, v, lse):
    quarter, model = pieces[0].shape
    rows, width = q.shape
    piece = jax.ShapeDtypeStruct((2, quarter, model), BF16)
    heads = width // HEAD
    return pl.pallas_call(
        attn_bwd_body,
        in_specs=[SCALAR, SCALAR] + [WHOLE] * 9,
        out_shape=(
            piece, piece,
            jax.ShapeDtypeStruct((rows, model), BF16),
            jax.ShapeDtypeStruct((rows, 3 * width), BF16),
        ),
        scratch_shapes=[
            pltpu.VMEM((rows, width), BF16),
            pltpu.VMEM((width, rows), F32),
            pltpu.VMEM((heads, rows, HEAD), F32),
            pltpu.VMEM((heads, rows, HEAD), F32),
        ],
        compiler_params=pltpu.CompilerParams(vmem_limit_bytes=VMEM_LIMIT),
        cost_estimate=cost(14),
        name="attn_backward",
    )(core, length, *pieces, w, q, k, v, lse)


EPSILON = 1e-05


def kernel_call(body, outs, name, us, scalars=0, scratch=()):
    def call(*args):
        return pl.pallas_call(
            body,
            in_specs=[SCALAR] * scalars + [WHOLE] * (len(args) - scalars),
            out_shape=outs,
            scratch_shapes=list(scratch),
            cost_estimate=cost(us),
            compiler_params=pltpu.CompilerParams(vmem_limit_bytes=VMEM_LIMIT),
            name=name,
        )(*args)

    return call


def shaped(shape, dtype):
    return jax.ShapeDtypeStruct(shape, dtype)


def statistics(h):
    average = jnp.mean(h, axis=1, keepdims=True)
    centred = h - average
    inverse = lax.rsqrt(jnp.mean(centred * centred, axis=1, keepdims=True) + EPSILON)
    return centred * inverse, inverse


def norm_gradient(grad_normed, h, gain):
    unit, inverse = statistics(h)
    scaled = grad_normed * gain
    first_mean = jnp.mean(scaled, axis=1, keepdims=True)
    second_mean = jnp.mean(scaled * unit, axis=1, keepdims=True)
    gain_grad = jnp.sum(grad_normed * unit, axis=0, keepdims=True)
    return inverse * (scaled - first_mean - unit * second_mean), gain_grad


def first_norm_body(chip_ref, mine_ref, other_ref, gain_ref, h0_ref, n0_ref, h1_ref, n1_ref):
    mine = mine_ref[...].astype(F32)
    other = other_ref[...].astype(F32)
    first = chip_ref[0] == 0
    for h, h_ref, n_ref in (
        (jnp.where(first, mine, other), h0_ref, n0_ref),
        (jnp.where(first, other, mine), h1_ref, n1_ref),
    ):
        h_ref[...] = h
        unit, _ = statistics(h)
        n_ref[...] = (unit * gain_ref[...]).astype(BF16)


def first_norm(chip, mine, other, gain):
    state, normed = shaped(mine.shape, F32), shaped(mine.shape, BF16)
    outs = (state, normed, state, normed)
    return kernel_call(first_norm_body, outs, "first_norm", 2.5, 1)(chip, mine, other, gain)


def both(pair_ref, received_ref):
    return pair_ref[...].astype(F32) + received_ref[...].astype(F32)


def norm_body(h_ref, pair_ref, received_ref, gain_ref, state_ref, normed_ref):
    h = h_ref[...] + both(pair_ref, received_ref)
    state_ref[...] = h
    unit, _ = statistics(h)
    normed_ref[...] = (unit * gain_ref[...]).astype(BF16)


def norm_step(h, pair, received, gain):
    outs = (shaped(h.shape, F32), shaped(h.shape, BF16))
    return kernel_call(norm_body, outs, "norm_step", 1.5)(h, pair, received, gain)


def back_body(g_ref, pair_ref, received_ref, h_ref, gain_ref, grad_ref, low_ref, gain_grad_ref):
    grad, gain_grad_ref[...] = norm_gradient(
        both(pair_ref, received_ref), h_ref[...], gain_ref[...]
    )
    grad = g_ref[...].astype(F32) + grad
    grad_ref[...] = grad
    low_ref[...] = grad.astype(BF16)


def back_step(g, pair, received, h, gain):
    outs = (shaped(g.shape, F32), shaped(g.shape, BF16), shaped(gain.shape, F32))
    return kernel_call(back_body, outs, "back_step", 2)(g, pair, received, h, gain)


def last_back_body(chip_ref, g0, h0, g1, h1, own_ref, received_ref, gain_ref, out_ref):
    first = chip_ref[0] == 0
    grad_normed = both(own_ref, received_ref)
    h = jnp.where(first, h0[...], h1[...])
    grad = jnp.where(first, g0[...], g1[...])
    out_ref[...] = (grad + norm_gradient(grad_normed, h, gain_ref[...])[0]).astype(BF16)


def last_back(chip, grads, states, own, received, gain):
    outs = shaped(received.shape, BF16)
    return kernel_call(last_back_body, outs, "last_back", 2, 1)(
        chip, grads[0], states[0], grads[1], states[1], own, received, gain
    )


def own_half_body(chip_ref, keep_ref, received_ref, own_ref, send_ref):
    first = chip_ref[0] == 0
    low = keep_ref[0].astype(F32) + received_ref[0].astype(F32)
    high = keep_ref[1].astype(F32) + received_ref[1].astype(F32)
    own_ref[...] = jnp.where(first, low, high).astype(BF16)
    send_ref[...] = jnp.where(first, high, low).astype(BF16)


def own_half(chip, keep, received):
    piece = shaped(keep.shape[1:], BF16)
    return kernel_call(own_half_body, (piece, piece), "own_half", 2, 1)(chip, keep, received)


ROOT = 0.7978845608028654
CUBIC = 0.044715


def gelu(u):
    return 0.5 * u * (1.0 + jnp.tanh(ROOT * (u + CUBIC * u * u * u)))


def gelu_parts(u):
    square = u * u
    t = jnp.tanh(ROOT * (u + CUBIC * u * square))
    half = 0.5 * (1.0 + t)
    slope = half + 0.5 * u * (1.0 - t * t) * (ROOT * (1.0 + 3.0 * CUBIC * square))
    return u * half, slope


PIECE = 768


def unit_pieces(units, *refs):
    for i, ref in enumerate(refs):
        yield slice(i * units, (i + 1) * units), ref[:, :units], ref[:, units : 2 * units]


def ffn_fwd_body(
    h_ref, pair_ref, received_ref, gain_ref, own_ref, mate_ref, state_ref, n_ref, hidden_ref, out_ref
):
    units = mate_ref.shape[1] // 2
    h = h_ref[...] + both(pair_ref, received_ref)
    state_ref[...] = h
    unit, _ = statistics(h)
    n = (unit * gain_ref[...]).astype(BF16)
    n_ref[...] = n
    out = None
    for lanes, up, down in unit_pieces(units, own_ref, mate_ref):
        hidden = dot(n, up)
        hidden_ref[:, lanes] = hidden
        part = dot_nt(gelu(hidden).astype(BF16), down)
        out = part if out is None else out + part
    out_ref[...] = out.astype(BF16)


def ffn_forward(h, pair, received, gain, own, mate):
    piece = shaped(h.shape, BF16)
    hidden = shaped((h.shape[0], mate.shape[1]), F32)
    outs = (shaped(h.shape, F32), piece, hidden, piece)
    return kernel_call(ffn_fwd_body, outs, "ffn_forward", 50)(h, pair, received, gain, own, mate)


def ffn_both_body(
    h_ref, pair_ref, received_ref, gain_ref, g_ref, own_ref, mate_ref,
    state_ref, n_ref, grad_ref, active_ref, out_ref,
):
    units = mate_ref.shape[1] // 2
    h = h_ref[...] + both(pair_ref, received_ref)
    state_ref[...] = h
    unit, _ = statistics(h)
    n = (unit * gain_ref[...]).astype(BF16)
    n_ref[...] = n
    g = g_ref[...]
    out = None
    for lanes, up, down in unit_pieces(units, own_ref, mate_ref):
        active, slope = gelu_parts(dot(n, up))
        active_ref[:, lanes] = active.astype(BF16)
        grad = (dot(g, down) * slope).astype(BF16)
        grad_ref[:, lanes] = grad
        part = dot_nt(grad, up)
        out = part if out is None else out + part
    out_ref[...] = out.astype(BF16)


def ffn_both(h, pair, received, gain, g, own, mate):
    piece = shaped(h.shape, BF16)
    rows = shaped((h.shape[0], mate.shape[1]), BF16)
    outs = (shaped(h.shape, F32), piece, rows, rows, piece)
    return kernel_call(ffn_both_body, outs, "ffn_both", 60)(h, pair, received, gain, g, own, mate)


def ffn_bwd_body(
    g_ref, pair_ref, received_ref, h_ref, gain_ref, hidden_ref, own_ref, mate_ref,
    total_ref, low_ref, grad_ref, active_ref, out_ref, gain_grad_ref,
):
    units = mate_ref.shape[1] // 2
    total, gain_grad_ref[...] = norm_gradient(
        both(pair_ref, received_ref), h_ref[...], gain_ref[...]
    )
    total = g_ref[...] + total
    total_ref[...] = total
    g = total.astype(BF16)
    low_ref[...] = g
    out = None
    for lanes, up, down in unit_pieces(units, own_ref, mate_ref):
        active, slope = gelu_parts(hidden_ref[:, lanes])
        active_ref[:, lanes] = active.astype(BF16)
        grad = (dot(g, down) * slope).astype(BF16)
        grad_ref[:, lanes] = grad
        part = dot_nt(grad, up)
        out = part if out is None else out + part
    out_ref[...] = out.astype(BF16)


def ffn_backward(g, pair, received, h, gain, hidden, own, mate):
    piece = shaped(h.shape, BF16)
    rows = shaped(hidden.shape, BF16)
    outs = (shaped(h.shape, F32), piece, rows, rows, piece, shaped(gain.shape, F32))
    return kernel_call(ffn_bwd_body, outs, "ffn_backward", 60)(
        g, pair, received, h, gain, hidden, own, mate
    )


def ffn_out_body(chip_ref, a0_ref, a1_ref, own_ref, mate_ref, out_ref, send_ref):
    units = mate_ref.shape[1] // 2
    outs = []
    for a_ref in (a0_ref, a1_ref):
        out = None
        for lanes, _, down in unit_pieces(units, own_ref, mate_ref):
            part = dot_nt(a_ref[:, lanes], down)
            out = part if out is None else out + part
        outs.append(out)
    first = chip_ref[0] == 0
    out_ref[...] = jnp.where(first, outs[0], outs[1]).astype(BF16)
    send_ref[...] = jnp.where(first, outs[1], outs[0]).astype(BF16)


def ffn_out(chip, active0, active1, own, mate):
    piece = shaped((active0.shape[0], own.shape[0]), BF16)
    return kernel_call(ffn_out_body, (piece, piece), "ffn_out", 3, 1)(
        chip, active0, active1, own, mate
    )


def output_body(chip_ref, h0_ref, h1_ref, own_ref, received_ref, out_ref):
    h = jnp.where(chip_ref[0] == 0, h0_ref[...], h1_ref[...])
    out_ref[...] = (h + both(own_ref, received_ref)).astype(BF16)


def output_step(chip, states, own, received):
    outs = shaped(own.shape, BF16)
    return kernel_call(output_body, outs, "output_step", 2, 1)(chip, *states, own, received)


def ffn_grads_body(n0, n1, g0, g1, gh0, gh1, a0, a1, own_ref, *mate_refs):
    count = len(mate_refs) // 2
    units = count * PIECE
    for i in range(count):
        lanes = slice(units + i * PIECE, units + (i + 1) * PIECE)
        mate_refs[i][...] = (
            dot_tn(n0[...], gh0[:, lanes]) + dot_tn(n1[...], gh1[:, lanes])
        ).astype(BF16)
        mate_refs[count + i][...] = (
            dot_tn(g0[...], a0[:, lanes]) + dot_tn(g1[...], a1[:, lanes])
        ).astype(BF16)
    own_ref[:, :units] = (
        dot_tn(n0[...], gh0[:, :units]) + dot_tn(n1[...], gh1[:, :units])
    ).astype(BF16)
    own_ref[:, units:] = (
        dot_tn(g0[...], a0[:, :units]) + dot_tn(g1[...], a1[:, :units])
    ).astype(BF16)


def ffn_grads(n, g, grad_hidden, active):
    model, units = n[0].shape[1], active[0].shape[1]
    outs = (shaped((model, units), BF16),) + (shaped((model, PIECE), BF16),) * (units // PIECE)
    own, *mate = kernel_call(ffn_grads_body, outs, "ffn_grads", 6)(*n, *g, *grad_hidden, *active)
    return own, mate


def attn_grads_body(x_ref, gp_ref, g_ref, att_ref, own_ref, *refs):
    *mate_refs, out_ref = refs
    first = own_ref.shape[1]
    joined = first + gp_ref.shape[1]
    for i, mate_ref in enumerate(mate_refs):
        lanes = slice(i * PIECE, (i + 1) * PIECE)
        out_ref[:, lanes] = (own_ref[:, lanes].astype(F32) + mate_ref[...].astype(F32)).astype(BF16)
    out_ref[:, first:joined] = dot_tn(x_ref[...], gp_ref[...]).astype(BF16)
    out_ref[:, joined:] = lax.dot_general(
        g_ref[...], att_ref[...], (((0,), (1,)), ((), ())), preferred_element_type=F32
    ).astype(BF16)


def attn_grads(x, joined, g, attended_t, own, mate):
    columns = own.shape[1] + joined.shape[1] + attended_t.shape[0]
    outs = shaped((x.shape[1], columns), BF16)
    return kernel_call(attn_grads_body, outs, "attn_grads", 8)(
        x, joined, g, attended_t, own, *mate
    )


def halved(side, count, bit, rows_of, keep_ref, send_ref, lanes=slice(None)):
    block = keep_ref.shape[0] * 2 // count
    place = 0
    for j in range(count):
        if j & bit:
            continue
        low, high = rows_of(j * block, block), rows_of((j | bit) * block, block)
        here = slice(place, place + block)
        keep_ref[here, lanes] = jnp.where(side == 0, low, high).astype(BF16)
        send_ref[here, lanes] = jnp.where(side == 0, high, low).astype(BF16)
        place += block


def halves_of(rows, columns):
    return (shaped((rows // 2, columns), BF16),) * 2


def ffn_cut(side, own, mate, count, bit):
    def body(side_ref, own_ref, *refs):
        *mate_refs, keep_ref, send_ref = refs
        for i, mate_ref in enumerate(mate_refs):
            lanes = slice(i * PIECE, (i + 1) * PIECE)

            def rows_of(first, size, mate_ref=mate_ref, lanes=lanes):
                here = slice(first, first + size)
                return own_ref[here, lanes].astype(F32) + mate_ref[here].astype(F32)

            halved(side_ref[0], count, bit, rows_of, keep_ref, send_ref, lanes)

    return kernel_call(body, halves_of(*own.shape), "ffn_cut", 3, 1)(side, own, *mate)


def mixer_grads(side, x, joined, g, mixed, w, count, bit):
    model, columns = x.shape[1], joined.shape[1] + mixed.shape[1]
    inputs = joined.shape[1]

    def body(side_ref, x_ref, gp_ref, g_ref, mixed_ref, w_ref, keep_ref, send_ref, gain_ref, total):
        total[:, :inputs] = dot_tn(x_ref[...], gp_ref[...])
        total[:, inputs:] = dot_tn(g_ref[...], mixed_ref[...])
        halved(
            side_ref[0], count, bit, lambda first, size: total[first : first + size], keep_ref, send_ref
        )
        weighted = total[:, :inputs] * w_ref[:, :inputs].astype(F32)
        high, low = split(weighted)
        ones = jnp.ones((8, inputs), BF16)
        gain_ref[...] = (dot_nt(ones, high) + dot_nt(ones, low))[:1]

    outs = halves_of(model, columns) + (shaped((1, model), F32),)
    return kernel_call(body, outs, "mixer_grads", 6, 1, [pltpu.VMEM((model, columns), F32)])(
        side, x, joined, g, mixed, w
    )


def scatter_step(side, keep, received, count, bit):
    def body(side_ref, kept_ref, received_ref, keep_ref, send_ref):
        def rows_of(first, size):
            here = slice(first, first + size)
            return kept_ref[here].astype(F32) + received_ref[here].astype(F32)

        halved(side_ref[0], count, bit, rows_of, keep_ref, send_ref)

    return kernel_call(body, halves_of(*keep.shape), "scatter_step", 2, 1)(side, keep, received)


def gain_places(count, rows, model, gains):
    block = model // count
    lanes = gains * block // rows
    step = math.gcd(block, lanes)
    places = []
    for j in range(count):
        for i in range(gains):
            for first in range(0, block, step):
                flat = i * block + first
                places.append((i, j * block + first, step, j * rows + flat // lanes, flat % lanes))
    return places, lanes


def small_cut(side, taps, tiles, gains, count, bit):
    width = taps.shape[1]
    starts = [0] * len(tiles)
    for i in range(1, len(tiles)):
        starts[i] = starts[i - 1] + tiles[i - 1][0].shape[1]
    places, lanes = gain_places(count, taps.shape[0] // count, gains.shape[1], gains.shape[0])

    def body(side_ref, taps_ref, gains_ref, *refs):
        *tile_refs, keep_ref, send_ref, total = refs
        total[:, :width] = taps_ref[...]
        for i, start in enumerate(starts):
            size = tile_refs[2 * i].shape[1]
            total[:, width + start : width + start + size] = tile_refs[2 * i][...]
            total[:, 2 * width + start : 2 * width + start + size] = tile_refs[2 * i + 1][...]
        for i, first, size, row, lane in places:
            here = slice(3 * width + lane, 3 * width + lane + size)
            total[row : row + 1, here] = gains_ref[i : i + 1, first : first + size]
        halved(
            side_ref[0], count, bit, lambda first, size: total[first : first + size], keep_ref, send_ref
        )

    shape = (taps.shape[0], 3 * width + lanes)
    return kernel_call(
        body, halves_of(*shape), "small_cut", 2, 1, [pltpu.VMEM(shape, F32)]
    )(side, taps, gains, *[x for tile in tiles for x in tile])


def finish_small(keep, received, gains, width):
    rows = keep.shape[0]
    count, block = gains.shape
    places, _ = gain_places(1, rows, block, count)

    def body(keep_ref, received_ref, gains_ref, taps_ref, decay_ref, coef_ref, gain_grad_ref):
        total = keep_ref[...].astype(F32) + received_ref[...].astype(F32)
        taps_ref[...] = total[:, :width]
        decay_ref[...] = total[:, width : 2 * width]
        coef_ref[...] = total[:, 2 * width : 3 * width]
        for i, first, size, row, lane in places:
            lanes = slice(3 * width + lane, 3 * width + lane + size)
            part = total[row : row + 1, lanes]
            if i == 0:
                part = part / gains_ref[:1, first : first + size]
            gain_grad_ref[i : i + 1, first : first + size] = part

    outs = (
        shaped((rows, width), F32), shaped((rows, width), F32), shaped((rows, width), F32),
        shaped((count, block), F32),
    )
    return kernel_call(body, outs, "finish_small", 2)(keep, received, gains)


def summed(parts, lanes):
    total = parts[0][:, lanes].astype(F32)
    for part in parts[1:]:
        total = total + part[:, lanes].astype(F32)
    return total


def finish(parts, ffn_parts, first, ffn_first, width, units):
    rows = parts[0].shape[0]
    count = len(parts)

    def body(*refs):
        part_refs, ffn_refs = refs[:count], refs[count : 2 * count]
        q_ref, k_ref, v_ref, o_ref, up_ref, down_ref = refs[2 * count :]
        for i, out_ref in enumerate((q_ref, k_ref, v_ref)):
            out_ref[...] = summed(part_refs, slice(first + i * width, first + (i + 1) * width))
        o_ref[...] = summed(part_refs, slice(first + 3 * width, first + 4 * width)).T
        up_ref[...] = summed(ffn_refs, slice(ffn_first, ffn_first + units))
        down_ref[...] = summed(ffn_refs, slice(ffn_first + units, ffn_first + 2 * units))

    square = shaped((rows, width), F32)
    outs = (
        square, square, square, shaped((width, rows), F32),
        shaped((rows, units), F32), shaped((rows, units), F32),
    )
    return kernel_call(body, outs, "finish", 5)(*parts, *ffn_parts)


TENSOR = "tensor"
DATA = "dp"


def swap(x, bit):
    return lax.ppermute(x, TENSOR, [(i, i ^ bit) for i in range(4)])


def from_mate(x):
    return swap(x, 1)


def from_chip(x):
    return swap(x, 2)


def tie(*values):
    return lax.optimization_barrier(values)


def after(value, *others):
    return lax.optimization_barrier((value,) + others)[0]


def row_major(x):
    return with_layout_constraint(x, Layout(major_to_minor=tuple(range(x.ndim))))


def add_cores(keep, send):
    return (keep.astype(F32) + from_mate(send).astype(F32)).astype(BF16)


class Rows:
    def __init__(self):
        self.count = lax.axis_size(DATA)
        self.index = lax.axis_index(DATA)
        self.depth = self.count.bit_length() - 1
        self.bits = [1 << i for i in reversed(range(self.depth))]

    def swap(self, x, bit):
        return lax.ppermute(x, DATA, [(i, i ^ bit) for i in range(self.count)])

    def gather_send(self, x, step):
        return self.swap(x, self.bits[step])

    def gather_merge(self, x, other, step):
        upper = (self.index & self.bits[step]) != 0
        return jnp.stack([jnp.where(upper, other, x), jnp.where(upper, x, other)], axis=step)

    def gather_step(self, x, step):
        return self.gather_merge(x, self.gather_send(x, step), step)

    def gather(self, x, first=0, last=None):
        for step in range(first, self.depth if last is None else last):
            x = self.gather_step(x, step)
        return x

    def flat(self, x):
        return x.reshape(self.count * x.shape[-2], x.shape[-1])

    def parts(self, x):
        return x.reshape((2,) * self.depth + (x.shape[0] // self.count, x.shape[1]))

    def cut(self, x, step):
        side = ((self.index & self.bits[step]) != 0).astype(jnp.int32)
        keep = lax.dynamic_slice_in_dim(x, side, 1, step)
        send = lax.dynamic_slice_in_dim(x, 1 - side, 1, step)
        return keep, send.astype(BF16)

    def side(self, step):
        return ((self.index & self.bits[step]) != 0).astype(jnp.int32).reshape(1)

    def without(self, x, step):
        shape = [2] * self.depth
        shape[step] = 1
        return x.reshape(tuple(shape) + (x.shape[0] * 2 // self.count, x.shape[1]))

    def scatter(self, x, steps):
        for step in steps:
            keep, send = self.cut(x, step)
            x = keep.astype(F32) + self.swap(send, self.bits[step]).astype(F32)
        return x


def on_device(
    tokens, cotangent, seq_lengths,
    gain_mixer, mixer_query, mixer_key, mixer_value, shift_taps, ssm_decay, ssm_coef, mixer_out,
    gain_ffn1, ffn1_up, ffn1_down,
    gain_attn, attn_query, attn_key, attn_value, attn_out,
    gain_ffn2, ffn2_up, ffn2_down,
):
    place = lax.axis_index(TENSOR)
    chip = place >> 1
    core = (place & 1).astype(jnp.int32).reshape(1)
    chips = chip.astype(jnp.int32).reshape(1)
    rows = Rows()
    fwd, inv = spectral_tables()
    quarter, model = tokens.shape
    length = 4 * quarter
    block, width = mixer_query.shape
    units = ffn1_up.shape[1]
    unit_rows = shift_taps.shape[0]
    states = unit_rows * rows.count

    own_gains = jnp.stack([gain_mixer, gain_ffn1, gain_attn, gain_ffn2], axis=0)
    small = jnp.zeros((16, model), BF16)
    small = small.at[:unit_rows, : 3 * width].set(
        jnp.concatenate([shift_taps, ssm_decay.T, ssm_coef.T], axis=1)
    )
    small = small.at[12:16, :block].set(own_gains)
    mixer_own = jnp.concatenate([mixer_query, mixer_key, mixer_value, mixer_out.T], axis=1)
    ffn1_own = jnp.concatenate([ffn1_up, ffn1_down.T], axis=1)
    attn_own = jnp.concatenate([attn_query, attn_key, attn_value, attn_out.T], axis=1)
    ffn2_own = jnp.concatenate([ffn2_up, ffn2_down.T], axis=1)
    top = rows.depth - 1
    positions = place * quarter + jnp.arange(quarter)
    live = (positions < seq_lengths[0])[:, None]
    masked = jnp.where(live, cotangent, jnp.zeros_like(cotangent))
    small = rows.gather(small, 0, 1)
    mixer_w = rows.gather(mixer_own, 0, 1)
    there = from_chip(tokens)
    first_w = lax.all_gather(
        jnp.concatenate([ffn1_own, attn_own], axis=1), DATA, axis=0, tiled=True
    )
    small = rows.gather(small, 1, top)
    mixer_w = rows.gather(mixer_w, 1, top)
    small = rows.gather(small, top).reshape(rows.count, 16, model)
    small, mixer_w = tie(small, mixer_w)
    mixer_other = rows.gather_send(mixer_w, top)

    gains = small[:, 12:16, :block].transpose(1, 0, 2).reshape(4, 1, model).astype(F32)
    vectors = small[:, :unit_rows, : 3 * width].reshape(states, 3 * width).astype(F32)
    taps_w, decay_t, coef_t = (vectors[:, i * width : (i + 1) * width] for i in range(3))
    h0, n0, h1, n1 = first_norm(chips, tokens, there, gains[0])
    start = [h0, h1]
    grad_other = from_chip(after(masked, n0))
    spectra = kernel_spectra(after(decay_t, n0), coef_t, taps_w, fwd, length)
    pieces = [n0, from_mate(n0), n1, from_mate(n1)]
    mixer_other, grad_other = after((mixer_other, grad_other), spectra[0])
    mixer_w = rows.flat(rows.gather_merge(mixer_w, mixer_other, top))
    keep, send, x1, mixed, *saved = mixer_forward_kernel(
        core, pieces, mixer_w, spectra, fwd, inv
    )

    def core_sums(keep, send):
        other = from_mate(send)
        return [(keep[i].astype(F32) + other[i].astype(F32)).astype(BF16) for i in range(2)]

    def exchanged(keep, send):
        sums = core_sums(keep, send)
        return sums, [from_chip(p) for p in sums]

    pairs, received = exchanged(keep, send)
    first_w = after(first_w, pairs[1])
    ffn1_w, attn_w = first_w[:, : 2 * units], first_w[:, 2 * units :]
    grad = [jnp.where(chip == 0, masked, grad_other), jnp.where(chip == 0, grad_other, masked)]
    received[0], attn_w, *grad = tie(received[0], attn_w, *grad)
    ffn1_mate = from_mate(ffn1_w)
    ffn2_w = lax.all_gather(after(ffn2_own, pairs[1]), DATA, axis=0, tiled=True)
    ffn1_mate = after(ffn1_mate, received[0])
    after_mixer, n2, hidden1, nexts, arrived = [], [], [], [], []
    for half in range(2):
        wait = received[0] if half == 0 else after(received[1], nexts[0])
        h, n, hidden, out = ffn_forward(
            start[half], pairs[half], wait, gains[1], ffn1_w, ffn1_mate
        )
        after_mixer.append(h)
        n2.append(n)
        hidden1.append(hidden)
        nexts.append(out)
        arrived.append(from_chip(out))
    after_ffn1, pieces = [], []
    for half in range(2):
        wait = after(arrived[half], nexts[1]) if half == 0 else after(arrived[1], pieces[0])
        h, n = norm_step(after_mixer[half], nexts[half], wait, gains[2])
        after_ffn1.append(h)
        pieces += [n, from_mate(n)]
    keep, send, x3, q2, k2, v2, attended_t, log_total = attn_forward_kernel(
        core, seq_lengths, pieces, attn_w
    )
    pairs, received = exchanged(keep, send)
    ffn2_w = after(ffn2_w, pairs[1])

    ffn2_mate = from_mate(ffn2_w)
    g4 = list(grad)
    ffn2_mate = after(ffn2_mate, received[0])
    after_attn, n4, gh, act, nexts, arrived = [], [], [], [], [], []
    for half in range(2):
        wait = received[0] if half == 0 else after(received[1], nexts[0])
        h, n, grad_hidden, active, out = ffn_both(
            after_ffn1[half], pairs[half], wait, gains[3], g4[half], ffn2_w, ffn2_mate
        )
        after_attn.append(h)
        n4.append(n)
        gh.append(grad_hidden)
        act.append(active)
        nexts.append(out)
        arrived.append(from_chip(out))
    lows, ffn2_gain = [], []
    wait = after(arrived[0], nexts[1])
    grad[0], low, part = back_step(grad[0], nexts[0], wait, after_attn[0], gains[3])
    ffn2_gain.append(part)
    lows.append(low)
    gh, act = after((gh, act), low)
    own, mate = ffn_grads(n4, g4, gh, act)
    wait = after(arrived[1], mate[-1])
    grad[1], low, part = back_step(grad[1], nexts[1], wait, after_attn[1], gains[3])
    ffn2_gain.append(part)
    lows.append(low)
    pieces = [lows[0], from_mate(after(lows[0], low)), lows[1], from_mate(lows[1])]
    ffn2_mate_g = [from_mate(x) for x in after(tuple(mate), pieces[1], pieces[3])]
    keep, send, g3, grad_joined = attn_backward_kernel(
        core, seq_lengths, pieces, attn_w, q2, k2, v2, log_total
    )
    pairs, received = exchanged(keep, send)
    own, ffn2_mate_g = after((own, ffn2_mate_g), pairs[1])
    second_p = attn_grads(x3, grad_joined, g3, attended_t, own, ffn2_mate_g)
    step = rows.depth - 1
    final_own, final_sent = ffn_out(chips, *after(tuple(act), second_p), ffn2_w, ffn2_mate)
    received = list(after(tuple(received), second_p, final_sent))

    g2, gh, act_b, nexts, arrived, attn_gain = [], [], [], [], [], []
    for half in range(2):
        wait = received[half]
        grad[half], low, grad_hidden, active, out, part = ffn_backward(
            grad[half].astype(F32), pairs[half], wait, after_ffn1[half], gains[2], hidden1[half],
            ffn1_w, ffn1_mate,
        )
        g2.append(low)
        attn_gain.append(part)
        gh.append(grad_hidden)
        act_b.append(active)
        nexts.append(out)
        arrived.append(from_chip(out))
    second_g = lax.psum_scatter(after(second_p, nexts[0]), DATA, scatter_dimension=0, tiled=True)
    lows, ffn1_gain = [], []
    wait = after(arrived[0], nexts[1])
    grad[0], low, part = back_step(grad[0], nexts[0], wait, after_mixer[0], gains[1])
    ffn1_gain.append(part)
    lows.append(low)
    gh, act_b = after((gh, act_b), low)
    own, mate = ffn_grads(n2, g2, gh, act_b)
    wait = after(arrived[1], mate[-1])
    grad[1], low, part = back_step(grad[1], nexts[1], wait, after_mixer[1], gains[1])
    ffn1_gain.append(part)
    lows.append(low)
    pieces = [lows[0], from_mate(lows[0]), lows[1], from_mate(lows[1])]
    mate_g = [from_mate(x) for x in after(tuple(mate), pieces[1], arrived[1])]
    mate_g, pieces[1], pieces[3] = tie(mate_g, pieces[1], pieces[3])
    ffn1_keep, ffn1_send = ffn_cut(rows.side(step), own, mate_g, rows.count, rows.bits[step])
    pieces[0], ffn1_send, final_sent = tie(pieces[0], ffn1_send, final_sent)
    final_received = from_chip(final_sent)
    ffn1_received = rows.swap(ffn1_send, rows.bits[step])
    keep, send, g1, grad_joined, grad_taps, *g_spectrum = mixer_backward_kernel(
        core, pieces, mixer_w, saved[:6], spectra, fwd, inv, states
    )
    mixer_keep, mixer_send, mixer_gain = mixer_grads(
        rows.side(step - 1), x1, grad_joined, g1, mixed, mixer_w, rows.count, rows.bits[step - 1]
    )
    gain_rows = jnp.concatenate(
        [mixer_gain] + [0.5 * (p[0] + p[1]) for p in (ffn1_gain, attn_gain, ffn2_gain)], axis=0
    )
    gain_rows = gain_rows + from_mate(gain_rows)
    gain_rows = gain_rows + from_chip(gain_rows)
    mixer_received = rows.swap(mixer_send, rows.bits[step - 1])
    own, last_sent = own_half(chips, keep, from_mate(after(send, mixer_send)))
    last_received = from_chip(last_sent)
    g_spectrum = after(tuple(g_spectrum), last_sent)
    ssm = [ssm_grad_kernel(g_spectrum, saved[6:], decay_t, coef_t, inv, 0)]

    half, pair = rows.count // 2, rows.count // 4

    def send_on(arrays, step, *ready):
        return [rows.swap(x, rows.bits[step]) for x in arrays]

    ffn1_received = after(ffn1_received, ssm[0][0])
    ffn1_keep, ffn1_send = scatter_step(rows.side(step - 1), ffn1_keep, ffn1_received, half, 1)
    mixer_received = after(mixer_received, ffn1_send)
    mixer_keep, mixer_send = scatter_step(rows.side(step), mixer_keep, mixer_received, half, 1)
    ffn1_received = rows.swap(ffn1_send, rows.bits[step - 1])
    mixer_received = rows.swap(mixer_send, rows.bits[step])
    g_spectrum = after(g_spectrum, mixer_send)
    ssm += [
        ssm_grad_kernel(g_spectrum, saved[6:], decay_t, coef_t, inv, i)
        for i in range(1, len(channel_tiles(width)))
    ]
    small_keep, small_send = small_cut(
        rows.side(step), grad_taps, ssm, gain_rows, rows.count, rows.bits[step]
    )
    small_received = rows.swap(small_send, rows.bits[step])
    small_received = after(small_received, small_send)
    small_keep, small_send = scatter_step(rows.side(step - 1), small_keep, small_received, half, 1)
    small_received = rows.swap(small_send, rows.bits[step - 1])
    ffn1_received, mixer_received, last_received = tie(
        *after((ffn1_received, mixer_received, last_received), small_send)
    )
    ffn1_keep, ffn1_send = scatter_step(rows.side(step - 2), ffn1_keep, ffn1_received, pair, 1)
    mixer_received = after(mixer_received, ffn1_send)
    mixer_keep, mixer_send = scatter_step(rows.side(step - 2), mixer_keep, mixer_received, pair, 1)
    last_received, final_received = after((last_received, final_received), mixer_send)
    input_grad = last_back(chips, grad, start, own, last_received, gains[0])
    output = output_step(chips, after_attn, final_own, final_received)
    small_received = after(small_received, input_grad, output)
    small_keep, small_send = scatter_step(rows.side(step - 2), small_keep, small_received, pair, 1)

    ffn1_received = rows.swap(ffn1_send, rows.bits[step - 2])
    mixer_received = rows.swap(mixer_send, rows.bits[step - 2])
    small_received = rows.swap(small_send, rows.bits[step - 2])
    second_g = [after(second_g, small_send)]

    aq, ak, av, ao, u2, d2 = finish(second_g, second_g, 2 * units, 0, width, units)
    ffn1_received, mixer_received, small_received = after(
        (ffn1_received, mixer_received, small_received), aq, input_grad, output
    )
    level, tail = pair // 2, step - 3
    while tail >= 0:
        ffn1_keep, ffn1_send = scatter_step(rows.side(tail), ffn1_keep, ffn1_received, level, 1)
        mixer_keep, mixer_send = scatter_step(rows.side(tail), mixer_keep, mixer_received, level, 1)
        small_keep, small_send = scatter_step(rows.side(tail), small_keep, small_received, level, 1)
        ffn1_received = rows.swap(ffn1_send, rows.bits[tail])
        mixer_received = rows.swap(mixer_send, rows.bits[tail])
        small_received = rows.swap(small_send, rows.bits[tail])
        level, tail = level // 2, tail - 1
    mq, mk, mv, mo, u1, d1 = finish(
        [mixer_keep, mixer_received], [ffn1_keep, ffn1_received], 0, 0, width, units
    )
    gt, gd, gc, gain_grads = finish_small(
        small_keep, after(small_received, mq), own_gains.astype(F32), width
    )
    return (
        output, input_grad,
        gain_grads[0], mq, mk, mv, gt, gd.T, gc.T, mo,
        gain_grads[1], u1, d1.T,
        gain_grads[2], aq, ak, av, ao,
        gain_grads[3], u2, d2.T,
    )


def solution(mesh):
    rows = P(("dp", "tensor"), None)
    up = P("dp", "tensor")
    down = P("tensor", "dp")
    vector = P("dp")
    mixer = (vector, up, up, up, up, down, down, down)
    ffn = (vector, up, down)
    attn = (vector, up, up, up, down)
    weights = mixer + ffn + attn + ffn
    return jax.shard_map(
        on_device,
        mesh=mesh,
        in_specs=(rows, rows, vector) + weights,
        out_specs=(rows, rows) + weights,
        check_vma=False,
    )
```
